32 devices in a mesh: dp: 16 (over z, y, x), group: 2 (over core).
Axes of the slice: x: 2, y: 2, z: 4, core: 2. Of those that a mesh axis runs over, the one named last changes fastest.
Arguments:
- acts_first: bfloat16 [32, 32, 32, 256], P(('dp', 'group'))
- grads_first: bfloat16 [32, 32, 32, 256], P(('dp', 'group'))
- acts_second: bfloat16 [32, 32, 32, 256], P(('dp', 'group'))
- grads_second: bfloat16 [32, 16, 16, 256], P(('dp', 'group'))
- grad_w: bfloat16 [2, 256, 2304], P(None, 'dp'), may hold values from -6 to 6
- owner: int32 [2], replicated, may hold values from 0 to 7, as said below
- basis_in: bfloat16 [8, 256, 256], P('group'), may hold values from -0.375 to 0.375
- basis_spatial: bfloat16 [8, 9, 9], P('group'), may hold values from -2 to 2
- basis_out: bfloat16 [8, 256, 256], P('group'), may hold values from -0.375 to 0.375
Outputs:
- precond: bfloat16 [2, 256, 2304], P(None, 'dp')
- factor_in: float32 [2, 256, 256], replicated
- factor_spatial: float32 [2, 9, 9], replicated
- factor_out: float32 [2, 256, 256], replicated
The draws below stay inside these ranges and needn't reach their ends.
Inputs may be any that keep to these rules, and one draw needn't show every extreme that they name: owner[l] is the slot that holds layer l's bases, one of the 4 slots of group owner[l] // 4; no two layers share a slot.
All inputs are finite; a program needn't handle non-finite values.
Results may differ from the reference program's by a relative error of at most 0.0045.
Values may be sent and summed in bfloat16 or wider, within the bound.
A program may use at most 64 MiB of HBM per device.

```python
import math
import jax
import jax.numpy as jnp
from jax import lax

C = 256
HI = 32
LAYERS = 2
SLOTS = 4
HO = 16
IMAGES = 32
GROUPS = 2


def scaled_field(key, side_len):
    noise_key, chan_key, image_key = jax.random.split(key, 3)
    field_shape = (IMAGES, side_len, side_len, C)
    noise_vals = jax.random.normal(noise_key, field_shape, jnp.float32)
    chan_scale = jnp.exp(jax.random.uniform(chan_key, (C,), jnp.float32, math.log(0.3), math.log(3.0)))
    image_ramp = jnp.arange(IMAGES, dtype=jnp.float32) / IMAGES
    image_scale = jnp.exp(math.log(0.6) + math.log(3.0) * image_ramp + jax.random.uniform(image_key, (IMAGES,), jnp.float32, -0.2, 0.2))
    return noise_vals * chan_scale * image_scale[:, None, None, None]


def draw_acts_first(key, part):
    return scaled_field(jax.random.fold_in(key, 11), HI).astype(jnp.bfloat16)


def draw_grads_first(key, part):
    return scaled_field(jax.random.fold_in(key, 12), HI).astype(jnp.bfloat16)


def draw_acts_second(key, part):
    return scaled_field(jax.random.fold_in(key, 13), HI).astype(jnp.bfloat16)


def draw_grads_second(key, part):
    return scaled_field(jax.random.fold_in(key, 14), HO).astype(jnp.bfloat16)


def draw_owner(key, part):
    lead_key, order_key = jax.random.split(jax.random.fold_in(key, 21))
    slot_total = GROUPS * SLOTS
    shuffled = jax.random.permutation(order_key, slot_total - 1)[:LAYERS]
    lead = jax.random.randint(lead_key, (), 0, LAYERS)
    slots = jnp.where(jnp.arange(LAYERS) == lead, slot_total - 1, shuffled)
    return slots.astype(jnp.int32)


def block_scale(stream_key, shape, cuts, smallest, high):
    gain, own = 1.0, jax.random.fold_in(stream_key, 6)
    for position, blocks in cuts:
        draws = jnp.exp(jax.random.uniform(jax.random.fold_in(own, position), (blocks,), jnp.float32, smallest / len(cuts), high / len(cuts)))
        gain = gain * jnp.repeat(draws, shape[position] // blocks).reshape([-1 if axis == position else 1 for axis in range(len(shape))])
    return gain


def bell_draw(stream_key, shape, spread, bound, pieces=(), kind=jnp.bfloat16):
    gain = block_scale(stream_key, shape, pieces, -0.22, 0.18) if pieces else 1.0
    values = jax.random.normal(stream_key, shape, jnp.float32) * spread * gain
    return jnp.minimum(jnp.maximum(values, -bound), bound).astype(kind)


def setup_inputs(seed: int = 0) -> dict:
    splits = jax.random.split(jax.random.key(seed), 10)
    return {
        "acts_first": draw_acts_first(jax.random.fold_in(splits[9], 71), 0),
        "grads_first": draw_grads_first(jax.random.fold_in(splits[9], 71), 0),
        "acts_second": draw_acts_second(jax.random.fold_in(splits[9], 71), 0),
        "grads_second": draw_grads_second(jax.random.fold_in(splits[9], 71), 0),
        "grad_w": bell_draw(splits[4], (LAYERS, C, 9 * C), 1.0, 6.0, ((1, 16),)),
        "owner": draw_owner(jax.random.fold_in(splits[9], 71), 0),
        "basis_in": bell_draw(splits[6], (GROUPS * SLOTS, C, C), C ** -0.5, 0.375, ((0, 2),)),
        "basis_spatial": bell_draw(splits[7], (GROUPS * SLOTS, 9, 9), 9 ** -0.5, 2.0, ((0, 2),)),
        "basis_out": bell_draw(splits[8], (GROUPS * SLOTS, C, C), C ** -0.5, 0.375, ((0, 2),)),
    }


DAMPING = 0.1

def window_views(images, stride, out_side):
    padded = jnp.pad(images, ((0, 0), (1, 1), (1, 1), (0, 0)))
    extent = stride * (out_side - 1) + 1
    limit_n = images.shape[0]
    channels = images.shape[3]
    windows = []
    for row_off in range(3):
        for col_off in range(3):
            windows.append(lax.slice(padded, (0, row_off, col_off, 0), (limit_n, row_off + extent, col_off + extent, channels), (1, stride, stride, 1)))
    return jnp.stack(windows)

def gram_terms(images, grads_out, stride):
    stacked = window_views(images, stride, grads_out.shape[1])
    channels = images.shape[3]
    patch_rows = stacked.reshape(-1, channels)
    channel_sum = lax.dot_general(patch_rows, patch_rows, (((0,), (0,)), ((), ())), preferred_element_type=jnp.float32)
    tap_rows = stacked.reshape(9, -1)
    spatial_sum = lax.dot_general(tap_rows, tap_rows, (((1,), (1,)), ((), ())), preferred_element_type=jnp.float32)
    out_rows = grads_out.reshape(-1, channels)
    output_sum = lax.dot_general(out_rows, out_rows, (((0,), (0,)), ((), ())), preferred_element_type=jnp.float32)
    return (channel_sum, spatial_sum, output_sum)

def whole_factors(images, grads_out, stride):
    block_count = images.shape[0] // 16
    image_blocks = images.reshape((block_count, 16) + images.shape[1:])
    grad_blocks = grads_out.reshape((block_count, 16) + grads_out.shape[1:])
    channels = images.shape[3]

    def add_block(carry, pair_in):
        terms = gram_terms(pair_in[0], pair_in[1], stride)
        return ((carry[0] + terms[0], carry[1] + terms[1], carry[2] + terms[2]), None)
    start_sums = (jnp.zeros((channels, channels), jnp.float32), jnp.zeros((9, 9), jnp.float32), jnp.zeros((channels, channels), jnp.float32))
    totals, unused = lax.scan(add_block, start_sums, (image_blocks, grad_blocks))
    positions = images.shape[0] * grads_out.shape[1] * grads_out.shape[2]
    return (totals[0] / (9.0 * positions), totals[1] / (1.0 * channels * positions), totals[2] / (1.0 * positions))

def eigen_values(basis, factor):
    basis_f = basis.astype(jnp.float32)
    return lax.optimization_barrier(jnp.sum(basis_f * jnp.dot(factor, basis_f, precision=lax.Precision.HIGHEST), axis=0))

def rotated_grad(weights, basis_chan, basis_tap):
    outs_n, taps_n, chans_n = weights.shape
    inner_in = jnp.dot(weights.reshape(outs_n * taps_n, chans_n), basis_chan, preferred_element_type=jnp.float32).reshape(outs_n, taps_n, -1)
    turned = jnp.einsum('okj,kl->olj', inner_in, basis_tap.astype(jnp.float32), precision=lax.Precision.HIGHEST)
    return turned.astype(jnp.bfloat16)

def scaled_coords(rotated, basis_outc, scale_out, scale_tap, scale_in):
    chans_out = basis_outc.shape[0]
    projected = lax.dot_general(basis_outc, rotated.reshape(chans_out, -1), (((0,), (0,)), ((), ())), preferred_element_type=jnp.float32).reshape(rotated.shape)
    divisor = scale_out[:, None, None] * scale_tap[None, :, None] * scale_in[None, None, :] + DAMPING
    return (projected / divisor).astype(jnp.bfloat16)

def back_rows(coords, rows_basis, basis_chan, basis_tap):
    row_n = rows_basis.shape[0]
    col_n = coords.shape[2]
    turned_back = jnp.dot(rows_basis, coords.reshape(coords.shape[0], -1), preferred_element_type=jnp.float32).astype(jnp.bfloat16)
    chan_back = lax.dot_general(turned_back.reshape(row_n * 9, col_n), basis_chan, (((1,), (1,)), ((), ())), preferred_element_type=jnp.float32).reshape(row_n, 9, -1)
    return jnp.einsum('okc,lk->olc', chan_back, basis_tap.astype(jnp.float32), precision=lax.Precision.HIGHEST)

def reference(acts_first, grads_first, acts_second, grads_second, grad_w, owner, basis_in, basis_spatial, basis_out):
    layer_inputs = ((acts_first, grads_first, 1), (acts_second, grads_second, 2))
    precond_list, fin_list, fsp_list, fout_list = ([], [], [], [])
    for layer_idx in range(LAYERS):
        images, grads_out, stride = layer_inputs[layer_idx]
        channel_f, spatial_f, output_f = whole_factors(images, grads_out, stride)
        slot_index = owner[layer_idx].astype(jnp.int32)
        basis_chan = lax.dynamic_index_in_dim(basis_in, slot_index, 0, keepdims=False)
        basis_tap = lax.dynamic_index_in_dim(basis_spatial, slot_index, 0, keepdims=False)
        basis_outc = lax.dynamic_index_in_dim(basis_out, slot_index, 0, keepdims=False)
        scale_in = eigen_values(basis_chan, channel_f)
        scale_tap = eigen_values(basis_tap, spatial_f)
        scale_out = eigen_values(basis_outc, output_f)
        weights = grad_w[layer_idx].reshape(C, 9, C)
        rotated = rotated_grad(weights, basis_chan, basis_tap)
        coords = scaled_coords(rotated, basis_outc, scale_out, scale_tap, scale_in)
        result = back_rows(coords, basis_outc, basis_chan, basis_tap).astype(jnp.bfloat16).reshape(C, 9 * C)
        precond_list.append(result)
        fin_list.append(channel_f)
        fsp_list.append(spatial_f)
        fout_list.append(output_f)
    return (jnp.stack(precond_list), jnp.stack(fin_list), jnp.stack(fsp_list), jnp.stack(fout_list))
```

```python
import functools

import jax
import jax.numpy as jnp
from jax import lax
from jax.experimental import pallas as pl
from jax.experimental.pallas import tpu as pltpu
from jax.sharding import PartitionSpec as P

LAYERS = 2
STRIDES = (1, 2)
DAMPING = 0.1
LANES = 128
CUBE = 8
MESH = pl.DeviceIdType.MESH
F32 = jnp.float32
BF16 = jnp.bfloat16
I32 = jnp.int32
CONTRACT_ROWS = (((0,), (0,)), ((), ()))
CONTRACT_COLS = (((1,), (1,)), ((), ()))
PAIRS = ((0, 0), (1, 1), (2, 2), (0, 1), (1, 2), (0, 2))


def dot(a, b):
    return jnp.dot(a, b, preferred_element_type=F32)


def dot_rows(a, b):
    return lax.dot_general(a, b, CONTRACT_ROWS, preferred_element_type=F32)


def dot_cols(a, b):
    return lax.dot_general(a, b, CONTRACT_COLS, preferred_element_type=F32)


def iota(shape, dim):
    return lax.broadcasted_iota(I32, shape, dim)


def each(start, stop, fn):
    def body(k, c):
        fn(k)
        return c
    lax.fori_loop(start, stop, body, 0)


def when(static, cond, fn):
    if static:
        fn()
    else:
        pl.when(cond)(fn)


def stacked(pieces):
    if pieces[0].shape[0] % 16 == 0:
        return jnp.concatenate(pieces, axis=0)
    return jnp.concatenate([piece.astype(F32) for piece in pieces], axis=0).astype(BF16)


def packed(left, right):
    half = left.shape[0]
    return jnp.concatenate([left[:, :half], left[:, half:], right], axis=0)


def channel_gram(x, side, stride):
    chans = x.shape[1]
    half = chans // 2
    col = iota((side, chans), 0)
    x3 = x.reshape(side, side, chans)

    def weighted(by_row):
        return jnp.concatenate([x3[i] * by_row(i) for i in range(side)], axis=0)

    lead, rest = x[:, :half], x[:, half:]
    if stride == 1:
        edge = (col == 0) | (col == side - 1)
        high_in = jnp.where(edge, 4.0, 8.0).astype(BF16)
        high_edge = jnp.full((side, chans), 4.0, BF16)
        low_in = jnp.where(edge, 2.0, 1.0).astype(BF16)
        low_edge = jnp.where(edge, 0.0, 2.0).astype(BF16)
        at_edge = lambda i: i in (0, side - 1)
        high = weighted(lambda i: high_edge if at_edge(i) else high_in)
        low = weighted(lambda i: low_edge if at_edge(i) else low_in)
        left = dot_rows(lead, high) + dot_rows(lead, low)
        right = dot_rows(rest, high[:, half:]) + dot_rows(rest, low[:, half:])
    else:
        odd = (col % 2 == 1) & (col < side - 1)
        once = jnp.where(odd, 2.0, 1.0).astype(BF16)
        twice = jnp.where(odd, 4.0, 2.0).astype(BF16)
        w = weighted(lambda i: twice if i % 2 == 1 and i < side - 1 else once)
        left, right = dot_rows(lead, w), dot_rows(rest, w[:, half:])
    return packed(left, right)


def plain_gram(g):
    half = g.shape[1] // 2
    return packed(dot_rows(g[:, :half], g), dot_rows(g[:, half:], g[:, half:]))


def tap_places(k):
    form, rest = k // 96, k % 96
    first = rest // 32
    rest = rest % 32
    pair, second = rest // 5, first + rest % 5 - 2
    a = jnp.where(pair < 3, pair, jnp.where(pair == 4, 1, 0))
    b = jnp.where(pair < 3, pair, jnp.where(pair == 3, 1, 2))
    one, two = 3 * a + first, 3 * b + second
    stands = (rest < 30) & (second >= 0) & (second < 3) & ((form == 0) | (pair >= 3))
    return jnp.where(form == 0, one, two), jnp.where(form == 0, two, one), stands


def tap_tables(rows_ref, cols_ref):
    shape = rows_ref.shape
    row, _, stands = tap_places(iota(shape, 1))
    rows_ref[...] = jnp.where((row == iota(shape, 0)) & stands, 1.0, 0.0).astype(BF16)
    shape = cols_ref.shape
    _, col, stands = tap_places(iota(shape, 0))
    cols_ref[...] = jnp.where((col == iota(shape, 1)) & stands, 1.0, 0.0)


def tap_gram(x_ref, rows_ref, cols_ref, sums_ref, side, stride, out_side):
    per = LANES // side
    total = None
    for q in range(side // per):
        at = q * LANES
        term = dot_cols(x_ref[at:at + LANES + 2 * side, :], x_ref[at:at + LANES, :])
        total = term if total is None else total + term
    shape = (side, LANES)
    below, lane = iota(shape, 0), iota(shape, 1)
    block, col = lane // side, lane % side

    def row_pairs(dy):
        out = total[(per - 1 + dy) * side:(per + dy) * side]
        for r in range(per - 1):
            out = jnp.where(block == r, total[(r + dy) * side:(r + dy + 1) * side], out)
        return out

    same, one, two = row_pairs(0), row_pairs(1), row_pairs(2)
    size = side * side
    last = jnp.where(block == per - 1,
                     dot_cols(x_ref[size - side:size, :], x_ref[size - LANES:size, :]), 0.0)
    if stride == 1:
        first = jnp.where(block == 0, dot_cols(x_ref[0:side, :], x_ref[0:LANES, :]), 0.0)
        by_pair = (same - last, same, same - first, one, one, two)
    else:
        even = block % 2 == 0
        odd_same = jnp.where(even, 0.0, same)
        by_pair = (odd_same - last, jnp.where(even, same, 0.0), odd_same,
                   jnp.where(even, 0.0, one), jnp.where(even, one, 0.0), jnp.where(even, 0.0, two))
    for p in range(6):
        for d in range(5):
            k = 5 * p + d
            sums_ref[k:k + 1, :] = jnp.sum(jnp.where(below - col == d - 2, by_pair[p], 0.0),
                                           axis=0, keepdims=True)
    sums = sums_ref[...]
    col = iota(sums.shape, 1) % side
    values = []
    for b in range(3):
        base = col + 1 - b
        mask = (base >= 0) & (base <= stride * (out_side - 1)) & (base % stride == 0)
        values.append(jnp.sum(jnp.where(mask, sums, 0.0), axis=1, keepdims=True))
    values = jnp.concatenate(values + values, axis=0)
    return dot(rows_ref[...], (values * cols_ref[...]).astype(BF16))


def through_basis(parts, basis, rows, flip):
    product = (lambda a: dot_cols(a, basis)) if flip else (lambda a: dot(a, basis))
    if rows % 16 == 0:
        whole = product(jnp.concatenate(parts, axis=0))
        return [whole[u * rows:(u + 1) * rows] for u in range(9)]
    return [product(part) for part in parts]


def mixed_taps(parts, coef):
    out = []
    for t in range(9):
        total = parts[0] * coef(0, t)
        for u in range(1, 9):
            total = total + parts[u] * coef(u, t)
        out.append(total)
    return out


def quadratic(blocks, basis):
    half = blocks.shape[0] // 3
    upper = jnp.concatenate([blocks[0:half], blocks[half:2 * half] * 2], axis=1)
    total = jnp.sum(basis[0:half].astype(F32) * dot(upper, basis), axis=0, keepdims=True)
    rest = basis[half:]
    return total + jnp.sum(rest.astype(F32) * dot(blocks[2 * half:], rest), axis=0, keepdims=True)


def remote(src, dst, send, recv, to):
    return pltpu.make_async_remote_copy(src_ref=src, dst_ref=dst, send_sem=send, recv_sem=recv,
                                        device_id=to, device_id_type=MESH)


def main_kernel(cfg, owner_ref, x0_hbm, g0_hbm, x1_hbm, g1_hbm, w_hbm, qa_hbm, qg_hbm, qs_hbm,
                out_ref, tot_out, tap_out, *scratch):
    side, outs, chans, rows, dp, ng, slot_total, slots, positions = cfg
    (x0_ref, g0_ref, x1_ref, g1_ref, w_ref, qa_ref, qg_ref, qs_ref,
     rows_tab, cols_tab, pick_ref, sums_ref, base_out, base_in, base_ref, part_ref, peer_ref,
     ra_ref, raa_ref, rb_ref, tot_ref, tap_ref, note_ref, notes_ref,
     rot_ref, rotin_ref, proj_ref, back_ref, backin_ref, fsp_ref, res_ref,
     loads, s_base, r_base, s_part, r_part, s_a, r_a, s_b, r_b, s_c, r_c, s_d, r_d,
     s_rot, r_rot, s_back, r_back, s_note, r_note, s_tap, r_tap, s_res, r_res) = scratch
    me, grp = lax.axis_index("dp"), lax.axis_index("group")
    cube = CUBE if dp % CUBE == 0 else dp
    halves = dp // cube
    member, part = lax.rem(me, cube), me // cube
    half = chans // 2
    blocks = 9 * chans // LANES
    size = side * side
    whole = ng == LAYERS
    off_qs, off_qg, off_x, off_rest = chans, chans + 16, 2 * chans + 16, 3 * chans + 16
    handles = lambda fn: when(whole, grp < LAYERS, fn)

    pairs = ((qs_hbm, qs_ref), (qa_hbm, qa_ref), (qg_hbm, qg_ref), (x0_hbm, x0_ref.at[pl.ds(0, size)]),
             (g0_hbm, g0_ref), (w_hbm, w_ref), (x1_hbm, x1_ref.at[pl.ds(0, size)]), (g1_hbm, g1_ref))
    copies = [pltpu.make_async_copy(src, dst, loads.at[i]) for i, (src, dst) in enumerate(pairs)]
    for copy in copies:
        copy.start()
    arrive = lambda i: copies[i].wait()

    barrier = pltpu.get_barrier_semaphore()
    for q in range(ng):
        to_grp = lax.rem(grp + q, ng)
        each(0 if q else 1, dp, lambda r, to_grp=to_grp: pl.semaphore_signal(
            barrier, inc=1, device_id={"dp": lax.rem(me + r, dp), "group": to_grp},
            device_id_type=MESH))

    def sibling(q):
        return lax.rem(grp + q, ng)

    def from_group(q):
        return lax.rem(grp + ng - q, ng)

    def copy_base(q, i):
        at, n = ((0, off_qg), (off_qg, off_rest + 16 - off_qg))[i]
        return remote(base_out.at[sibling(q), pl.ds(at, n)], base_in.at[q - 1, pl.ds(at, n)],
                      s_base.at[q, i], r_base.at[q, i], {"group": sibling(q)})

    def copy_part(l, q):
        return remote(part_ref.at[l, sibling(q)], peer_ref.at[l, q - 1], s_part.at[l, q],
                      r_part.at[l, q], {"group": sibling(q)})

    def copy_a(l, r):
        to = lax.rem(member + r, cube)
        return remote(ra_ref.at[l, to], raa_ref.at[l, r - 1], s_a.at[l, r], r_a.at[l, r],
                      {"dp": part * cube + to})

    def copy_b(l, r):
        to = lax.rem(part + r, halves)
        return remote(rb_ref.at[l, part], rb_ref.at[l, part], s_b.at[l, r], r_b.at[l, r],
                      {"dp": to * cube + member})

    def copy_c(l, r):
        to = lax.rem(member + r, cube)
        block = tot_ref.at[grp, l, member]
        return remote(block, block, s_c.at[l, r], r_c.at[l, r], {"dp": part * cube + to})

    def copy_d(l, r, q, k=grp):
        block = tot_ref.at[k, l, lax.rem(member + cube - r, cube)]
        return remote(block, block, s_d.at[l, r, q], r_d.at[l, r, q], {"group": sibling(q)})

    def copy_rot(s, r):
        to = lax.rem(me + r, dp)
        return remote(rot_ref.at[s, to], rotin_ref.at[s, me], s_rot.at[s, r], r_rot.at[s, r],
                      {"dp": to})

    def copy_back(s, r):
        to = lax.rem(me + r, dp)
        return remote(back_ref.at[s, to], backin_ref.at[s, me], s_back.at[s, r], r_back.at[s, r],
                      {"dp": to})

    def copy_note(l, r):
        return remote(note_ref.at[l], notes_ref.at[grp, me], s_note.at[l, r], r_note.at[grp, r],
                      {"dp": lax.rem(me + r, dp), "group": l})

    def note_from(k, r):
        return remote(note_ref.at[0], notes_ref.at[k, me], s_note.at[0, r], r_note.at[k, r],
                      {"dp": lax.rem(me + r, dp), "group": k})

    def copy_tap(q, k=grp):
        return remote(tap_ref.at[k], tap_ref.at[k], s_tap.at[q], r_tap.at[q],
                      {"group": sibling(q)})

    def copy_res(q, k=grp):
        return remote(res_ref.at[k], res_ref.at[k], s_res.at[q], r_res.at[q],
                      {"group": sibling(q)})

    def has_block(s, device):
        return s * dp + device < blocks

    def if_block(s, device, fn):
        when((s + 1) * dp <= blocks, has_block(s, device), fn)

    def if_to(q, fn):
        when(whole, sibling(q) < LAYERS, fn)

    def if_from(q, fn):
        when(whole, from_group(q) < LAYERS, fn)

    tap_tables(rows_tab, cols_tab)
    shape = pick_ref.shape
    pick_ref[...] = jnp.where(iota(shape, 0) % 16 == 9 + iota(shape, 1) // LANES, 1.0, 0.0).astype(BF16)
    for ref in (x0_ref, x1_ref):
        ref[size:size + 2 * side, :] = jnp.zeros((2 * side, chans), BF16)
    sums_ref[...] = jnp.zeros(sums_ref.shape, F32)
    for p in range(ng):
        for at in (off_qs, off_rest):
            base_out[p, at:at + 16] = jnp.zeros((16, chans), BF16)
    for p in range(LAYERS, ng):
        base_out[p, 0:off_qs] = jnp.zeros((off_qs, chans), BF16)
        base_out[p, off_qg:off_rest] = jnp.zeros((off_rest - off_qg, chans), BF16)

    arrive(0)
    slot = [owner_ref[l] % slot_total for l in range(LAYERS)]
    mine = [owner_ref[l] // slot_total == grp for l in range(LAYERS)]
    taps = qs_ref[...].astype(F32)
    level = iota(taps.shape, 1)

    def held_taps(l):
        value = jnp.sum(jnp.where((level == slot[l]) & mine[l], taps, 0.0), axis=1)
        return jnp.pad(value, ((0, 7), (0, LANES - 9))).astype(BF16)

    held = [held_taps(l) for l in range(LAYERS)]
    arrive(1)
    arrive(2)
    keep = lambda l, ref: jnp.where(mine[l], ref[slot[l]], jnp.zeros(ref.shape[1:], BF16))
    for p in range(LAYERS):
        base_out[p, 0:chans] = keep(p, qa_ref)
        base_out[p, off_qs:off_qs + 16, 0:LANES] = held[p]
        base_out[p, off_qg:off_qg + chans] = keep(p, qg_ref)
        base_out[p, off_x:off_x + chans] = keep(1 - p, qg_ref if p else qa_ref)
        base_out[p, off_rest:off_rest + 16, 0:LANES] = held[1 - p]
    for p in range(LAYERS, ng):
        base_out[p, off_qs:off_qs + 16, 0:LANES] = held[0]
        base_out[p, off_rest:off_rest + 16, 0:LANES] = held[1]
    pl.semaphore_wait(barrier, dp * ng - 1)
    for q in range(1, ng):
        for i in range(2):
            copy_base(q, i).start()

    def take_base(i):
        at, n = ((0, off_qg), (off_qg, off_rest + 16 - off_qg))[i]
        total = base_out[grp, at:at + n]
        for q in range(1, ng):
            copy_base(q, i).wait_recv()
            total = total + base_in[q - 1, at:at + n]
        base_ref[at:at + n] = total

    def local_factors(l, x_ref, g_ref, x_load):
        arrive(x_load)
        part_ref[l, 0] = channel_gram(x_ref[0:size, :], side, STRIDES[l]).astype(BF16)
        arrive(x_load + (1 if l else 1))
        part_ref[l, 1] = plain_gram(g_ref[...]).astype(BF16)
        for q in range(1, ng):
            if_to(q, lambda q=q: copy_part(l, q).start())

    def local_taps(l, x_ref):
        fsp_ref[l] = tap_gram(x_ref, rows_tab, cols_tab, sums_ref, side, STRIDES[l], outs[l])

    def chip_sum(l):
        def run():
            total = part_ref[l, grp].astype(F32)
            for q in range(1, ng):
                copy_part(l, q).wait_recv()
                total = total + peer_ref[l, q - 1].astype(F32)
            ra_ref[l] = total.astype(BF16).reshape(cube, 3 * half // cube, LANES)
        handles(run)

    def send_a(l):
        handles(lambda: each(1, cube, lambda r: copy_a(l, r).start()))

    def send_note(l):
        at = jnp.where(grp == l, jnp.where(grp == 0, 0, off_qg), off_x)
        basis = base_ref[pl.ds(pl.multiple_of(at, 16), chans), :]
        blk = ra_ref[l].reshape(3 * half, LANES)
        scale = 1.0 / (jnp.where(grp == 0, 9.0, 1.0) * positions[l])
        lam = quadratic(blk, basis) * scale
        near = grp == l if l else (grp == l) | (grp >= LAYERS)
        at = jnp.where(near, off_qs, off_rest)
        qs = base_ref[pl.ds(pl.multiple_of(at, 16), 16), 0:LANES].astype(F32)
        fsp = fsp_ref[l]
        turned = fsp[:, 0:1] * qs[0:1, :]
        for v in range(1, 9):
            turned = turned + fsp[:, v:v + 1] * qs[v:v + 1, :]
        tap = jnp.sum(turned * qs, axis=0, keepdims=True) * (1.0 / (chans * positions[l]))
        row = iota((16, LANES), 0)
        if not whole:
            lam = jnp.where(grp < LAYERS, lam, 0.0)
        note = jnp.where(row == 9, lam[:, 0:half], jnp.where(row == 10, lam[:, half:], fsp))
        note_ref[l] = jnp.where(row == 11, tap, note).astype(BF16)

        def own():
            notes_ref[grp, me] = note_ref[l]
        pl.when(grp == l)(own)
        pl.when(grp != l)(lambda: copy_note(l, 0).start())
        each(1, dp, lambda r: copy_note(l, r).start())

    def reduce_b(l):
        def run():
            each(1, cube, lambda r: copy_a(l, r).wait_recv())
            total = ra_ref[l, member].astype(F32)
            for r in range(1, cube):
                total = total + raa_ref[l, r - 1].astype(F32)
            rb_ref[l, part] = total.astype(BF16)
            for r in range(1, halves):
                copy_b(l, r).start()
        handles(run)

    def gather_c(l):
        def run():
            for r in range(1, halves):
                copy_b(l, r).wait_recv()
            total = rb_ref[l, 0].astype(F32)
            for h in range(1, halves):
                total = total + rb_ref[l, h].astype(F32)
            tot_ref[grp, l, member] = total.astype(BF16)
            each(1, cube, lambda r: copy_c(l, r).start())
            for q in range(1, ng):
                copy_d(l, 0, q).start()
        handles(run)

    def forward_d(l):
        def run():
            def step(r):
                copy_c(l, r).wait_recv()
                for q in range(1, ng):
                    copy_d(l, r, q).start()
            each(1, cube, step)
        handles(run)

    def rotate():
        qs = base_ref[off_qs:off_qs + 16, 0:LANES].astype(F32)
        parts = [w_ref[grp, :, u * chans:(u + 1) * chans] for u in range(9)]
        inner = through_basis(parts, base_ref[0:chans, :], rows, False)
        turned = mixed_taps(inner, lambda u, t: qs[u:u + 1, t:t + 1])
        per = chans // LANES
        for k in range(blocks):
            lane = (k % per) * LANES
            rot_ref[k // dp, k % dp] = turned[k // per][:, lane:lane + LANES].astype(BF16)
        for s in range(slots):
            each(1, dp, lambda r: if_block(s, lax.rem(me + r, dp), lambda: copy_rot(s, r).start()))

            def own(s=s):
                rotin_ref[s, me] = rot_ref[s, me]
            if_block(s, me, own)

    def project():
        for s in range(slots):
            def run(s=s):
                each(1, dp, lambda r: copy_rot(s, r).wait_recv())
                rot = stacked([rotin_ref[s, e] for e in range(dp)])
                proj_ref[s] = dot_rows(base_ref[off_qg:off_qg + chans, :], rot)
            if_block(s, me, run)

    def precondition():
        for k in range(ng):
            each(1, dp, lambda r: note_from(k, r).wait_recv())
            pl.when(grp != k)(lambda: note_from(k, 0).wait_recv())
        sums = []
        for k in range(ng):
            total = notes_ref[k, 0].astype(F32)
            for e in range(1, dp):
                total = total + notes_ref[k, e].astype(F32)
            sums.append(total)
        every = sums[0]
        for k in range(1, ng):
            every = every + sums[k]
        inv = jnp.where(grp == 0, 1.0 / (chans * positions[0]), 1.0 / (chans * positions[1]))
        tap_ref[grp] = every * inv
        for q in range(1, ng):
            copy_tap(q).start()
        col = dot_rows(notes_ref[1].reshape(dp * 16, LANES), pick_ref[...])
        lam_out = jnp.concatenate([col[:, 0:LANES], col[:, LANES:]], axis=0)
        lane = iota((1, LANES), 1)
        per = chans // LANES
        for s in range(slots):
            def run(s=s):
                k = s * dp + me
                tap = jnp.sum(jnp.where(lane == k // per, every[11:12, :], 0.0), axis=1, keepdims=True)
                lam_in = jnp.where(k % per == 0, sums[0][9:10, :], sums[0][10:11, :])
                coords = (proj_ref[s] / (lam_out * (lam_in * tap) + DAMPING)).astype(BF16)
                back = dot(base_ref[off_qg:off_qg + chans, :], coords)
                for e in range(dp):
                    back_ref[s, e] = back[e * rows:(e + 1) * rows].astype(BF16)
                each(1, dp, lambda r: copy_back(s, r).start())
                backin_ref[s, me] = back_ref[s, me]
            if_block(s, me, run)

    def result():
        for s in range(slots):
            each(1, dp, lambda r: if_block(s, lax.rem(me + dp - r, dp),
                                           lambda: copy_back(s, r).wait_recv()))
        qs = base_ref[off_qs:off_qs + 16, 0:LANES].astype(F32)
        per = chans // LANES
        parts = []
        for t in range(9):
            pieces = [backin_ref[k // dp, k % dp] for k in range(t * per, (t + 1) * per)]
            parts.append(jnp.concatenate(pieces, axis=1))
        turned = mixed_taps(through_basis(parts, base_ref[0:chans, :], rows, True),
                            lambda t, u: qs[u:u + 1, t:t + 1])
        for u in range(9):
            res_ref[grp, :, u * chans:(u + 1) * chans] = turned[u].astype(BF16)
        for q in range(1, ng):
            copy_res(q).start()

    scope = jax.named_scope
    with scope("first"):
        local_factors(0, x0_ref, g0_ref, 3)
    with scope("first_taps"):
        local_taps(0, x0_ref)
    arrive(5)
    with scope("rotate"):
        take_base(0)
        handles(rotate)
    with scope("first_sum"):
        chip_sum(0)
        send_a(0)
    with scope("second"):
        local_factors(1, x1_ref, g1_ref, 6)
    with scope("first_note"):
        take_base(1)
        send_note(0)
    with scope("second_taps"):
        local_taps(1, x1_ref)
    with scope("second_sum"):
        chip_sum(1)
    with scope("second_note"):
        send_note(1)
        send_a(1)
    with scope("first_b"):
        reduce_b(0)
    with scope("project"):
        handles(project)
    with scope("precondition"):
        handles(precondition)
    with scope("second_b"):
        reduce_b(1)
    with scope("first_c"):
        gather_c(0)
    with scope("result"):
        handles(result)
    with scope("second_c"):
        gather_c(1)
    with scope("forward"):
        forward_d(0)
        forward_d(1)

    with scope("rest"):
        for q in range(1, ng):
            def arrived(q=q):
                k = from_group(q)
                copy_tap(q, k).wait_recv()
                copy_res(q, k).wait_recv()
                for l in range(LAYERS):
                    each(0, cube, lambda r: copy_d(l, r, q, k).wait_recv())
            if_from(q, arrived)

    with scope("outs"):
        out_ref[...] = res_ref[...]
        tot_out[...] = tot_ref[...].reshape(tot_out.shape)
        tap_out[...] = tap_ref[...]

    with scope("sent"):
        for q in range(1, ng):
            def sent_to(q=q):
                for l in range(LAYERS):
                    copy_part(l, q).wait_send()
            if_to(q, sent_to)
            for i in range(2):
                copy_base(q, i).wait_send()
        for l in range(LAYERS):
            each(1, dp, lambda r: copy_note(l, r).wait_send())
            pl.when(grp != l)(lambda: copy_note(l, 0).wait_send())

        def sent():
            for l in range(LAYERS):
                each(1, cube, lambda r: copy_a(l, r).wait_send())
                each(1, cube, lambda r: copy_c(l, r).wait_send())
                for r in range(1, halves):
                    copy_b(l, r).wait_send()
                for q in range(1, ng):
                    each(0, cube, lambda r: copy_d(l, r, q).wait_send())
            for s in range(slots):
                each(1, dp, lambda r: if_block(s, lax.rem(me + r, dp),
                                               lambda: copy_rot(s, r).wait_send()))
                if_block(s, me, lambda: each(1, dp, lambda r: copy_back(s, r).wait_send()))
            for q in range(1, ng):
                copy_tap(q).wait_send()
                copy_res(q).wait_send()
        handles(sent)


def finish_kernel(positions, res_ref, tot_ref, tap_ref, out_ref, fin_ref, fsp_ref, fout_ref):
    for l in range(LAYERS):
        for kind, ref, scale in ((0, fin_ref, 9.0), (1, fout_ref, 1.0)):
            blk = tot_ref[kind, l].astype(F32) / (scale * positions[l])
            half = blk.shape[0] // 3
            mid = blk[half:2 * half]
            ref[l, 0:half, 0:half] = blk[0:half]
            ref[l, 0:half, half:] = mid
            ref[l, half:, 0:half] = jnp.transpose(mid)
            ref[l, half:, half:] = blk[2 * half:]
        for u in range(9):
            fsp_ref[u, l:l + 1, :] = tap_ref[l, u:u + 1, 0:9]
    out_ref[...] = res_ref[...]


def on_device(dp, ng, acts_first, grads_first, acts_second, grads_second, grad_w, owner,
              basis_in, basis_spatial, basis_out):
    images, side = acts_first.shape[0], acts_first.shape[1]
    chans = basis_in.shape[1]
    rows = grad_w.shape[1]
    slot_total = basis_in.shape[0]
    outs = (grads_first.shape[1], grads_second.shape[1])
    positions = tuple(images * o * o * dp * ng for o in outs)
    slots = -(-9 * chans // LANES // dp)
    cube = CUBE if dp % CUBE == 0 else dp
    halves = dp // cube
    half = chans // 2
    share = 3 * half // cube
    base_rows = 3 * chans + 32
    vmem = pl.BlockSpec(memory_space=pltpu.VMEM)
    smem = pl.BlockSpec(memory_space=pltpu.SMEM)
    hbm = pl.BlockSpec(memory_space=pltpu.HBM)
    struct = jax.ShapeDtypeStruct
    dma = pltpu.SemaphoreType.DMA
    bf = lambda *shape: pltpu.VMEM(shape, BF16)
    ff = lambda *shape: pltpu.VMEM(shape, F32)
    taps = jnp.transpose(basis_spatial, (1, 0, 2))

    cfg = (side, outs, chans, rows, dp, ng, slot_total, slots, positions)
    res, tot, tap = pl.pallas_call(
        functools.partial(main_kernel, cfg),
        out_shape=(struct((LAYERS, rows, 9 * chans), BF16),
                   struct((2, LAYERS, 3 * half, LANES), BF16),
                   struct((LAYERS, 16, LANES), F32)),
        in_specs=[smem] + [hbm] * 8,
        out_specs=(vmem,) * 3,
        scratch_shapes=[
            bf((side + 2) * side, chans), bf(outs[0] * outs[0], chans),
            bf((side + 2) * side, chans), bf(outs[1] * outs[1], chans),
            bf(*grad_w.shape), bf(*basis_in.shape), bf(*basis_out.shape), bf(*taps.shape),
            bf(16, 192), ff(192, LANES), bf(dp * 16, 2 * LANES), ff(32, LANES),
            bf(ng, base_rows, chans), bf(ng - 1, base_rows, chans),
            bf(base_rows, chans),
            bf(LAYERS, 2, 3 * half, LANES), bf(LAYERS, ng - 1, 3 * half, LANES),
            bf(LAYERS, cube, share, LANES), bf(LAYERS, max(cube - 1, 1), share, LANES),
            bf(LAYERS, halves, share, LANES), bf(2, LAYERS, cube, share, LANES),
            ff(LAYERS, 16, LANES), bf(LAYERS, 16, LANES), bf(ng, dp, 16, LANES),
            bf(slots, dp, rows, LANES), bf(slots, dp, rows, LANES), ff(slots, chans, LANES),
            bf(slots, dp, rows, LANES), bf(slots, dp, rows, LANES), ff(LAYERS, 16, LANES),
            bf(LAYERS, rows, 9 * chans),
            dma((8,)), dma((ng, 2)), dma((ng, 2)), dma((LAYERS, ng)), dma((LAYERS, ng)),
            dma((LAYERS, cube)), dma((LAYERS, cube)), dma((LAYERS, halves)), dma((LAYERS, halves)),
            dma((LAYERS, cube)), dma((LAYERS, cube)), dma((LAYERS, cube, ng)), dma((LAYERS, cube, ng)),
            dma((slots, dp)), dma((slots, dp)), dma((slots, dp)), dma((slots, dp)),
            dma((LAYERS, dp)), dma((ng, dp)), dma((ng,)), dma((ng,)), dma((ng,)), dma((ng,))],
        compiler_params=pltpu.CompilerParams(collective_id=0, has_side_effects=True,
                                             vmem_limit_bytes=32 << 20),
        name="precondition",
    )(owner, acts_first.reshape(-1, chans), grads_first.reshape(-1, chans),
      acts_second.reshape(-1, chans), grads_second.reshape(-1, chans), grad_w, basis_in,
      basis_out, taps)

    out, fin, fsp, fout = pl.pallas_call(
        functools.partial(finish_kernel, positions),
        out_shape=(struct((LAYERS, rows, 9 * chans), BF16), struct((LAYERS, chans, chans), F32),
                   struct((9, LAYERS, 9), F32), struct((LAYERS, chans, chans), F32)),
        in_specs=[vmem] * 3,
        out_specs=(vmem,) * 4,
        name="finish",
    )(res, tot, tap)
    return out, fin, jnp.transpose(fsp, (1, 0, 2)), fout


def solution(mesh):
    placed = (
        P(("dp", "group"), None, None, None),
        P(("dp", "group"), None, None, None),
        P(("dp", "group"), None, None, None),
        P(("dp", "group"), None, None, None),
        P(None, "dp", None),
        P(),
        P("group", None, None),
        P("group", None, None),
        P("group", None, None),
    )
    return jax.shard_map(
        functools.partial(on_device, mesh.shape["dp"], mesh.shape["group"]),
        mesh=mesh,
        in_specs=placed,
        out_specs=(P(None, "dp", None), P(), P(), P()),
        check_vma=False,
    )
```

```python
import functools

import jax
import jax.numpy as jnp
from jax import lax
from jax.experimental import pallas as pl
from jax.experimental.pallas import tpu as pltpu
from jax.sharding import PartitionSpec as P

LAYERS = 2
STRIDES = (1, 2)
DAMPING = 0.1
LANES = 128
CUBE = 8
MESH = pl.DeviceIdType.MESH
F32 = jnp.float32
BF16 = jnp.bfloat16
I32 = jnp.int32
CONTRACT_ROWS = (((0,), (0,)), ((), ()))
CONTRACT_COLS = (((1,), (1,)), ((), ()))
PAIRS = ((0, 0), (1, 1), (2, 2), (0, 1), (1, 2), (0, 2))


def dot(a, b):
    return jnp.dot(a, b, preferred_element_type=F32)


def dot_rows(a, b):
    return lax.dot_general(a, b, CONTRACT_ROWS, preferred_element_type=F32)


def dot_cols(a, b):
    return lax.dot_general(a, b, CONTRACT_COLS, preferred_element_type=F32)


def iota(shape, dim):
    return lax.broadcasted_iota(I32, shape, dim)


def each(start, stop, fn):
    def body(k, c):
        fn(k)
        return c
    lax.fori_loop(start, stop, body, 0)


def when(static, cond, fn):
    if static:
        fn()
    else:
        pl.when(cond)(fn)


def stacked(pieces):
    if pieces[0].shape[0] % 16 == 0:
        return jnp.concatenate(pieces, axis=0)
    return jnp.concatenate([piece.astype(F32) for piece in pieces], axis=0).astype(BF16)


def packed(left, right):
    half = left.shape[0]
    return jnp.concatenate([left[:, :half], left[:, half:], right], axis=0)


def channel_gram(x, side, stride):
    chans = x.shape[1]
    half = chans // 2
    col = iota((side, chans), 0)
    x3 = x.reshape(side, side, chans)

    def weighted(by_row):
        return jnp.concatenate([x3[i] * by_row(i) for i in range(side)], axis=0)

    lead, rest = x[:, :half], x[:, half:]
    if stride == 1:
        edge = (col == 0) | (col == side - 1)
        high_in = jnp.where(edge, 4.0, 8.0).astype(BF16)
        high_edge = jnp.full((side, chans), 4.0, BF16)
        low_in = jnp.where(edge, 2.0, 1.0).astype(BF16)
        low_edge = jnp.where(edge, 0.0, 2.0).astype(BF16)
        at_edge = lambda i: i in (0, side - 1)
        high = weighted(lambda i: high_edge if at_edge(i) else high_in)
        low = weighted(lambda i: low_edge if at_edge(i) else low_in)
        left = dot_rows(lead, high) + dot_rows(lead, low)
        right = dot_rows(rest, high[:, half:]) + dot_rows(rest, low[:, half:])
    else:
        odd = (col % 2 == 1) & (col < side - 1)
        once = jnp.where(odd, 2.0, 1.0).astype(BF16)
        twice = jnp.where(odd, 4.0, 2.0).astype(BF16)
        w = weighted(lambda i: twice if i % 2 == 1 and i < side - 1 else once)
        left, right = dot_rows(lead, w), dot_rows(rest, w[:, half:])
    return packed(left, right)


def plain_gram(g):
    half = g.shape[1] // 2
    return packed(dot_rows(g[:, :half], g), dot_rows(g[:, half:], g[:, half:]))


def tap_places(k):
    form, rest = k // 96, k % 96
    first = rest // 32
    rest = rest % 32
    pair, second = rest // 5, first + rest % 5 - 2
    a = jnp.where(pair < 3, pair, jnp.where(pair == 4, 1, 0))
    b = jnp.where(pair < 3, pair, jnp.where(pair == 3, 1, 2))
    one, two = 3 * a + first, 3 * b + second
    stands = (rest < 30) & (second >= 0) & (second < 3) & ((form == 0) | (pair >= 3))
    return jnp.where(form == 0, one, two), jnp.where(form == 0, two, one), stands


def tap_tables(ones_ref, twos_ref, flat_ref):
    row, col, stands = tap_places(iota(ones_ref.shape, 0))
    lane = iota(ones_ref.shape, 1)
    ones_ref[...] = jnp.where((row == lane) & stands, 1.0, 0.0).astype(BF16)
    twos_ref[...] = jnp.where((col == lane) & stands, 1.0, 0.0).astype(BF16)
    row, col, stands = tap_places(iota(flat_ref.shape, 0))
    flat_ref[...] = jnp.where((9 * row + col == iota(flat_ref.shape, 1)) & stands, 1.0, 0.0)


def tap_gram(x_ref, sums_ref, side, stride, out_side):
    per = LANES // side
    total = None
    for q in range(side // per):
        at = q * LANES
        term = dot_cols(x_ref[at:at + LANES + 2 * side, :], x_ref[at:at + LANES, :])
        total = term if total is None else total + term
    shape = (side, LANES)
    below, lane = iota(shape, 0), iota(shape, 1)
    block, col = lane // side, lane % side

    def row_pairs(dy):
        out = total[(per - 1 + dy) * side:(per + dy) * side]
        for r in range(per - 1):
            out = jnp.where(block == r, total[(r + dy) * side:(r + dy + 1) * side], out)
        return out

    same, one, two = row_pairs(0), row_pairs(1), row_pairs(2)
    size = side * side
    last = jnp.where(block == per - 1,
                     dot_cols(x_ref[size - side:size, :], x_ref[size - LANES:size, :]), 0.0)
    if stride == 1:
        first = jnp.where(block == 0, dot_cols(x_ref[0:side, :], x_ref[0:LANES, :]), 0.0)
        by_pair = (same - last, same, same - first, one, one, two)
    else:
        even = block % 2 == 0
        odd_same = jnp.where(even, 0.0, same)
        by_pair = (odd_same - last, jnp.where(even, same, 0.0), odd_same,
                   jnp.where(even, 0.0, one), jnp.where(even, one, 0.0), jnp.where(even, 0.0, two))
    for p in range(6):
        for d in range(5):
            k = 5 * p + d
            sums_ref[k:k + 1, :] = jnp.sum(jnp.where(below - col == d - 2, by_pair[p], 0.0),
                                           axis=0, keepdims=True)
    sums = sums_ref[...]
    col = iota(sums.shape, 1) % side
    values = []
    for b in range(3):
        base = col + 1 - b
        mask = (base >= 0) & (base <= stride * (out_side - 1)) & (base % stride == 0)
        values.append(jnp.sum(jnp.where(mask, sums, 0.0), axis=1, keepdims=True))
    return jnp.concatenate(values + values, axis=0)


def through_basis(parts, basis, rows, flip):
    product = (lambda a: dot_cols(a, basis)) if flip else (lambda a: dot(a, basis))
    if rows % 16 == 0:
        whole = product(jnp.concatenate(parts, axis=0))
        return [whole[u * rows:(u + 1) * rows] for u in range(9)]
    return [product(part) for part in parts]


def mixed_taps(parts, coef):
    out = []
    for t in range(9):
        total = parts[0] * coef(0, t)
        for u in range(1, 9):
            total = total + parts[u] * coef(u, t)
        out.append(total)
    return out


def quadratic(blocks, basis):
    half = blocks.shape[0] // 3
    upper = jnp.concatenate([blocks[0:half], blocks[half:2 * half] * 2], axis=1)
    total = jnp.sum(basis[0:half].astype(F32) * dot(upper, basis), axis=0, keepdims=True)
    rest = basis[half:]
    return total + jnp.sum(rest.astype(F32) * dot(blocks[2 * half:], rest), axis=0, keepdims=True)


def remote(src, dst, send, recv, to):
    return pltpu.make_async_remote_copy(src_ref=src, dst_ref=dst, send_sem=send, recv_sem=recv,
                                        device_id=to, device_id_type=MESH)


def main_kernel(cfg, owner_ref, x0_hbm, g0_hbm, x1_hbm, g1_hbm, w_hbm, qa_hbm, qg_hbm, qs_hbm,
                out_ref, tot_out, tap_out, *scratch):
    side, outs, chans, rows, dp, ng, slot_total, slots, positions = cfg
    (x0_ref, g0_ref, x1_ref, g1_ref, w_ref, qa_ref, qg_ref, qs_ref,
     ones_ref, twos_ref, flat_ref, pick_ref, table_ref, sums_ref, base_out, base_in, base_ref, part_ref, peer_ref,
     ra_ref, raa_ref, rb_ref, tot_ref, tap_ref, note_ref, notes_ref,
     rot_ref, rotin_ref, proj_ref, back_ref, backin_ref, fsp_ref, res_ref,
     loads, s_base, r_base, s_part, r_part, s_a, r_a, s_b, r_b, s_c, r_c, s_d, r_d,
     s_rot, r_rot, s_back, r_back, s_note, r_note, s_tap, r_tap, s_res, r_res) = scratch
    me, grp = lax.axis_index("dp"), lax.axis_index("group")
    cube = CUBE if dp % CUBE == 0 else dp
    halves = dp // cube
    member, part = lax.rem(me, cube), me // cube
    half = chans // 2
    blocks = 9 * chans // LANES
    size = side * side
    whole = ng == LAYERS
    off_qs, off_qg, off_x, off_rest = chans, chans + 16, 2 * chans + 16, 3 * chans + 16
    handles = lambda fn: when(whole, grp < LAYERS, fn)

    pairs = ((qs_hbm, qs_ref), (qa_hbm, qa_ref), (qg_hbm, qg_ref), (x0_hbm, x0_ref.at[pl.ds(0, size)]),
             (g0_hbm, g0_ref), (w_hbm, w_ref), (x1_hbm, x1_ref.at[pl.ds(0, size)]), (g1_hbm, g1_ref))
    copies = [pltpu.make_async_copy(src, dst, loads.at[i]) for i, (src, dst) in enumerate(pairs)]
    for copy in copies:
        copy.start()
    arrive = lambda i: copies[i].wait()

    barrier = pltpu.get_barrier_semaphore()
    with jax.named_scope("greet"):
        for q in range(ng):
            to_grp = lax.rem(grp + q, ng)
            each(0 if q else 1, dp, lambda r, to_grp=to_grp: pl.semaphore_signal(
                barrier, inc=1, device_id={"dp": lax.rem(me + r, dp), "group": to_grp},
                device_id_type=MESH))

    def sibling(q):
        return lax.rem(grp + q, ng)

    def from_group(q):
        return lax.rem(grp + ng - q, ng)

    def copy_base(q, i):
        at, n = ((0, off_qg), (off_qg, off_rest + 16 - off_qg))[i]
        return remote(base_out.at[sibling(q), pl.ds(at, n)], base_in.at[q - 1, pl.ds(at, n)],
                      s_base.at[q - 1, i], r_base.at[q - 1, i], {"group": sibling(q)})

    def copy_part(l, q):
        return remote(part_ref.at[l, sibling(q)], peer_ref.at[l, q - 1], s_part.at[l, q - 1],
                      r_part.at[l, q - 1], {"group": sibling(q)})

    def copy_a(l, r):
        to = lax.rem(member + r, cube)
        return remote(ra_ref.at[l, to], raa_ref.at[l, r - 1], s_a.at[l], r_a.at[l],
                      {"dp": part * cube + to})

    def all_a(l):
        return remote(raa_ref.at[l], raa_ref.at[l], s_a.at[l], r_a.at[l], {"dp": me})

    def copy_b(l, r):
        to = lax.rem(part + r, halves)
        return remote(rb_ref.at[l, part], rb_ref.at[l, part], s_b.at[l, r - 1], r_b.at[l, r - 1],
                      {"dp": to * cube + member})

    def copy_c(l, r):
        to = lax.rem(member + r, cube)
        block = tot_ref.at[grp, l, member]
        return remote(block, block, s_c.at[l], r_c.at[l], {"dp": part * cube + to})

    def all_c(l):
        blocks = tot_ref.at[grp, l, pl.ds(0, cube - 1)]
        return remote(blocks, blocks, s_c.at[l], r_c.at[l], {"dp": me})

    def copy_d(l, q, k=grp):
        return remote(tot_ref.at[k, l], tot_ref.at[k, l], s_d.at[l, q - 1], r_d.at[l, q - 1],
                      {"group": sibling(q)})

    def copy_rot(r):
        to = lax.rem(me + r, dp)
        return remote(rot_ref.at[to], rotin_ref.at[0, me], s_rot.at[0], r_rot.at[0], {"dp": to})

    def copy_rot_late(k):
        to = k % dp
        return remote(rot_ref.at[k], rotin_ref.at[k // dp, me], s_rot.at[1 + k - dp],
                      r_rot.at[k // dp], {"dp": to})

    def all_rot(s):
        blocks = rotin_ref.at[s, pl.ds(0, dp - 1)]
        return remote(blocks, blocks, s_rot.at[0], r_rot.at[s], {"dp": me})

    def copy_back(s, r):
        to = lax.rem(me + r, dp)
        k = s * dp + me
        recv = r_back.at[0] if s == 0 else r_back.at[k - dp + 1]
        return remote(back_ref.at[s, to], backin_ref.at[k], s_back.at[s], recv, {"dp": to})

    def all_back(s):
        some = backin_ref.at[pl.ds(0, dp - 1)]
        return remote(some, some, s_back.at[s], r_back.at[0], {"dp": me})

    def back_from(k):
        return remote(backin_ref.at[k], backin_ref.at[k], s_back.at[0], r_back.at[k - dp + 1],
                      {"dp": me})

    def copy_note(l, r):
        return remote(note_ref.at[l], notes_ref.at[grp * dp + me], s_note, r_note,
                      {"dp": lax.rem(me + r, dp), "group": l})

    def all_notes(n):
        some = notes_ref.at[pl.ds(0, n)]
        return remote(some, some, s_note, r_note, {"dp": me})

    def copy_tap(q, k=grp):
        return remote(tap_ref.at[k], tap_ref.at[k], s_tap.at[q - 1], r_tap.at[q - 1],
                      {"group": sibling(q)})

    def copy_res(q, k=grp):
        return remote(res_ref.at[k], res_ref.at[k], s_res.at[q - 1], r_res.at[q - 1],
                      {"group": sibling(q)})

    late = range(dp, blocks)

    def if_block(s, device, fn):
        when((s + 1) * dp <= blocks, s * dp + device < blocks, fn)

    def if_to(q, fn):
        when(whole, sibling(q) < LAYERS, fn)

    def if_from(q, fn):
        when(whole, from_group(q) < LAYERS, fn)

    scope = jax.named_scope
    with scope("tables"):
        tap_tables(ones_ref, twos_ref, flat_ref)
        shape = pick_ref.shape
        pick_ref[...] = jnp.where(iota(shape, 0) % 4 == 1 + iota(shape, 1) // LANES, 1.0, 0.0)
        for ref in (x0_ref, x1_ref):
            ref[size:size + 2 * side, :] = jnp.zeros((2 * side, chans), BF16)
        sums_ref[...] = jnp.zeros(sums_ref.shape, F32)
        note_ref[...] = jnp.zeros(note_ref.shape, F32)
        for p in range(ng):
            for at in (off_qs, off_rest):
                base_out[p, at:at + 16] = jnp.zeros((16, chans), BF16)
        for p in range(LAYERS, ng):
            base_out[p, 0:off_qs] = jnp.zeros((off_qs, chans), BF16)
            base_out[p, off_qg:off_rest] = jnp.zeros((off_rest - off_qg, chans), BF16)

    with scope("held"):
        arrive(0)
        slot = [owner_ref[l] % slot_total for l in range(LAYERS)]
        mine = [owner_ref[l] // slot_total == grp for l in range(LAYERS)]
        taps = qs_ref[...].astype(F32)
        level = iota(taps.shape, 1)

        def held_taps(l):
            value = jnp.sum(jnp.where((level == slot[l]) & mine[l], taps, 0.0), axis=1)
            return jnp.pad(value, ((0, 7), (0, LANES - 9))).astype(BF16)

        held = [held_taps(l) for l in range(LAYERS)]
    with scope("mask"):
        arrive(1)
        arrive(2)
        keep = lambda l, ref: jnp.where(mine[l], ref[slot[l]], jnp.zeros(ref.shape[1:], BF16))
        for p in range(LAYERS):
            base_out[p, 0:chans] = keep(p, qa_ref)
            base_out[p, off_qs:off_qs + 16, 0:LANES] = held[p]
            base_out[p, off_qg:off_qg + chans] = keep(p, qg_ref)
            base_out[p, off_x:off_x + chans] = keep(1 - p, qg_ref if p else qa_ref)
            base_out[p, off_rest:off_rest + 16, 0:LANES] = held[1 - p]
        for p in range(LAYERS, ng):
            base_out[p, off_qs:off_qs + 16, 0:LANES] = held[0]
            base_out[p, off_rest:off_rest + 16, 0:LANES] = held[1]

    def take_base(i):
        at, n = ((0, off_qg), (off_qg, off_rest + 16 - off_qg))[i]
        total = base_out[grp, at:at + n]
        for q in range(1, ng):
            copy_base(q, i).wait_recv()
            total = total + base_in[q - 1, at:at + n]
        base_ref[at:at + n] = total

    def tap_table(l):
        near = grp == l if l else (grp == l) | (grp >= LAYERS)
        at = jnp.where(near, off_qs, off_rest)
        qs = base_ref[pl.ds(pl.multiple_of(at, 16), 16), 0:LANES]
        both = dot(ones_ref[...], qs) * dot(twos_ref[...], qs)
        table_ref[l] = flat_ref[...] + pltpu.roll(both, 96, 1)

    def local_factors(l, x_ref, g_ref, x_load):
        arrive(x_load)
        part_ref[l, 0] = channel_gram(x_ref[0:size, :], side, STRIDES[l]).astype(BF16)
        arrive(x_load + 1)
        part_ref[l, 1] = plain_gram(g_ref[...]).astype(BF16)

    def send_part(l):
        for q in range(1, ng):
            if_to(q, lambda q=q: copy_part(l, q).start())

    def local_taps(l, x_ref):
        values = tap_gram(x_ref, sums_ref, side, STRIDES[l], outs[l])
        fsp_ref[l] = jnp.sum(values * table_ref[l], axis=0, keepdims=True)

    def chip_sum(l):
        def run():
            total = part_ref[l, grp].astype(F32)
            for q in range(1, ng):
                copy_part(l, q).wait_recv()
                total = total + peer_ref[l, q - 1].astype(F32)
            ra_ref[l] = total.astype(BF16).reshape(cube, 3 * half // cube, LANES)
        handles(run)

    def send_a(l):
        handles(lambda: each(1, cube, lambda r: copy_a(l, r).start()))

    def send_note(l):
        at = jnp.where(grp == l, jnp.where(grp == 0, 0, off_qg), off_x)
        basis = base_ref[pl.ds(pl.multiple_of(at, 16), chans), :]
        blk = ra_ref[l].reshape(3 * half, LANES)
        scale = 1.0 / (jnp.where(grp == 0, 9.0, 1.0) * positions[l])
        lam = quadratic(blk, basis) * scale
        note_ref[l, 0:1] = fsp_ref[l]
        if not whole:
            lam = jnp.where(grp < LAYERS, lam, 0.0)
        note_ref[l, 1:2] = lam[:, 0:half]
        note_ref[l, 2:3] = lam[:, half:]

        def own():
            notes_ref[grp * dp + me] = note_ref[l]
        pl.when(grp == l)(own)
        pl.when(grp != l)(lambda: copy_note(l, 0).start())
        each(1, dp, lambda r: copy_note(l, r).start())

    def reduce_b(l):
        def run():
            all_a(l).wait_recv()
            total = ra_ref[l, member].astype(F32)
            for r in range(1, cube):
                total = total + raa_ref[l, r - 1].astype(F32)
            rb_ref[l, part] = total.astype(BF16)
            for r in range(1, halves):
                copy_b(l, r).start()
        handles(run)

    def gather_c(l):
        def run():
            for r in range(1, halves):
                copy_b(l, r).wait_recv()
            total = rb_ref[l, 0].astype(F32)
            for h in range(1, halves):
                total = total + rb_ref[l, h].astype(F32)
            tot_ref[grp, l, member] = total.astype(BF16)
            each(1, cube, lambda r: copy_c(l, r).start())
        handles(run)

    def forward_d(l):
        def run():
            all_c(l).wait_recv()
            for q in range(1, ng):
                copy_d(l, q).start()
        handles(run)

    def rotate():
        qs = base_ref[off_qs:off_qs + 16, 0:LANES].astype(F32)
        parts = [w_ref[grp, :, u * chans:(u + 1) * chans] for u in range(9)]
        inner = through_basis(parts, base_ref[0:chans, :], rows, False)
        turned = mixed_taps(inner, lambda u, t: qs[u:u + 1, t:t + 1])
        per = chans // LANES
        for k in range(blocks):
            lane = (k % per) * LANES
            rot_ref[k] = turned[k // per][:, lane:lane + LANES].astype(BF16)
        if dp <= blocks:
            each(1, dp, lambda r: copy_rot(r).start())
        else:
            each(1, dp, lambda r: pl.when(lax.rem(me + r, dp) < blocks)(lambda: copy_rot(r).start()))
        for k in late:
            pl.when(me != k % dp)(lambda k=k: copy_rot_late(k).start())
        for s in range(slots):
            def own(s=s):
                rotin_ref[s, me] = rot_ref[s * dp + me]
            if_block(s, me, own)

    def project():
        for s in range(slots):
            def run(s=s):
                all_rot(s).wait_recv()
                rot = stacked([rotin_ref[s, e] for e in range(dp)])
                proj_ref[s] = dot_rows(base_ref[off_qg:off_qg + chans, :], rot)
            if_block(s, me, run)

    def precondition():
        with jax.named_scope("notes"):
            all_notes(ng * dp - 1).wait_recv()
        sums = []
        for k in range(ng):
            total = notes_ref[k * dp]
            for e in range(1, dp):
                total = total + notes_ref[k * dp + e]
            sums.append(total)
        every = sums[0]
        for k in range(1, ng):
            every = every + sums[k]
        inv = jnp.where(grp == 0, 1.0 / (chans * positions[0]), 1.0 / (chans * positions[1]))
        every = every[0:1] * inv
        tap_ref[grp] = every
        for q in range(1, ng):
            copy_tap(q).start()
        high = sums[1].astype(BF16).astype(F32)
        col = dot_rows(jnp.concatenate([high, sums[1] - high], axis=0), pick_ref[...])
        lam_out = jnp.concatenate([col[:, 0:LANES], col[:, LANES:]], axis=0)
        lane = iota((1, LANES), 1)
        per = chans // LANES
        for s in range(slots):
            def run(s=s):
                k = s * dp + me
                tap = jnp.sum(jnp.where(lane == 96 + k // per, every, 0.0), axis=1, keepdims=True)
                lam_in = jnp.where(k % per == 0, sums[0][1:2, :], sums[0][2:3, :])
                coords = (proj_ref[s] / (lam_out * (lam_in * tap) + DAMPING)).astype(BF16)
                back = dot(base_ref[off_qg:off_qg + chans, :], coords)
                for e in range(dp):
                    back_ref[s, e] = back[e * rows:(e + 1) * rows].astype(BF16)
                each(1, dp, lambda r: copy_back(s, r).start())
                backin_ref[s * dp + me] = back_ref[s, me]
            if_block(s, me, run)

    def result():
        with jax.named_scope("back"):
            if dp <= blocks:
                all_back(0).wait_recv()
            else:
                each(0, blocks, lambda k: pl.when(me != k)(
                    lambda: remote(backin_ref.at[k], backin_ref.at[k], s_back.at[0], r_back.at[0],
                                   {"dp": me}).wait_recv()))
            for k in late:
                pl.when(me != k % dp)(lambda k=k: back_from(k).wait_recv())
        qs = base_ref[off_qs:off_qs + 16, 0:LANES].astype(F32)
        per = chans // LANES
        parts = []
        for t in range(9):
            pieces = [backin_ref[k] for k in range(t * per, (t + 1) * per)]
            parts.append(jnp.concatenate(pieces, axis=1))
        turned = mixed_taps(through_basis(parts, base_ref[0:chans, :], rows, True),
                            lambda t, u: qs[u:u + 1, t:t + 1])
        for u in range(9):
            res_ref[grp, :, u * chans:(u + 1) * chans] = turned[u].astype(BF16)
        for q in range(1, ng):
            copy_res(q).start()

    with scope("first"):
        local_factors(0, x0_ref, g0_ref, 3)
    with scope("barrier"):
        pl.semaphore_wait(barrier, dp * ng - 1)
    for q in range(1, ng):
        for i in range(2):
            copy_base(q, i).start()
    send_part(0)
    with scope("base"):
        take_base(0)
        take_base(1)
        for l in range(LAYERS):
            tap_table(l)
    with scope("first_taps"):
        local_taps(0, x0_ref)
    with scope("first_sum"):
        chip_sum(0)
        send_a(0)
    arrive(5)
    with scope("rotate"):
        handles(rotate)
    with scope("second"):
        local_factors(1, x1_ref, g1_ref, 6)
        send_part(1)
    with scope("first_note"):
        send_note(0)
    with scope("second_taps"):
        local_taps(1, x1_ref)
    with scope("second_sum"):
        chip_sum(1)
    with scope("second_note"):
        send_note(1)
        send_a(1)
    with scope("first_b"):
        reduce_b(0)
    with scope("project"):
        handles(project)
    with scope("precondition"):
        handles(precondition)
    with scope("second_b"):
        reduce_b(1)
    with scope("first_c"):
        gather_c(0)
    with scope("second_c"):
        gather_c(1)
    with scope("forward0"):
        forward_d(0)
    with scope("result"):
        handles(result)
    with scope("forward"):
        forward_d(1)

    with scope("rest"):
        for q in range(1, ng):
            def arrived(q=q):
                k = from_group(q)
                copy_tap(q, k).wait_recv()
                copy_res(q, k).wait_recv()
                for l in range(LAYERS):
                    copy_d(l, q, k).wait_recv()
            if_from(q, arrived)

    with scope("outs"):
        out_ref[...] = res_ref[...]
        tot_out[...] = tot_ref[...].reshape(tot_out.shape)
        tap_out[...] = tap_ref[...]

    with scope("sent"):
        for q in range(1, ng):
            def sent_to(q=q):
                for l in range(LAYERS):
                    copy_part(l, q).wait_send()
            if_to(q, sent_to)
            for i in range(2):
                copy_base(q, i).wait_send()
        if whole:
            all_notes(ng * dp - 1).wait_send()
        else:
            pl.when(grp < LAYERS)(lambda: all_notes(LAYERS * dp - 1).wait_send())
            pl.when(grp >= LAYERS)(lambda: all_notes(LAYERS * dp).wait_send())

        def sent():
            for l in range(LAYERS):
                all_a(l).wait_send()
                all_c(l).wait_send()
                for r in range(1, halves):
                    copy_b(l, r).wait_send()
                for q in range(1, ng):
                    copy_d(l, q).wait_send()
            if dp <= blocks:
                all_rot(0).wait_send()
            else:
                each(1, dp, lambda r: pl.when(lax.rem(me + r, dp) < blocks)(
                    lambda: copy_rot(r).wait_send()))
            for k in late:
                pl.when(me != k % dp)(lambda k=k: copy_rot_late(k).wait_send())
            for s in range(slots):
                if_block(s, me, lambda s=s: all_back(s).wait_send())
            for q in range(1, ng):
                copy_tap(q).wait_send()
                copy_res(q).wait_send()
        handles(sent)


def finish_kernel(positions, res_ref, tot_ref, tap_ref, out_ref, fin_ref, fsp_ref, fout_ref):
    for l in range(LAYERS):
        for kind, ref, scale in ((0, fin_ref, 9.0), (1, fout_ref, 1.0)):
            blk = tot_ref[kind, l].astype(F32) / (scale * positions[l])
            half = blk.shape[0] // 3
            mid = blk[half:2 * half]
            ref[l, 0:half, 0:half] = blk[0:half]
            ref[l, 0:half, half:] = mid
            ref[l, half:, 0:half] = jnp.transpose(mid)
            ref[l, half:, half:] = blk[2 * half:]
        for u in range(9):
            fsp_ref[u, l:l + 1, :] = tap_ref[l, 0:1, 9 * u:9 * u + 9]
    out_ref[...] = res_ref[...]


def on_device(dp, ng, acts_first, grads_first, acts_second, grads_second, grad_w, owner,
              basis_in, basis_spatial, basis_out):
    images, side = acts_first.shape[0], acts_first.shape[1]
    chans = basis_in.shape[1]
    rows = grad_w.shape[1]
    slot_total = basis_in.shape[0]
    outs = (grads_first.shape[1], grads_second.shape[1])
    positions = tuple(images * o * o * dp * ng for o in outs)
    slots = -(-9 * chans // LANES // dp)
    cube = CUBE if dp % CUBE == 0 else dp
    halves = dp // cube
    half = chans // 2
    share = 3 * half // cube
    base_rows = 3 * chans + 32
    extra = max(9 * chans // LANES - dp, 0)
    vmem = pl.BlockSpec(memory_space=pltpu.VMEM)
    smem = pl.BlockSpec(memory_space=pltpu.SMEM)
    hbm = pl.BlockSpec(memory_space=pltpu.HBM)
    struct = jax.ShapeDtypeStruct
    dma = pltpu.SemaphoreType.DMA
    bf = lambda *shape: pltpu.VMEM(shape, BF16)
    ff = lambda *shape: pltpu.VMEM(shape, F32)
    taps = jnp.transpose(basis_spatial, (1, 0, 2))

    cfg = (side, outs, chans, rows, dp, ng, slot_total, slots, positions)
    res, tot, tap = pl.pallas_call(
        functools.partial(main_kernel, cfg),
        out_shape=(struct((LAYERS, rows, 9 * chans), BF16),
                   struct((2, LAYERS, 3 * half, LANES), BF16),
                   struct((LAYERS, 1, LANES), F32)),
        in_specs=[smem] + [hbm] * 8,
        out_specs=(vmem,) * 3,
        scratch_shapes=[
            bf((side + 2) * side, chans), bf(outs[0] * outs[0], chans),
            bf((side + 2) * side, chans), bf(outs[1] * outs[1], chans),
            bf(*grad_w.shape), bf(*basis_in.shape), bf(*basis_out.shape), bf(*taps.shape),
            bf(192, 16), bf(192, 16), ff(192, LANES), ff(8, 2 * LANES), ff(LAYERS, 192, LANES), ff(32, LANES),
            bf(ng, base_rows, chans), bf(ng - 1, base_rows, chans),
            bf(base_rows, chans),
            bf(LAYERS, 2, 3 * half, LANES), bf(LAYERS, ng - 1, 3 * half, LANES),
            bf(LAYERS, cube, share, LANES), bf(LAYERS, max(cube - 1, 1), share, LANES),
            bf(LAYERS, halves, share, LANES), bf(2, LAYERS, cube, share, LANES),
            ff(LAYERS, 1, LANES), ff(LAYERS, 4, LANES), ff(ng * dp, 4, LANES),
            bf(max(9 * chans // LANES, slots * dp), rows, LANES), bf(slots, dp, rows, LANES), ff(slots, chans, LANES),
            bf(slots, dp, rows, LANES), bf(slots * dp, rows, LANES), ff(LAYERS, 1, LANES),
            bf(LAYERS, rows, 9 * chans),
            dma((8,)), dma((ng - 1, 2)), dma((ng - 1, 2)), dma((LAYERS, ng - 1)), dma((LAYERS, ng - 1)),
            dma((LAYERS,)), dma((LAYERS,)), dma((LAYERS, max(halves - 1, 1))), dma((LAYERS, max(halves - 1, 1))),
            dma((LAYERS,)), dma((LAYERS,)), dma((LAYERS, ng - 1)), dma((LAYERS, ng - 1)),
            dma((extra + 1,)), dma((slots,)), dma((slots,)), dma((extra + 1,)),
            dma, dma, dma((ng - 1,)), dma((ng - 1,)), dma((ng - 1,)), dma((ng - 1,))],
        compiler_params=pltpu.CompilerParams(collective_id=0, has_side_effects=True,
                                             vmem_limit_bytes=62 << 20),
        name="precondition",
    )(owner, acts_first.reshape(-1, chans), grads_first.reshape(-1, chans),
      acts_second.reshape(-1, chans), grads_second.reshape(-1, chans), grad_w, basis_in,
      basis_out, taps)

    out, fin, fsp, fout = pl.pallas_call(
        functools.partial(finish_kernel, positions),
        out_shape=(struct((LAYERS, rows, 9 * chans), BF16), struct((LAYERS, chans, chans), F32),
                   struct((9, LAYERS, 9), F32), struct((LAYERS, chans, chans), F32)),
        in_specs=[vmem] * 3,
        out_specs=(vmem,) * 4,
        compiler_params=pltpu.CompilerParams(vmem_limit_bytes=62 << 20),
        name="finish",
    )(res, tot, tap)
    return out, fin, jnp.transpose(fsp, (1, 0, 2)), fout


def solution(mesh):
    placed = (
        P(("dp", "group"), None, None, None),
        P(("dp", "group"), None, None, None),
        P(("dp", "group"), None, None, None),
        P(("dp", "group"), None, None, None),
        P(None, "dp", None),
        P(),
        P("group", None, None),
        P("group", None, None),
        P("group", None, None),
    )
    return jax.shard_map(
        functools.partial(on_device, mesh.shape["dp"], mesh.shape["group"]),
        mesh=mesh,
        in_specs=placed,
        out_specs=(P(None, "dp", None), P(), P(), P()),
        check_vma=False,
    )
```

```python
import functools

import jax
import jax.numpy as jnp
from jax import lax
from jax.experimental import pallas as pl
from jax.experimental.pallas import tpu as pltpu
from jax.sharding import PartitionSpec as P

LAYERS = 2
STRIDES = (1, 2)
DAMPING = 0.1
LANES = 128
CUBE = 8
MESH = pl.DeviceIdType.MESH
F32 = jnp.float32
BF16 = jnp.bfloat16
I32 = jnp.int32
CONTRACT_ROWS = (((0,), (0,)), ((), ()))
CONTRACT_COLS = (((1,), (1,)), ((), ()))
PAIRS = ((0, 0), (1, 1), (2, 2), (0, 1), (1, 2), (0, 2))


def dot(a, b):
    return jnp.dot(a, b, preferred_element_type=F32)


def dot_rows(a, b):
    return lax.dot_general(a, b, CONTRACT_ROWS, preferred_element_type=F32)


def dot_cols(a, b):
    return lax.dot_general(a, b, CONTRACT_COLS, preferred_element_type=F32)


def iota(shape, dim):
    return lax.broadcasted_iota(I32, shape, dim)


def each(start, stop, fn):
    def body(k, c):
        fn(k)
        return c
    lax.fori_loop(start, stop, body, 0)


def when(static, cond, fn):
    if static:
        fn()
    else:
        pl.when(cond)(fn)


def stacked(pieces):
    if pieces[0].shape[0] % 16 == 0:
        return jnp.concatenate(pieces, axis=0)
    return jnp.concatenate([piece.astype(F32) for piece in pieces], axis=0).astype(BF16)


def store_packed(ref, full):
    half = full.shape[0] // 2
    ref[0:half] = full[:half, :half].astype(BF16)
    ref[half:2 * half] = full[:half, half:].astype(BF16)
    ref[2 * half:] = full[half:, half:].astype(BF16)


def channel_gram(x, side, stride):
    chans = x.shape[1]
    col = iota((side, chans), 0)
    if stride == 1:
        counts = jnp.where((col == 0) | (col == side - 1), 2.0, 3.0)
        per_row = lambda i: 2.0 if i in (0, side - 1) else 3.0
    else:
        counts = jnp.where((col % 2 == 1) & (col < side - 1), 2.0, 1.0)
        per_row = lambda i: 2.0 if i % 2 == 1 and i < side - 1 else 1.0
    weights = {n: (n * counts).astype(BF16) for n in sorted({per_row(i) for i in range(side)})}
    weighted = jnp.concatenate([x[i * side:(i + 1) * side] * weights[per_row(i)]
                                for i in range(side)], axis=0)
    return dot_rows(x, weighted)


def tap_places(k):
    form, rest = k // 96, k % 96
    first = rest // 32
    rest = rest % 32
    pair, second = rest // 5, first + rest % 5 - 2
    a = jnp.where(pair < 3, pair, jnp.where(pair == 4, 1, 0))
    b = jnp.where(pair < 3, pair, jnp.where(pair == 3, 1, 2))
    one, two = 3 * a + first, 3 * b + second
    stands = (rest < 30) & (second >= 0) & (second < 3) & ((form == 0) | (pair >= 3))
    return jnp.where(form == 0, one, two), jnp.where(form == 0, two, one), stands


def tap_tables(ones_ref, twos_ref, flat_ref):
    row, col, stands = tap_places(iota(ones_ref.shape, 0))
    lane = iota(ones_ref.shape, 1)
    ones_ref[...] = jnp.where((row == lane) & stands, 1.0, 0.0).astype(BF16)
    twos_ref[...] = jnp.where((col == lane) & stands, 1.0, 0.0).astype(BF16)
    row, col, stands = tap_places(iota(flat_ref.shape, 0))
    flat_ref[...] = jnp.where((9 * row + col == iota(flat_ref.shape, 1)) & stands, 1.0, 0.0)


def tap_gram(x_ref, sums_ref, side, stride, out_side):
    per = 2 * LANES // side
    terms = []
    for q in range(side // per):
        at = 2 * q * LANES
        terms.append(dot_cols(x_ref[at:at + 2 * LANES + 2 * side, :], x_ref[at:at + 2 * LANES, :]))
    total = terms[0]
    for term in terms[1:]:
        total = total + term
    shape = (side, LANES)
    below, lane = iota(shape, 0), iota(shape, 1)
    block, col = lane // side, lane % side

    def row_pairs(dy):
        out = None
        for h in range(2):
            lanes = slice(h * LANES, (h + 1) * LANES)
            pick = None
            for r in range(per // 2):
                at = (h * per // 2 + r + dy) * side
                rows = total[at:at + side, lanes]
                pick = rows if pick is None else jnp.where(block == r, rows, pick)
            out = pick if out is None else out + pick
        return out

    same, one, two = row_pairs(0), row_pairs(1), row_pairs(2)
    last = jnp.where(block == per // 2 - 1, terms[-1][(per - 1) * side:per * side, LANES:], 0.0)
    if stride == 1:
        first = jnp.where(block == 0, terms[0][0:side, 0:LANES], 0.0)
        by_pair = (same - last, same, same - first, one, one, two)
    else:
        even = block % 2 == 0
        odd_same = jnp.where(even, 0.0, same)
        by_pair = (odd_same - last, jnp.where(even, same, 0.0), odd_same,
                   jnp.where(even, 0.0, one), jnp.where(even, one, 0.0), jnp.where(even, 0.0, two))
    for p in range(6):
        for d in range(5):
            k = 5 * p + d
            sums_ref[k:k + 1, :] = jnp.sum(jnp.where(below - col == d - 2, by_pair[p], 0.0),
                                           axis=0, keepdims=True)
    sums = sums_ref[...]
    col = iota(sums.shape, 1) % side
    values = []
    for b in range(3):
        base = col + 1 - b
        mask = (base >= 0) & (base <= stride * (out_side - 1)) & (base % stride == 0)
        values.append(jnp.sum(jnp.where(mask, sums, 0.0), axis=1, keepdims=True))
    return jnp.concatenate(values + values, axis=0)


def through_basis(parts, basis, rows, flip):
    product = (lambda a: dot_cols(a, basis)) if flip else (lambda a: dot(a, basis))
    if rows % 16 == 0:
        whole = product(jnp.concatenate(parts, axis=0))
        return [whole[u * rows:(u + 1) * rows] for u in range(9)]
    return [product(part) for part in parts]


def mixed_taps(parts, coef):
    out = []
    for t in range(9):
        total = parts[0] * coef(0, t)
        for u in range(1, 9):
            total = total + parts[u] * coef(u, t)
        out.append(total)
    return out


def quadratic(blocks, basis):
    half = blocks.shape[0] // 3
    upper = jnp.concatenate([blocks[0:half], blocks[half:2 * half] * 2], axis=1)
    total = jnp.sum(basis[0:half].astype(F32) * dot(upper, basis), axis=0, keepdims=True)
    rest = basis[half:]
    return total + jnp.sum(rest.astype(F32) * dot(blocks[2 * half:], rest), axis=0, keepdims=True)


def remote(src, dst, send, recv, to):
    return pltpu.make_async_remote_copy(src_ref=src, dst_ref=dst, send_sem=send, recv_sem=recv,
                                        device_id=to, device_id_type=MESH)


def main_kernel(cfg, owner_ref, x0_hbm, g0_hbm, x1_hbm, g1_hbm, w_hbm, qa_hbm, qg_hbm, qs_hbm,
                out_ref, tot_out, tap_out, *scratch):
    side, outs, chans, rows, dp, ng, slot_total, slots, positions = cfg
    (x0_ref, g0_ref, x1_ref, g1_ref, w_ref, qa_ref, qg_ref, qs_ref,
     ones_ref, twos_ref, flat_ref, pick_ref, sums_ref, base_out, base_in, base_ref, part_ref, peer_ref,
     ra_ref, raa_ref, rb_ref, tot_ref, tap_ref, note_ref, notes_ref,
     rot_ref, rotin_ref, proj_ref, back_ref, backin_ref, fsp_ref, res_ref,
     loads, s_base, r_base, s_part, r_part, s_a, r_a, s_b, r_b, s_c, r_c, s_d, r_d,
     s_rot, r_rot, s_back, r_back, s_note, r_note, s_tap, r_tap, s_res, r_res) = scratch
    me, grp = lax.axis_index("dp"), lax.axis_index("group")
    cube = CUBE if dp % CUBE == 0 else dp
    halves = dp // cube
    member, part = lax.rem(me, cube), me // cube
    half = chans // 2
    blocks = 9 * chans // LANES
    size = side * side
    whole = ng == LAYERS
    off_qs, off_qg, off_x, off_rest = chans, chans + 16, 2 * chans + 16, 3 * chans + 16
    handles = lambda fn: when(whole, grp < LAYERS, fn)

    pairs = ((qs_hbm, qs_ref), (qa_hbm, qa_ref), (qg_hbm, qg_ref), (x0_hbm, x0_ref.at[pl.ds(0, size)]),
             (g0_hbm, g0_ref), (w_hbm, w_ref), (x1_hbm, x1_ref.at[pl.ds(0, size)]), (g1_hbm, g1_ref))
    order = (3, 4, 0, 1, 2, 6, 7, 5)
    copies = [pltpu.make_async_copy(src, dst, loads.at[i]) for i, (src, dst) in enumerate(pairs)]
    for i in order:
        copies[i].start()
    arrive = lambda i: copies[i].wait()

    barrier = pltpu.get_barrier_semaphore()
    with jax.named_scope("greet"):
        for q in range(ng):
            to_grp = lax.rem(grp + q, ng)
            each(0 if q else 1, dp, lambda r, to_grp=to_grp: pl.semaphore_signal(
                barrier, inc=1, device_id={"dp": lax.rem(me + r, dp), "group": to_grp},
                device_id_type=MESH))

    def sibling(q):
        return lax.rem(grp + q, ng)

    def from_group(q):
        return lax.rem(grp + ng - q, ng)

    def copy_base(q, i):
        at, n = ((0, off_qg), (off_qg, off_rest + 16 - off_qg))[i]
        return remote(base_out.at[sibling(q), pl.ds(at, n)], base_in.at[q - 1, pl.ds(at, n)],
                      s_base.at[q - 1, i], r_base.at[q - 1, i], {"group": sibling(q)})

    def copy_part(l, q):
        return remote(part_ref.at[l, sibling(q)], peer_ref.at[l, q - 1], s_part.at[l, q - 1],
                      r_part.at[l, q - 1], {"group": sibling(q)})

    def copy_a(l, r):
        to = lax.rem(member + r, cube)
        return remote(ra_ref.at[l, to], raa_ref.at[l, r - 1], s_a.at[l], r_a.at[l],
                      {"dp": part * cube + to})

    def all_a(l):
        return remote(raa_ref.at[l], raa_ref.at[l], s_a.at[l], r_a.at[l], {"dp": me})

    def copy_b(l, r):
        to = lax.rem(part + r, halves)
        return remote(rb_ref.at[l, part], rb_ref.at[l, part], s_b.at[l, r - 1], r_b.at[l, r - 1],
                      {"dp": to * cube + member})

    def copy_c(l, r):
        to = lax.rem(member + r, cube)
        block = tot_ref.at[grp, l, member]
        return remote(block, block, s_c.at[l], r_c.at[l], {"dp": part * cube + to})

    def all_c(l):
        blocks = tot_ref.at[grp, l, pl.ds(0, cube - 1)]
        return remote(blocks, blocks, s_c.at[l], r_c.at[l], {"dp": me})

    def copy_d(l, q, k=grp):
        return remote(tot_ref.at[k, l], tot_ref.at[k, l], s_d.at[l, q - 1], r_d.at[l, q - 1],
                      {"group": sibling(q)})

    def copy_rot(r):
        to = lax.rem(me + r, dp)
        return remote(rot_ref.at[to], rotin_ref.at[0, me], s_rot.at[0], r_rot.at[0], {"dp": to})

    def copy_rot_late(k):
        to = k % dp
        return remote(rot_ref.at[k], rotin_ref.at[k // dp, me], s_rot.at[1 + k - dp],
                      r_rot.at[k // dp], {"dp": to})

    def all_rot(s):
        blocks = rotin_ref.at[s, pl.ds(0, dp - 1)]
        return remote(blocks, blocks, s_rot.at[0], r_rot.at[s], {"dp": me})

    def copy_back(s, r):
        to = lax.rem(me + r, dp)
        k = s * dp + me
        recv = r_back.at[0] if s == 0 else r_back.at[k - dp + 1]
        return remote(back_ref.at[s, to], backin_ref.at[k], s_back.at[s], recv, {"dp": to})

    def all_back(s):
        some = backin_ref.at[pl.ds(0, dp - 1)]
        return remote(some, some, s_back.at[s], r_back.at[0], {"dp": me})

    def back_from(k):
        return remote(backin_ref.at[k], backin_ref.at[k], s_back.at[0], r_back.at[k - dp + 1],
                      {"dp": me})

    def copy_note(l, r):
        return remote(note_ref.at[l], notes_ref.at[grp * dp + me], s_note, r_note,
                      {"dp": lax.rem(me + r, dp), "group": l})

    def all_notes(n):
        some = notes_ref.at[pl.ds(0, n)]
        return remote(some, some, s_note, r_note, {"dp": me})

    def copy_tap(q, k=grp):
        return remote(tap_ref.at[k], tap_ref.at[k], s_tap.at[q - 1], r_tap.at[q - 1],
                      {"group": sibling(q)})

    def copy_res(q, k=grp):
        return remote(res_ref.at[k], res_ref.at[k], s_res.at[q - 1], r_res.at[q - 1],
                      {"group": sibling(q)})

    late = range(dp, blocks)

    def if_block(s, device, fn):
        when((s + 1) * dp <= blocks, s * dp + device < blocks, fn)

    def if_to(q, fn):
        when(whole, sibling(q) < LAYERS, fn)

    def if_from(q, fn):
        when(whole, from_group(q) < LAYERS, fn)

    scope = jax.named_scope
    with scope("tables"):
        tap_tables(ones_ref, twos_ref, flat_ref)
        shape = pick_ref.shape
        pick_ref[...] = jnp.where(iota(shape, 0) % 4 == 1 + iota(shape, 1) // LANES, 1.0, 0.0)
        for ref in (x0_ref, x1_ref):
            ref[size:size + 2 * side, :] = jnp.zeros((2 * side, chans), BF16)
        sums_ref[...] = jnp.zeros(sums_ref.shape, F32)
        note_ref[...] = jnp.zeros(note_ref.shape, F32)
        for p in range(ng):
            for at in (off_qs, off_rest):
                base_out[p, at:at + 16] = jnp.zeros((16, chans), BF16)
        for p in range(LAYERS, ng):
            base_out[p, 0:off_qs] = jnp.zeros((off_qs, chans), BF16)
            base_out[p, off_qg:off_rest] = jnp.zeros((off_rest - off_qg, chans), BF16)

    def own_bases():
        with scope("held"):
            arrive(0)
            slot = [owner_ref[l] % slot_total for l in range(LAYERS)]
            mine = [owner_ref[l] // slot_total == grp for l in range(LAYERS)]
            taps = qs_ref[...].astype(F32)
            level = iota(taps.shape, 1)

            def held_taps(l):
                value = jnp.sum(jnp.where((level == slot[l]) & mine[l], taps, 0.0), axis=1)
                return jnp.pad(value, ((0, 7), (0, LANES - 9))).astype(BF16)

            held = [held_taps(l) for l in range(LAYERS)]
        with scope("mask"):
            arrive(1)
            arrive(2)
            keep = lambda l, ref: jnp.where(mine[l], ref[slot[l]], jnp.zeros(ref.shape[1:], BF16))
            for p in range(LAYERS):
                base_out[p, 0:chans] = keep(p, qa_ref)
                base_out[p, off_qs:off_qs + 16, 0:LANES] = held[p]
                base_out[p, off_qg:off_qg + chans] = keep(p, qg_ref)
                base_out[p, off_x:off_x + chans] = keep(1 - p, qg_ref if p else qa_ref)
                base_out[p, off_rest:off_rest + 16, 0:LANES] = held[1 - p]
            for p in range(LAYERS, ng):
                base_out[p, off_qs:off_qs + 16, 0:LANES] = held[0]
                base_out[p, off_rest:off_rest + 16, 0:LANES] = held[1]

    def take_base(i):
        at, n = ((0, off_qg), (off_qg, off_rest + 16 - off_qg))[i]
        total = base_out[grp, at:at + n]
        for q in range(1, ng):
            copy_base(q, i).wait_recv()
            total = total + base_in[q - 1, at:at + n]
        base_ref[at:at + n] = total

    def tap_table(l):
        near = grp == l if l else (grp == l) | (grp >= LAYERS)
        at = jnp.where(near, off_qs, off_rest)
        qs = base_ref[pl.ds(pl.multiple_of(at, 16), 16), 0:LANES]
        both = dot(ones_ref[...], qs) * dot(twos_ref[...], qs)
        return flat_ref[...] + pltpu.roll(both, 96, 1)

    def local_factors(l, x_ref, g_ref, x_load):
        arrive(x_load)
        store_packed(part_ref.at[l, 0], channel_gram(x_ref[0:size, :], side, STRIDES[l]))
        arrive(x_load + 1)
        store_packed(part_ref.at[l, 1], dot_rows(g_ref[...], g_ref[...]))

    def send_part(l):
        for q in range(1, ng):
            if_to(q, lambda q=q: copy_part(l, q).start())

    def local_taps(l, x_ref):
        values = tap_gram(x_ref, sums_ref, side, STRIDES[l], outs[l])
        fsp_ref[l] = jnp.broadcast_to(values, fsp_ref.shape[1:])

    def chip_sum(l):
        def run():
            total = part_ref[l, grp].astype(F32)
            for q in range(1, ng):
                copy_part(l, q).wait_recv()
                total = total + peer_ref[l, q - 1].astype(F32)
            ra_ref[l] = total.astype(BF16).reshape(cube, 3 * half // cube, LANES)
        handles(run)

    def send_a(l):
        handles(lambda: each(1, cube, lambda r: copy_a(l, r).start()))

    def send_note(l):
        at = jnp.where(grp == l, jnp.where(grp == 0, 0, off_qg), off_x)
        basis = base_ref[pl.ds(pl.multiple_of(at, 16), chans), :]
        blk = ra_ref[l].reshape(3 * half, LANES)
        scale = 1.0 / (jnp.where(grp == 0, 9.0, 1.0) * positions[l])
        lam = quadratic(blk, basis) * scale
        note_ref[l, 0:1] = jnp.sum(fsp_ref[l] * tap_table(l), axis=0, keepdims=True)
        if not whole:
            lam = jnp.where(grp < LAYERS, lam, 0.0)
        note_ref[l, 1:2] = lam[:, 0:half]
        note_ref[l, 2:3] = lam[:, half:]

        def own():
            notes_ref[grp * dp + me] = note_ref[l]
        pl.when(grp == l)(own)
        pl.when(grp != l)(lambda: copy_note(l, 0).start())
        each(1, dp, lambda r: copy_note(l, r).start())

    def reduce_b(l):
        def run():
            all_a(l).wait_recv()
            total = ra_ref[l, member].astype(F32)
            for r in range(1, cube):
                total = total + raa_ref[l, r - 1].astype(F32)
            rb_ref[l, part] = total.astype(BF16)
            for r in range(1, halves):
                copy_b(l, r).start()
        handles(run)

    def gather_c(l):
        def run():
            for r in range(1, halves):
                copy_b(l, r).wait_recv()
            total = rb_ref[l, 0].astype(F32)
            for h in range(1, halves):
                total = total + rb_ref[l, h].astype(F32)
            tot_ref[grp, l, member] = total.astype(BF16)
            each(1, cube, lambda r: copy_c(l, r).start())
        handles(run)

    def forward_d(l):
        def run():
            all_c(l).wait_recv()
            for q in range(1, ng):
                copy_d(l, q).start()
        handles(run)

    def rotate():
        qs = base_ref[off_qs:off_qs + 16, 0:LANES].astype(F32)
        parts = [w_ref[grp, :, u * chans:(u + 1) * chans] for u in range(9)]
        inner = through_basis(parts, base_ref[0:chans, :], rows, False)
        turned = mixed_taps(inner, lambda u, t: qs[u:u + 1, t:t + 1])
        per = chans // LANES
        for k in range(blocks):
            lane = (k % per) * LANES
            rot_ref[k] = turned[k // per][:, lane:lane + LANES].astype(BF16)
        if dp <= blocks:
            each(1, dp, lambda r: copy_rot(r).start())
        else:
            each(1, dp, lambda r: pl.when(lax.rem(me + r, dp) < blocks)(lambda: copy_rot(r).start()))
        for k in late:
            pl.when(me != k % dp)(lambda k=k: copy_rot_late(k).start())
        for s in range(slots):
            def own(s=s):
                rotin_ref[s, me] = rot_ref[s * dp + me]
            if_block(s, me, own)

    def project():
        for s in range(slots):
            def run(s=s):
                all_rot(s).wait_recv()
                rot = stacked([rotin_ref[s, e] for e in range(dp)])
                proj_ref[s] = dot_rows(base_ref[off_qg:off_qg + chans, :], rot)
            if_block(s, me, run)

    def precondition():
        with jax.named_scope("notes"):
            all_notes(ng * dp - 1).wait_recv()
        sums = []
        for k in range(ng):
            total = notes_ref[k * dp]
            for e in range(1, dp):
                total = total + notes_ref[k * dp + e]
            sums.append(total)
        every = sums[0]
        for k in range(1, ng):
            every = every + sums[k]
        inv = jnp.where(grp == 0, 1.0 / (chans * positions[0]), 1.0 / (chans * positions[1]))
        every = every[0:1] * inv
        tap_ref[grp] = every
        for q in range(1, ng):
            copy_tap(q).start()
        high = sums[1].astype(BF16).astype(F32)
        col = dot_rows(jnp.concatenate([high, sums[1] - high], axis=0), pick_ref[...])
        lam_out = jnp.concatenate([col[:, 0:LANES], col[:, LANES:]], axis=0)
        lane = iota((1, LANES), 1)
        per = chans // LANES
        for s in range(slots):
            def run(s=s):
                k = s * dp + me
                tap = jnp.sum(jnp.where(lane == 96 + k // per, every, 0.0), axis=1, keepdims=True)
                lam_in = jnp.where(k % per == 0, sums[0][1:2, :], sums[0][2:3, :])
                coords = (proj_ref[s] / (lam_out * (lam_in * tap) + DAMPING)).astype(BF16)
                back = dot(base_ref[off_qg:off_qg + chans, :], coords)
                for e in range(dp):
                    back_ref[s, e] = back[e * rows:(e + 1) * rows].astype(BF16)
                each(1, dp, lambda r: copy_back(s, r).start())
                backin_ref[s * dp + me] = back_ref[s, me]
            if_block(s, me, run)

    def result():
        with jax.named_scope("back"):
            if dp <= blocks:
                all_back(0).wait_recv()
            else:
                each(0, blocks, lambda k: pl.when(me != k)(
                    lambda: remote(backin_ref.at[k], backin_ref.at[k], s_back.at[0], r_back.at[0],
                                   {"dp": me}).wait_recv()))
            for k in late:
                pl.when(me != k % dp)(lambda k=k: back_from(k).wait_recv())
        qs = base_ref[off_qs:off_qs + 16, 0:LANES].astype(F32)
        per = chans // LANES
        parts = []
        for t in range(9):
            pieces = [backin_ref[k] for k in range(t * per, (t + 1) * per)]
            parts.append(jnp.concatenate(pieces, axis=1))
        turned = mixed_taps(through_basis(parts, base_ref[0:chans, :], rows, True),
                            lambda t, u: qs[u:u + 1, t:t + 1])
        for u in range(9):
            res_ref[grp, :, u * chans:(u + 1) * chans] = turned[u].astype(BF16)
        for q in range(1, ng):
            copy_res(q).start()

    with scope("first"):
        local_factors(0, x0_ref, g0_ref, 3)
    own_bases()
    with scope("first_taps"):
        local_taps(0, x0_ref)
    with scope("barrier"):
        pl.semaphore_wait(barrier, dp * ng - 1)
    send_part(0)
    for q in range(1, ng):
        for i in range(2):
            copy_base(q, i).start()
    with scope("second"):
        local_factors(1, x1_ref, g1_ref, 6)
        send_part(1)
    with scope("first_sum"):
        chip_sum(0)
        send_a(0)
    with scope("second_taps"):
        local_taps(1, x1_ref)
    with scope("second_sum"):
        chip_sum(1)
        send_a(1)
    arrive(5)
    with scope("base"):
        take_base(0)
    with scope("rotate"):
        handles(rotate)
    with scope("base2"):
        take_base(1)
    with scope("first_note"):
        send_note(0)
    with scope("second_note"):
        send_note(1)
    with scope("first_b"):
        reduce_b(0)
    with scope("second_b"):
        reduce_b(1)
    with scope("project"):
        handles(project)
    with scope("precondition"):
        handles(precondition)
    with scope("first_c"):
        gather_c(0)
    with scope("second_c"):
        gather_c(1)
    with scope("forward0"):
        forward_d(0)
    with scope("result"):
        handles(result)
    with scope("forward"):
        forward_d(1)

    with scope("rest"):
        for q in range(1, ng):
            def arrived(q=q):
                k = from_group(q)
                copy_tap(q, k).wait_recv()
                copy_res(q, k).wait_recv()
                for l in range(LAYERS):
                    copy_d(l, q, k).wait_recv()
            if_from(q, arrived)

    with scope("outs"):
        out_ref[...] = res_ref[...]
        tot_out[...] = tot_ref[...].reshape(tot_out.shape)
        tap_out[...] = tap_ref[...]

    with scope("sent"):
        for q in range(1, ng):
            def sent_to(q=q):
                for l in range(LAYERS):
                    copy_part(l, q).wait_send()
            if_to(q, sent_to)
            for i in range(2):
                copy_base(q, i).wait_send()
        if whole:
            all_notes(ng * dp - 1).wait_send()
        else:
            pl.when(grp < LAYERS)(lambda: all_notes(LAYERS * dp - 1).wait_send())
            pl.when(grp >= LAYERS)(lambda: all_notes(LAYERS * dp).wait_send())

        def sent():
            for l in range(LAYERS):
                all_a(l).wait_send()
                all_c(l).wait_send()
                for r in range(1, halves):
                    copy_b(l, r).wait_send()
                for q in range(1, ng):
                    copy_d(l, q).wait_send()
            if dp <= blocks:
                all_rot(0).wait_send()
            else:
                each(1, dp, lambda r: pl.when(lax.rem(me + r, dp) < blocks)(
                    lambda: copy_rot(r).wait_send()))
            for k in late:
                pl.when(me != k % dp)(lambda k=k: copy_rot_late(k).wait_send())
            for s in range(slots):
                if_block(s, me, lambda s=s: all_back(s).wait_send())
            for q in range(1, ng):
                copy_tap(q).wait_send()
                copy_res(q).wait_send()
        handles(sent)


def finish_kernel(positions, res_ref, tot_ref, tap_ref, out_ref, fin_ref, fsp_ref, fout_ref):
    for l in range(LAYERS):
        for kind, ref, scale in ((0, fin_ref, 9.0), (1, fout_ref, 1.0)):
            blk = tot_ref[kind, l].astype(F32) / (scale * positions[l])
            half = blk.shape[0] // 3
            mid = blk[half:2 * half]
            ref[l, 0:half, 0:half] = blk[0:half]
            ref[l, 0:half, half:] = mid
            ref[l, half:, 0:half] = jnp.transpose(mid)
            ref[l, half:, half:] = blk[2 * half:]
        for u in range(9):
            fsp_ref[u, l:l + 1, :] = tap_ref[l, 0:1, 9 * u:9 * u + 9]
    out_ref[...] = res_ref[...]


def on_device(dp, ng, acts_first, grads_first, acts_second, grads_second, grad_w, owner,
              basis_in, basis_spatial, basis_out):
    images, side = acts_first.shape[0], acts_first.shape[1]
    chans = basis_in.shape[1]
    rows = grad_w.shape[1]
    slot_total = basis_in.shape[0]
    outs = (grads_first.shape[1], grads_second.shape[1])
    positions = tuple(images * o * o * dp * ng for o in outs)
    slots = -(-9 * chans // LANES // dp)
    cube = CUBE if dp % CUBE == 0 else dp
    halves = dp // cube
    half = chans // 2
    share = 3 * half // cube
    base_rows = 3 * chans + 32
    extra = max(9 * chans // LANES - dp, 0)
    vmem = pl.BlockSpec(memory_space=pltpu.VMEM)
    smem = pl.BlockSpec(memory_space=pltpu.SMEM)
    hbm = pl.BlockSpec(memory_space=pltpu.HBM)
    struct = jax.ShapeDtypeStruct
    dma = pltpu.SemaphoreType.DMA
    bf = lambda *shape: pltpu.VMEM(shape, BF16)
    ff = lambda *shape: pltpu.VMEM(shape, F32)
    taps = jnp.transpose(basis_spatial, (1, 0, 2))

    cfg = (side, outs, chans, rows, dp, ng, slot_total, slots, positions)
    res, tot, tap = pl.pallas_call(
        functools.partial(main_kernel, cfg),
        out_shape=(struct((LAYERS, rows, 9 * chans), BF16),
                   struct((2, LAYERS, 3 * half, LANES), BF16),
                   struct((LAYERS, 1, LANES), F32)),
        in_specs=[smem] + [hbm] * 8,
        out_specs=(vmem,) * 3,
        scratch_shapes=[
            bf((side + 2) * side, chans), bf(outs[0] * outs[0], chans),
            bf((side + 2) * side, chans), bf(outs[1] * outs[1], chans),
            bf(*grad_w.shape), bf(*basis_in.shape), bf(*basis_out.shape), bf(*taps.shape),
            bf(192, 16), bf(192, 16), ff(192, LANES), ff(8, 2 * LANES), ff(32, LANES),
            bf(ng, base_rows, chans), bf(ng - 1, base_rows, chans),
            bf(base_rows, chans),
            bf(LAYERS, 2, 3 * half, LANES), bf(LAYERS, ng - 1, 3 * half, LANES),
            bf(LAYERS, cube, share, LANES), bf(LAYERS, max(cube - 1, 1), share, LANES),
            bf(LAYERS, halves, share, LANES), bf(2, LAYERS, cube, share, LANES),
            ff(LAYERS, 1, LANES), ff(LAYERS, 4, LANES), ff(ng * dp, 4, LANES),
            bf(max(9 * chans // LANES, slots * dp), rows, LANES), bf(slots, dp, rows, LANES), ff(slots, chans, LANES),
            bf(slots, dp, rows, LANES), bf(slots * dp, rows, LANES), ff(LAYERS, 192, LANES),
            bf(LAYERS, rows, 9 * chans),
            dma((8,)), dma((ng - 1, 2)), dma((ng - 1, 2)), dma((LAYERS, ng - 1)), dma((LAYERS, ng - 1)),
            dma((LAYERS,)), dma((LAYERS,)), dma((LAYERS, max(halves - 1, 1))), dma((LAYERS, max(halves - 1, 1))),
            dma((LAYERS,)), dma((LAYERS,)), dma((LAYERS, ng - 1)), dma((LAYERS, ng - 1)),
            dma((extra + 1,)), dma((slots,)), dma((slots,)), dma((extra + 1,)),
            dma, dma, dma((ng - 1,)), dma((ng - 1,)), dma((ng - 1,)), dma((ng - 1,))],
        compiler_params=pltpu.CompilerParams(collective_id=0, has_side_effects=True,
                                             vmem_limit_bytes=62 << 20),
        name="precondition",
    )(owner, acts_first.reshape(-1, chans), grads_first.reshape(-1, chans),
      acts_second.reshape(-1, chans), grads_second.reshape(-1, chans), grad_w, basis_in,
      basis_out, taps)

    out, fin, fsp, fout = pl.pallas_call(
        functools.partial(finish_kernel, positions),
        out_shape=(struct((LAYERS, rows, 9 * chans), BF16), struct((LAYERS, chans, chans), F32),
                   struct((9, LAYERS, 9), F32), struct((LAYERS, chans, chans), F32)),
        in_specs=[vmem] * 3,
        out_specs=(vmem,) * 4,
        compiler_params=pltpu.CompilerParams(vmem_limit_bytes=62 << 20),
        name="finish",
    )(res, tot, tap)
    return out, fin, jnp.transpose(fsp, (1, 0, 2)), fout


def solution(mesh):
    placed = (
        P(("dp", "group"), None, None, None),
        P(("dp", "group"), None, None, None),
        P(("dp", "group"), None, None, None),
        P(("dp", "group"), None, None, None),
        P(None, "dp", None),
        P(),
        P("group", None, None),
        P("group", None, None),
        P("group", None, None),
    )
    return jax.shard_map(
        functools.partial(on_device, mesh.shape["dp"], mesh.shape["group"]),
        mesh=mesh,
        in_specs=placed,
        out_specs=(P(None, "dp", None), P(), P(), P()),
        check_vma=False,
    )
```

```python
import functools

import jax
import jax.numpy as jnp
from jax import lax
from jax.experimental import pallas as pl
from jax.experimental.pallas import tpu as pltpu
from jax.sharding import PartitionSpec as P

LAYERS = 2
STRIDES = (1, 2)
DAMPING = 0.1
LANES = 128
CUBE = 8
TAP_LANE = 96
MESH = pl.DeviceIdType.MESH
F32 = jnp.float32
BF16 = jnp.bfloat16
I32 = jnp.int32
CONTRACT_ROWS = (((0,), (0,)), ((), ()))
CONTRACT_COLS = (((1,), (1,)), ((), ()))
PAIRS = ((0, 0), (1, 1), (2, 2), (0, 1), (1, 2), (0, 2))


def dot(a, b):
    return jnp.dot(a, b, preferred_element_type=F32)


def dot_rows(a, b):
    return lax.dot_general(a, b, CONTRACT_ROWS, preferred_element_type=F32)


def dot_cols(a, b):
    return lax.dot_general(a, b, CONTRACT_COLS, preferred_element_type=F32)


def iota(shape, dim):
    return lax.broadcasted_iota(I32, shape, dim)


def each(start, stop, fn):
    def body(k, c):
        fn(k)
        return c
    lax.fori_loop(start, stop, body, 0)


def when(static, cond, fn):
    if static:
        fn()
    else:
        pl.when(cond)(fn)


def stacked(pieces):
    if pieces[0].shape[0] % 16 == 0:
        return jnp.concatenate(pieces, axis=0)
    return jnp.concatenate([piece.astype(F32) for piece in pieces], axis=0).astype(BF16)


def store_packed(ref, full):
    half = full.shape[0] // 2
    ref[0:half] = full[:half, :half].astype(BF16)
    ref[half:2 * half] = full[:half, half:].astype(BF16)
    ref[2 * half:] = full[half:, half:].astype(BF16)


def channel_gram(x, side, stride):
    chans = x.shape[1]
    col = iota((side, chans), 0)
    if stride == 1:
        counts = jnp.where((col == 0) | (col == side - 1), 2.0, 3.0)
        per_row = lambda i: 2.0 if i in (0, side - 1) else 3.0
    else:
        counts = jnp.where((col % 2 == 1) & (col < side - 1), 2.0, 1.0)
        per_row = lambda i: 2.0 if i % 2 == 1 and i < side - 1 else 1.0
    weights = {n: (n * counts).astype(BF16) for n in sorted({per_row(i) for i in range(side)})}
    weighted = jnp.concatenate([x[i * side:(i + 1) * side] * weights[per_row(i)]
                                for i in range(side)], axis=0)
    return dot_rows(x, weighted)


def tap_places(k):
    form, rest = k // 96, k % 96
    first = rest // 32
    rest = rest % 32
    pair, second = rest // 5, first + rest % 5 - 2
    a = jnp.where(pair < 3, pair, jnp.where(pair == 4, 1, 0))
    b = jnp.where(pair < 3, pair, jnp.where(pair == 3, 1, 2))
    one, two = 3 * a + first, 3 * b + second
    stands = (rest < 30) & (second >= 0) & (second < 3) & ((form == 0) | (pair >= 3))
    return jnp.where(form == 0, one, two), jnp.where(form == 0, two, one), stands


def tap_tables(ones_ref, twos_ref, flat_ref):
    row, col, stands = tap_places(iota(ones_ref.shape, 0))
    lane = iota(ones_ref.shape, 1)
    ones_ref[...] = jnp.where((row == lane) & stands, 1.0, 0.0).astype(BF16)
    twos_ref[...] = jnp.where((col == lane) & stands, 1.0, 0.0).astype(BF16)
    row, col, stands = tap_places(iota(flat_ref.shape, 0))
    flat_ref[...] = jnp.where((9 * row + col == iota(flat_ref.shape, 1)) & stands, 1.0, 0.0)


def tap_gram(x_ref, sums_ref, side, stride, out_side):
    per = 2 * LANES // side
    terms = []
    for q in range(side // per):
        at = 2 * q * LANES
        terms.append(dot_cols(x_ref[at:at + 2 * LANES + 2 * side, :], x_ref[at:at + 2 * LANES, :]))
    total = terms[0]
    for term in terms[1:]:
        total = total + term
    shape = (side, LANES)
    below, lane = iota(shape, 0), iota(shape, 1)
    block, col = lane // side, lane % side

    def row_pairs(dy):
        out = None
        for h in range(2):
            lanes = slice(h * LANES, (h + 1) * LANES)
            pick = None
            for r in range(per // 2):
                at = (h * per // 2 + r + dy) * side
                rows = total[at:at + side, lanes]
                pick = rows if pick is None else jnp.where(block == r, rows, pick)
            out = pick if out is None else out + pick
        return out

    same, one, two = row_pairs(0), row_pairs(1), row_pairs(2)
    last = jnp.where(block == per // 2 - 1, terms[-1][(per - 1) * side:per * side, LANES:], 0.0)
    if stride == 1:
        first = jnp.where(block == 0, terms[0][0:side, 0:LANES], 0.0)
        by_pair = (same - last, same, same - first, one, one, two)
    else:
        even = block % 2 == 0
        odd_same = jnp.where(even, 0.0, same)
        by_pair = (odd_same - last, jnp.where(even, same, 0.0), odd_same,
                   jnp.where(even, 0.0, one), jnp.where(even, one, 0.0), jnp.where(even, 0.0, two))
    for p in range(6):
        for d in range(5):
            k = 5 * p + d
            sums_ref[k:k + 1, :] = jnp.sum(jnp.where(below - col == d - 2, by_pair[p], 0.0),
                                           axis=0, keepdims=True)
    sums = sums_ref[...]
    col = iota(sums.shape, 1) % side
    values = []
    for b in range(3):
        base = col + 1 - b
        mask = (base >= 0) & (base <= stride * (out_side - 1)) & (base % stride == 0)
        values.append(jnp.sum(jnp.where(mask, sums, 0.0), axis=1, keepdims=True))
    return jnp.concatenate(values + values, axis=0)


def through_basis(parts, basis, rows, flip):
    product = (lambda a: dot_cols(a, basis)) if flip else (lambda a: dot(a, basis))
    if rows % 16 == 0:
        whole = product(jnp.concatenate(parts, axis=0))
        return [whole[u * rows:(u + 1) * rows] for u in range(9)]
    return [product(part) for part in parts]


def mixed_taps(parts, coef):
    out = []
    for t in range(9):
        total = parts[0] * coef(0, t)
        for u in range(1, 9):
            total = total + parts[u] * coef(u, t)
        out.append(total)
    return out


def quadratic(blocks, basis):
    half = blocks.shape[0] // 3
    upper = jnp.concatenate([blocks[0:half], blocks[half:2 * half] * 2], axis=1)
    lower = jnp.concatenate([jnp.zeros((half, half), BF16), blocks[2 * half:]], axis=1)
    turned = dot(jnp.concatenate([upper, lower], axis=0), basis)
    return jnp.sum(basis.astype(F32) * turned, axis=0, keepdims=True)


def remote(src, dst, send, recv, to):
    return pltpu.make_async_remote_copy(src_ref=src, dst_ref=dst, send_sem=send, recv_sem=recv,
                                        device_id=to, device_id_type=MESH)


def main_kernel(cfg, owner_hbm, x0_hbm, g0_hbm, x1_hbm, g1_hbm, w_hbm, qa_hbm, qg_hbm, qs_hbm,
                out_ref, tot_out, tap_out, *scratch):
    side, outs, chans, rows, dp, ng, slot_total, slots, positions = cfg
    (owner_ref, x0_ref, g0_ref, x1_ref, g1_ref, w_ref, qa_ref, qg_ref, qs_ref,
     ones_ref, twos_ref, flat_ref, pick_ref, table_ref, sums_ref, base_out, base_in, base_ref, part_ref, peer_ref,
     ra_ref, raa_ref, rb_ref, tot_ref, tap_ref, row_ref, rowin_ref, in_ref, ins_ref, out1_ref, outs_ref,
     rot_ref, rotin_ref, proj_ref, back_ref, backin_ref, fsp_ref, res_ref,
     loads, s_base, r_base, s_part, r_part, s_a, r_a, s_b, r_b, s_c, r_c, s_d, r_d,
     s_rot, r_rot, s_back, r_back, s_note, r_ins, r_outs, s_tap, r_tap, s_res, r_res, s_row, r_row,
     put_tot, put_tap, put_res) = scratch
    me, grp = lax.axis_index("dp"), lax.axis_index("group")
    cube = CUBE if dp % CUBE == 0 else dp
    halves = dp // cube
    member, part = lax.rem(me, cube), me // cube
    half = chans // 2
    blocks = 9 * chans // LANES
    per_chans = chans // LANES
    size = side * side
    whole = ng == LAYERS
    off_qs, off_qg, off_x, off_rest = chans, chans + 16, 2 * chans + 16, 3 * chans + 16
    handles = lambda fn: when(whole, grp < LAYERS, fn)

    pairs = ((qs_hbm, qs_ref), (qa_hbm, qa_ref), (qg_hbm, qg_ref), (x0_hbm, x0_ref.at[pl.ds(0, size)]),
             (g0_hbm, g0_ref), (w_hbm, w_ref), (x1_hbm, x1_ref.at[pl.ds(0, size)]), (g1_hbm, g1_ref), (owner_hbm, owner_ref))
    order = (3, 4, 8, 0, 1, 2, 6, 7, 5)
    copies = [pltpu.make_async_copy(src, dst, loads.at[i]) for i, (src, dst) in enumerate(pairs)]
    for i in order:
        copies[i].start()
    arrive = lambda i: copies[i].wait()

    barrier = pltpu.get_barrier_semaphore()
    with jax.named_scope("greet"):
        for q in range(ng):
            to_grp = lax.rem(grp + q, ng)
            each(0 if q else 1, dp, lambda r, to_grp=to_grp: pl.semaphore_signal(
                barrier, inc=1, device_id={"dp": lax.rem(me + r, dp), "group": to_grp},
                device_id_type=MESH))

    def sibling(q):
        return lax.rem(grp + q, ng)

    def from_group(q):
        return lax.rem(grp + ng - q, ng)

    def copy_base(q, i):
        at, n = ((0, off_qg), (off_qg, off_rest + 16 - off_qg))[i]
        return remote(base_out.at[sibling(q), pl.ds(at, n)], base_in.at[q - 1, pl.ds(at, n)],
                      s_base.at[q - 1, i], r_base.at[q - 1, i], {"group": sibling(q)})

    def copy_part(l, q):
        return remote(part_ref.at[l, sibling(q)], peer_ref.at[l, q - 1], s_part.at[l, q - 1],
                      r_part.at[l, q - 1], {"group": sibling(q)})

    def copy_a(l, r):
        to = lax.rem(member + r, cube)
        return remote(ra_ref.at[l, to], raa_ref.at[l, r - 1], s_a.at[l], r_a.at[l],
                      {"dp": part * cube + to})

    def all_a(l):
        return remote(raa_ref.at[l], raa_ref.at[l], s_a.at[l], r_a.at[l], {"dp": me})

    def copy_b(l, r):
        to = lax.rem(part + r, halves)
        return remote(rb_ref.at[l, part], rb_ref.at[l, part], s_b.at[l, r - 1], r_b.at[l, r - 1],
                      {"dp": to * cube + member})

    def copy_c(l, r):
        to = lax.rem(member + r, cube)
        block = tot_ref.at[grp, l, member]
        return remote(block, block, s_c.at[l], r_c.at[l], {"dp": part * cube + to})

    def all_c(l):
        blocks = tot_ref.at[grp, l, pl.ds(0, cube - 1)]
        return remote(blocks, blocks, s_c.at[l], r_c.at[l], {"dp": me})

    def copy_d(l, q, k=grp):
        return remote(tot_ref.at[k, l], tot_out.at[k, l], s_d.at[l, q - 1], r_d.at[l, q - 1],
                      {"group": sibling(q)})

    def put_d(l):
        return pltpu.make_async_copy(tot_ref.at[grp, l], tot_out.at[grp, l], put_tot.at[l])

    def copy_rot(r):
        to = lax.rem(me + r, dp)
        return remote(rot_ref.at[to], rotin_ref.at[0, me], s_rot.at[0], r_rot.at[0], {"dp": to})

    def copy_rot_late(k):
        to = late_at(k)
        return remote(rot_ref.at[k], rotin_ref.at[k // dp, me], s_rot.at[1 + k - dp],
                      r_rot.at[k // dp], {"dp": to})

    def all_rot(s):
        blocks = rotin_ref.at[s, pl.ds(0, dp - 1)]
        return remote(blocks, blocks, s_rot.at[0], r_rot.at[s], {"dp": me})

    def copy_back(s, r):
        to = lax.rem(me + r, dp)
        k = block_at(s)
        recv = r_back.at[0] if s == 0 else r_back.at[k - dp + 1]
        return remote(back_ref.at[s, to], backin_ref.at[k], s_back.at[s], recv, {"dp": to})

    def all_back(s):
        some = backin_ref.at[pl.ds(0, dp - 1)]
        return remote(some, some, s_back.at[s], r_back.at[0], {"dp": me})

    def back_from(k):
        return remote(backin_ref.at[k], backin_ref.at[k], s_back.at[0], r_back.at[k - dp + 1],
                      {"dp": me})

    def copy_row(l):
        k = jnp.maximum(grp, LAYERS) - LAYERS
        return remote(row_ref.at[l], rowin_ref.at[l, k], s_row.at[l], r_row.at[l, k], {"group": 0})

    def row_from(l, k):
        return remote(row_ref.at[l], rowin_ref.at[l, k - LAYERS], s_row.at[l],
                      r_row.at[l, k - LAYERS], {"group": k})

    def copy_in(l, r):
        to = lax.rem(me + r, dp)
        return remote(in_ref.at[l, lax.rem(to, per_chans)], ins_ref.at[me], s_note, r_ins,
                      {"dp": to, "group": l})

    def copy_out(l, r):
        return remote(out1_ref.at[l], outs_ref.at[me], s_note, r_outs,
                      {"dp": lax.rem(me + r, dp), "group": l})

    def some_notes(ref, recv, n):
        return remote(ref.at[pl.ds(0, n)], ref.at[pl.ds(0, n)], s_note, recv, {"dp": me})

    def copy_tap(q, k=grp):
        return remote(tap_ref, tap_out.at[k], s_tap.at[q - 1], r_tap.at[q - 1],
                      {"group": sibling(q)})

    def put_t():
        return pltpu.make_async_copy(tap_ref, tap_out.at[grp], put_tap)

    def copy_res(q, k=grp):
        return remote(res_ref, out_ref.at[k], s_res.at[q - 1], r_res.at[q - 1],
                      {"group": sibling(q)})

    def put_r():
        return pltpu.make_async_copy(res_ref, out_ref.at[grp], put_res)

    late = range(dp, blocks)
    spread = dp // 4 + 2 * grp

    def block_at(s):
        if s == 0:
            return me
        return s * dp + lax.rem((me + 4 * dp - spread) * pow(5, -1, dp), dp)

    def late_at(k):
        return lax.rem(5 * (k % dp) + spread, dp)

    def if_block(s, fn):
        when((s + 1) * dp <= blocks, block_at(s) < blocks, fn)

    def if_to(q, fn):
        when(whole, sibling(q) < LAYERS, fn)

    def if_from(q, fn):
        when(whole, from_group(q) < LAYERS, fn)

    scope = jax.named_scope
    with scope("tables"):
        tap_tables(ones_ref, twos_ref, flat_ref)
        shape = pick_ref.shape
        pick_ref[...] = jnp.where(iota(shape, 0) % 2 == iota(shape, 1) // LANES, 1.0, 0.0)
        for ref in (x0_ref, x1_ref):
            ref[size:size + 2 * side, :] = jnp.zeros((2 * side, chans), BF16)
        sums_ref[...] = jnp.zeros(sums_ref.shape, F32)
        for p in range(ng):
            for at in (off_qs, off_rest):
                base_out[p, at:at + 16] = jnp.zeros((16, chans), BF16)
        for p in range(LAYERS, ng):
            base_out[p, 0:off_qs] = jnp.zeros((off_qs, chans), BF16)
            base_out[p, off_qg:off_rest] = jnp.zeros((off_rest - off_qg, chans), BF16)

    def own_bases():
        with scope("held"):
            arrive(0)
            arrive(8)
            slot = [owner_ref[l] % slot_total for l in range(LAYERS)]
            mine = [owner_ref[l] // slot_total == grp for l in range(LAYERS)]
            taps = qs_ref[...].astype(F32)
            level = iota(taps.shape, 1)

            def held_taps(l):
                value = jnp.sum(jnp.where((level == slot[l]) & mine[l], taps, 0.0), axis=1)
                return jnp.pad(value, ((0, 7), (TAP_LANE, LANES - TAP_LANE - 9))).astype(BF16)

            held = [held_taps(l) for l in range(LAYERS)]
        with scope("mask"):
            arrive(1)
            arrive(2)
            keep = lambda l, ref: jnp.where(mine[l], ref[slot[l]], jnp.zeros(ref.shape[1:], BF16))
            for p in range(LAYERS):
                base_out[p, 0:chans] = keep(p, qa_ref)
                base_out[p, off_qs:off_qs + 16, 0:LANES] = held[p]
                base_out[p, off_qg:off_qg + chans] = keep(p, qg_ref)
                base_out[p, off_x:off_x + chans] = keep(1 - p, qg_ref if p else qa_ref)
                base_out[p, off_rest:off_rest + 16, 0:LANES] = held[1 - p]
            for p in range(LAYERS, ng):
                base_out[p, off_qs:off_qs + 16, 0:LANES] = held[0]
                base_out[p, off_rest:off_rest + 16, 0:LANES] = held[1]

    def take_base(i):
        at, n = ((0, off_qg), (off_qg, off_rest + 16 - off_qg))[i]
        total = base_out[grp, at:at + n]
        for q in range(1, ng):
            copy_base(q, i).wait_recv()
            total = total + base_in[q - 1, at:at + n]
        base_ref[at:at + n] = total

    def tap_table(l):
        near = grp == l if l else (grp == l) | (grp >= LAYERS)
        at = jnp.where(near, off_qs, off_rest)
        qs = base_ref[pl.ds(pl.multiple_of(at, 16), 16), 0:LANES]
        both = dot(ones_ref[...], qs) * dot(twos_ref[...], qs)
        table_ref[l] = flat_ref[...] + both

    def make_row(l):
        row_ref[l] = jnp.sum(fsp_ref[l] * table_ref[l], axis=0, keepdims=True)
        if ng > LAYERS:
            pl.when(grp >= LAYERS)(lambda: copy_row(l).start())

    def local_factors(l, x_ref, g_ref, x_load):
        arrive(x_load)
        arrive(x_load + 1)
        full = channel_gram(x_ref[0:size, :], side, STRIDES[l])
        out = dot_rows(g_ref[...], g_ref[...])
        values = tap_gram(x_ref, sums_ref, side, STRIDES[l], outs[l])
        store_packed(part_ref.at[l, 0], full)
        store_packed(part_ref.at[l, 1], out)
        fsp_ref[l] = jnp.broadcast_to(values, fsp_ref.shape[1:])

    def send_part(l):
        for q in range(1, ng):
            if_to(q, lambda q=q: copy_part(l, q).start())

    def local_taps(l, x_ref):
        values = tap_gram(x_ref, sums_ref, side, STRIDES[l], outs[l])
        fsp_ref[l] = jnp.broadcast_to(values, fsp_ref.shape[1:])

    def chip_sum(l):
        def run():
            total = part_ref[l, grp].astype(F32)
            for q in range(1, ng):
                copy_part(l, q).wait_recv()
                total = total + peer_ref[l, q - 1].astype(F32)
            ra_ref[l] = total.astype(BF16).reshape(cube, 3 * half // cube, LANES)
        handles(run)

    def send_a(l):
        handles(lambda: each(1, cube, lambda r: copy_a(l, r).start()))

    def make_note(l):
        at = jnp.where(grp == l, jnp.where(grp == 0, 0, off_qg), off_x)
        basis = base_ref[pl.ds(pl.multiple_of(at, 16), chans), :]
        blk = ra_ref[l].reshape(3 * half, LANES)
        scale = 1.0 / (jnp.where(grp == 0, 9.0, 1.0) * positions[l])
        lam = quadratic(blk, basis) * scale
        row = row_ref[l]
        for p in range(per_chans):
            in_ref[l, p] = jnp.concatenate([row, lam[:, p * LANES:(p + 1) * LANES]], axis=1)
        out1_ref[l] = jnp.concatenate([row, lam], axis=1)

    def add_rows():
        for l in range(LAYERS):
            total = row_ref[l]
            for k in range(LAYERS, ng):
                row_from(l, k).wait_recv()
                total = total + rowin_ref[l, k - LAYERS]
            row_ref[l] = total

    def send_notes():
        for k, copy in ((0, copy_in), (1, copy_out)):
            def send(k=k, copy=copy):
                def both(r):
                    for l in range(LAYERS):
                        copy(l, r).start()
                copy(1 - k, 0).start()
                each(1, dp, both)
                if k:
                    outs_ref[me] = out1_ref[k]
                else:
                    ins_ref[me] = in_ref[k, lax.rem(me, per_chans)]
            pl.when(grp == k)(send)

    def notes_here():
        for k in range(LAYERS):
            def run(k=k):
                some_notes(ins_ref, r_ins, dp - 1 if k == 0 else dp).wait_recv()
                some_notes(outs_ref, r_outs, dp - 1 if k else dp).wait_recv()
            pl.when(grp == k)(run)

    def reduce_b(l):
        def run():
            all_a(l).wait_recv()
            total = ra_ref[l, member].astype(F32)
            for r in range(1, cube):
                total = total + raa_ref[l, r - 1].astype(F32)
            rb_ref[l, part] = total.astype(BF16)
            for r in range(1, halves):
                copy_b(l, r).start()
        handles(run)

    def gather_c(l):
        def run():
            for r in range(1, halves):
                copy_b(l, r).wait_recv()
            total = rb_ref[l, 0].astype(F32)
            for h in range(1, halves):
                total = total + rb_ref[l, h].astype(F32)
            tot_ref[grp, l, member] = total.astype(BF16)
            each(1, cube, lambda r: copy_c(l, r).start())
        handles(run)

    def forward_d(l):
        def run():
            all_c(l).wait_recv()
            for q in range(1, ng):
                copy_d(l, q).start()
            put_d(l).start()
        handles(run)

    def rotate():
        qs = base_ref[off_qs:off_qs + 16, 0:LANES].astype(F32)
        parts = [w_ref[grp, :, u * chans:(u + 1) * chans] for u in range(9)]
        inner = through_basis(parts, base_ref[0:chans, :], rows, False)
        turned = mixed_taps(inner, lambda u, t: qs[u:u + 1, TAP_LANE + t:TAP_LANE + t + 1])
        per = chans // LANES
        for k in range(blocks):
            lane = (k % per) * LANES
            rot_ref[k] = turned[k // per][:, lane:lane + LANES].astype(BF16)
        if dp <= blocks:
            each(1, dp, lambda r: copy_rot(r).start())
        else:
            each(1, dp, lambda r: pl.when(lax.rem(me + r, dp) < blocks)(lambda: copy_rot(r).start()))
        for k in late:
            pl.when(me != late_at(k))(lambda k=k: copy_rot_late(k).start())
        for s in range(slots):
            def own(s=s):
                rotin_ref[s, me] = rot_ref[block_at(s)]
            if_block(s, own)

    def project():
        for s in range(slots):
            def run(s=s):
                all_rot(s).wait_recv()
                rot = stacked([rotin_ref[s, e] for e in range(dp)])
                proj_ref[s] = dot_rows(base_ref[off_qg:off_qg + chans, :], rot)
            if_block(s, run)

    def precondition():
        with jax.named_scope("notes"):
            notes_here()
        sums = []
        for ref in (ins_ref, outs_ref):
            total = ref[0]
            for e in range(1, dp):
                total = total + ref[e]
            sums.append(total)
        rows_sum = sums[0][:, 0:LANES] + sums[1][:, 0:LANES]
        lam_in = sums[0][:, LANES:]
        spread_out = jnp.concatenate([sums[1][:, LANES:2 * LANES], sums[1][:, 2 * LANES:]], axis=0)
        inv = jnp.where(grp == 0, 1.0 / (chans * positions[0]), 1.0 / (chans * positions[1]))
        every = rows_sum * inv
        tap_ref[...] = every
        for q in range(1, ng):
            copy_tap(q).start()
        put_t().start()
        high = spread_out.astype(BF16).astype(F32)
        col = dot_rows(jnp.concatenate([high, spread_out - high], axis=0), pick_ref[...])
        lam_out = jnp.concatenate([col[:, 0:LANES], col[:, LANES:]], axis=0)
        lane = iota((1, LANES), 1)
        per = chans // LANES
        for s in range(slots):
            def run(s=s):
                k = block_at(s)
                tap = jnp.sum(jnp.where(lane == TAP_LANE + k // per, every, 0.0), axis=1, keepdims=True)
                coords = (proj_ref[s] / (lam_out * (lam_in * tap) + DAMPING)).astype(BF16)
                back = dot(base_ref[off_qg:off_qg + chans, :], coords)
                for e in range(dp):
                    back_ref[s, e] = back[e * rows:(e + 1) * rows].astype(BF16)
                each(1, dp, lambda r: copy_back(s, r).start())
                backin_ref[block_at(s)] = back_ref[s, me]
            if_block(s, run)

    def result():
        with jax.named_scope("back"):
            if dp <= blocks:
                all_back(0).wait_recv()
            else:
                each(0, blocks, lambda k: pl.when(me != k)(
                    lambda: remote(backin_ref.at[k], backin_ref.at[k], s_back.at[0], r_back.at[0],
                                   {"dp": me}).wait_recv()))
            for k in late:
                pl.when(me != late_at(k))(lambda k=k: back_from(k).wait_recv())
        qs = base_ref[off_qs:off_qs + 16, 0:LANES].astype(F32)
        per = chans // LANES
        parts = []
        for t in range(9):
            pieces = [backin_ref[k] for k in range(t * per, (t + 1) * per)]
            parts.append(jnp.concatenate(pieces, axis=1))
        turned = mixed_taps(through_basis(parts, base_ref[0:chans, :], rows, True),
                            lambda t, u: qs[u:u + 1, TAP_LANE + t:TAP_LANE + t + 1])
        for u in range(9):
            res_ref[:, u * chans:(u + 1) * chans] = turned[u].astype(BF16)
        for q in range(1, ng):
            copy_res(q).start()
        put_r().start()

    with scope("first"):
        local_factors(0, x0_ref, g0_ref, 3)
    own_bases()
    with scope("barrier"):
        pl.semaphore_wait(barrier, dp * ng - 1)
    send_part(0)
    for q in range(1, ng):
        for i in range(2):
            copy_base(q, i).start()
    with scope("second"):
        local_factors(1, x1_ref, g1_ref, 6)
        send_part(1)
    with scope("first_sum"):
        chip_sum(0)
        send_a(0)
    with scope("base"):
        take_base(0)
        take_base(1)
    arrive(5)
    with scope("rotate"):
        handles(rotate)
    with scope("second_sum"):
        chip_sum(1)
        send_a(1)
    with scope("tables2"):
        for l in range(LAYERS):
            tap_table(l)
            make_row(l)

    def notes():
        if ng > LAYERS:
            pl.when(grp == 0)(add_rows)
        for l in range(LAYERS):
            make_note(l)
        send_notes()
    with scope("make_notes"):
        handles(notes)
    with scope("first_b"):
        reduce_b(0)
    with scope("second_b"):
        reduce_b(1)
    with scope("first_c"):
        gather_c(0)
    with scope("project"):
        handles(project)
    with scope("precondition"):
        handles(precondition)
    with scope("second_c"):
        gather_c(1)
    with scope("forward0"):
        forward_d(0)
    with scope("result"):
        handles(result)
    with scope("forward"):
        forward_d(1)

    with scope("rest"):
        for q in range(1, ng):
            def arrived(q=q):
                k = from_group(q)
                copy_tap(q, k).wait_recv()
                copy_res(q, k).wait_recv()
                for l in range(LAYERS):
                    copy_d(l, q, k).wait_recv()
            if_from(q, arrived)

    with scope("sent"):
        for q in range(1, ng):
            def sent_to(q=q):
                for l in range(LAYERS):
                    copy_part(l, q).wait_send()
            if_to(q, sent_to)
            for i in range(2):
                copy_base(q, i).wait_send()
        if ng > LAYERS:
            pl.when(grp >= LAYERS)(lambda: [copy_row(l).wait_send() for l in range(LAYERS)] and None)

        def sent():
            pl.when(grp == 0)(lambda: [some_notes(ins_ref, r_ins, n).wait_send() for n in (dp, dp - 1)] and None)
            pl.when(grp == 1)(lambda: [some_notes(outs_ref, r_outs, n).wait_send() for n in (dp, dp - 1)] and None)
            put_t().wait()
            put_r().wait()
            for l in range(LAYERS):
                put_d(l).wait()
                all_a(l).wait_send()
                all_c(l).wait_send()
                for r in range(1, halves):
                    copy_b(l, r).wait_send()
                for q in range(1, ng):
                    copy_d(l, q).wait_send()
            if dp <= blocks:
                all_rot(0).wait_send()
            else:
                each(1, dp, lambda r: pl.when(lax.rem(me + r, dp) < blocks)(
                    lambda: copy_rot(r).wait_send()))
            for k in late:
                pl.when(me != late_at(k))(lambda k=k: copy_rot_late(k).wait_send())
            for s in range(slots):
                if_block(s, lambda s=s: all_back(s).wait_send())
            for q in range(1, ng):
                copy_tap(q).wait_send()
                copy_res(q).wait_send()
        handles(sent)


def finish_kernel(positions, res_ref, tot_ref, tap_ref, out_ref, fin_ref, fsp_ref, fout_ref):
    for l in range(LAYERS):
        for kind, ref, scale in ((0, fin_ref, 9.0), (1, fout_ref, 1.0)):
            blk = tot_ref[kind, l].astype(F32) / (scale * positions[l])
            half = blk.shape[0] // 3
            mid = blk[half:2 * half]
            ref[l, 0:half, 0:half] = blk[0:half]
            ref[l, 0:half, half:] = mid
            ref[l, half:, 0:half] = jnp.transpose(mid)
            ref[l, half:, half:] = blk[2 * half:]
        for u in range(9):
            fsp_ref[u, l:l + 1, :] = tap_ref[l, 0:1, 9 * u:9 * u + 9]
    out_ref[...] = res_ref[...]


def on_device(dp, ng, acts_first, grads_first, acts_second, grads_second, grad_w, owner,
              basis_in, basis_spatial, basis_out):
    images, side = acts_first.shape[0], acts_first.shape[1]
    chans = basis_in.shape[1]
    rows = grad_w.shape[1]
    slot_total = basis_in.shape[0]
    outs = (grads_first.shape[1], grads_second.shape[1])
    positions = tuple(images * o * o * dp * ng for o in outs)
    slots = -(-9 * chans // LANES // dp)
    cube = CUBE if dp % CUBE == 0 else dp
    halves = dp // cube
    half = chans // 2
    share = 3 * half // cube
    base_rows = 3 * chans + 32
    extra = max(9 * chans // LANES - dp, 0)
    vmem = pl.BlockSpec(memory_space=pltpu.VMEM)
    hbm = pl.BlockSpec(memory_space=pltpu.HBM)
    struct = jax.ShapeDtypeStruct
    dma = pltpu.SemaphoreType.DMA
    bf = lambda *shape: pltpu.VMEM(shape, BF16)
    ff = lambda *shape: pltpu.VMEM(shape, F32)
    taps = jnp.transpose(basis_spatial, (1, 0, 2))

    cfg = (side, outs, chans, rows, dp, ng, slot_total, slots, positions)
    res, tot, tap = pl.pallas_call(
        functools.partial(main_kernel, cfg),
        out_shape=(struct((LAYERS, rows, 9 * chans), BF16),
                   struct((2, LAYERS, cube, share, LANES), BF16),
                   struct((LAYERS, 1, LANES), F32)),
        in_specs=[hbm] * 9,
        out_specs=(hbm,) * 3,
        scratch_shapes=[
            pltpu.SMEM((LAYERS,), I32), bf((side + 2) * side, chans), bf(outs[0] * outs[0], chans),
            bf((side + 2) * side, chans), bf(outs[1] * outs[1], chans),
            bf(*grad_w.shape), bf(*basis_in.shape), bf(*basis_out.shape), bf(*taps.shape),
            bf(192, 16), bf(192, 16), ff(192, LANES), ff(4, 2 * LANES), ff(LAYERS, 192, LANES), ff(32, LANES),
            bf(ng, base_rows, chans), bf(ng - 1, base_rows, chans),
            bf(base_rows, chans),
            bf(LAYERS, 2, 3 * half, LANES), bf(LAYERS, ng - 1, 3 * half, LANES),
            bf(LAYERS, cube, share, LANES), bf(LAYERS, max(cube - 1, 1), share, LANES),
            bf(LAYERS, halves, share, LANES), bf(2, LAYERS, cube, share, LANES),
            ff(1, LANES), ff(LAYERS, 1, LANES), ff(LAYERS, max(ng - LAYERS, 1), 1, LANES),
            ff(LAYERS, chans // LANES, 1, 2 * LANES), ff(dp, 1, 2 * LANES), ff(LAYERS, 1, LANES + chans),
            ff(dp, 1, LANES + chans),
            bf(max(9 * chans // LANES, slots * dp), rows, LANES), bf(slots, dp, rows, LANES), ff(slots, chans, LANES),
            bf(slots, dp, rows, LANES), bf(slots * dp, rows, LANES), ff(LAYERS, 192, LANES),
            bf(rows, 9 * chans),
            dma((9,)), dma((ng - 1, 2)), dma((ng - 1, 2)), dma((LAYERS, ng - 1)), dma((LAYERS, ng - 1)),
            dma((LAYERS,)), dma((LAYERS,)), dma((LAYERS, max(halves - 1, 1))), dma((LAYERS, max(halves - 1, 1))),
            dma((LAYERS,)), dma((LAYERS,)), dma((LAYERS, ng - 1)), dma((LAYERS, ng - 1)),
            dma((extra + 1,)), dma((slots,)), dma((slots,)), dma((extra + 1,)),
            dma, dma, dma, dma((ng - 1,)), dma((ng - 1,)), dma((ng - 1,)), dma((ng - 1,)),
            dma((LAYERS,)), dma((LAYERS, max(ng - LAYERS, 1))), dma((LAYERS,)), dma, dma],
        compiler_params=pltpu.CompilerParams(collective_id=0, has_side_effects=True,
                                             vmem_limit_bytes=62 << 20),
        name="precondition",
    )(owner, acts_first.reshape(-1, chans), grads_first.reshape(-1, chans),
      acts_second.reshape(-1, chans), grads_second.reshape(-1, chans), grad_w, basis_in,
      basis_out, taps)

    out, fin, fsp, fout = pl.pallas_call(
        functools.partial(finish_kernel, positions),
        out_shape=(struct((LAYERS, rows, 9 * chans), BF16), struct((LAYERS, chans, chans), F32),
                   struct((9, LAYERS, 9), F32), struct((LAYERS, chans, chans), F32)),
        in_specs=[vmem] * 3,
        out_specs=(vmem,) * 4,
        compiler_params=pltpu.CompilerParams(vmem_limit_bytes=62 << 20),
        name="finish",
    )(res, tot.reshape(2, LAYERS, 3 * half, LANES), tap)
    return out, fin, jnp.transpose(fsp, (1, 0, 2)), fout


def solution(mesh):
    placed = (
        P(("dp", "group"), None, None, None),
        P(("dp", "group"), None, None, None),
        P(("dp", "group"), None, None, None),
        P(("dp", "group"), None, None, None),
        P(None, "dp", None),
        P(),
        P("group", None, None),
        P("group", None, None),
        P("group", None, None),
    )
    return jax.shard_map(
        functools.partial(on_device, mesh.shape["dp"], mesh.shape["group"]),
        mesh=mesh,
        in_specs=placed,
        out_specs=(P(None, "dp", None), P(), P(), P()),
        check_vma=False,
    )
```

```python
import functools

import jax
import jax.numpy as jnp
from jax import lax
from jax.experimental import pallas as pl
from jax.experimental.pallas import tpu as pltpu
from jax.sharding import PartitionSpec as P

LAYERS = 2
STRIDES = (1, 2)
DAMPING = 0.1
LANES = 128
CUBE = 8
TAP_LANE = 96
MESH = pl.DeviceIdType.MESH
F32 = jnp.float32
BF16 = jnp.bfloat16
I32 = jnp.int32
CONTRACT_ROWS = (((0,), (0,)), ((), ()))
CONTRACT_COLS = (((1,), (1,)), ((), ()))
PAIRS = ((0, 0), (1, 1), (2, 2), (0, 1), (1, 2), (0, 2))


def dot(a, b):
    return jnp.dot(a, b, preferred_element_type=F32)


def dot_rows(a, b):
    return lax.dot_general(a, b, CONTRACT_ROWS, preferred_element_type=F32)


def dot_cols(a, b):
    return lax.dot_general(a, b, CONTRACT_COLS, preferred_element_type=F32)


def iota(shape, dim):
    return lax.broadcasted_iota(I32, shape, dim)


def each(start, stop, fn):
    if stop - start <= 16:
        for k in range(start, stop):
            fn(k)
        return

    def body(k, c):
        fn(k)
        return c
    lax.fori_loop(start, stop, body, 0)


def partner(index, step, count):
    if count & (count - 1):
        return lax.rem(index + step, count)
    step = count - step
    bit = 1
    out = index
    while bit < count:
        turn = bit - index // bit % 2 * (2 * bit)
        if not isinstance(step, int):
            out = out + lax.rem(lax.div(step, jnp.int32(bit)), jnp.int32(2)) * turn
        elif step & bit:
            out = out + turn
        bit *= 2
    return out


def when(static, cond, fn):
    if static:
        fn()
    else:
        pl.when(cond)(fn)


def stacked(pieces):
    if pieces[0].shape[0] % 16 == 0:
        return jnp.concatenate(pieces, axis=0)
    return jnp.concatenate([piece.astype(F32) for piece in pieces], axis=0).astype(BF16)


def store_packed(ref, full):
    half = full.shape[0] // 2
    ref[0:half] = full[:half, :half].astype(BF16)
    ref[half:2 * half] = full[:half, half:].astype(BF16)
    ref[2 * half:] = full[half:, half:].astype(BF16)


def channel_gram(x, side, stride):
    chans = x.shape[1]
    col = iota((side, chans), 0)
    if stride == 1:
        counts = jnp.where((col == 0) | (col == side - 1), 2.0, 3.0)
        per_row = lambda i: 2.0 if i in (0, side - 1) else 3.0
    else:
        counts = jnp.where((col % 2 == 1) & (col < side - 1), 2.0, 1.0)
        per_row = lambda i: 2.0 if i % 2 == 1 and i < side - 1 else 1.0
    weights = {n: (n * counts).astype(BF16) for n in sorted({per_row(i) for i in range(side)})}
    weighted = jnp.concatenate([x[i * side:(i + 1) * side] * weights[per_row(i)]
                                for i in range(side)], axis=0)
    return dot_rows(x, weighted)


def tap_places(k):
    form, rest = k // 96, k % 96
    first = rest // 32
    rest = rest % 32
    pair, second = rest // 5, first + rest % 5 - 2
    a = jnp.where(pair < 3, pair, jnp.where(pair == 4, 1, 0))
    b = jnp.where(pair < 3, pair, jnp.where(pair == 3, 1, 2))
    one, two = 3 * a + first, 3 * b + second
    stands = (rest < 30) & (second >= 0) & (second < 3) & ((form == 0) | (pair >= 3))
    return jnp.where(form == 0, one, two), jnp.where(form == 0, two, one), stands


def tap_tables(ones_ref, twos_ref, flat_ref):
    row, col, stands = tap_places(iota(ones_ref.shape, 0))
    lane = iota(ones_ref.shape, 1)
    ones_ref[...] = jnp.where((row == lane) & stands, 1.0, 0.0).astype(BF16)
    twos_ref[...] = jnp.where((col == lane) & stands, 1.0, 0.0).astype(BF16)
    row, col, stands = tap_places(iota(flat_ref.shape, 0))
    flat_ref[...] = jnp.where((9 * row + col == iota(flat_ref.shape, 1)) & stands, 1.0, 0.0)


def tap_gram(x_ref, sums_ref, side, stride, out_side):
    per = 2 * LANES // side
    terms = []
    for q in range(side // per):
        at = 2 * q * LANES
        terms.append(dot_cols(x_ref[at:at + 2 * LANES + 2 * side, :], x_ref[at:at + 2 * LANES, :]))
    total = terms[0]
    for term in terms[1:]:
        total = total + term
    shape = (side, LANES)
    below, lane = iota(shape, 0), iota(shape, 1)
    block, col = lane // side, lane % side

    def row_pairs(dy):
        out = None
        for h in range(2):
            lanes = slice(h * LANES, (h + 1) * LANES)
            pick = None
            for r in range(per // 2):
                at = (h * per // 2 + r + dy) * side
                rows = total[at:at + side, lanes]
                pick = rows if pick is None else jnp.where(block == r, rows, pick)
            out = pick if out is None else out + pick
        return out

    same, one, two = row_pairs(0), row_pairs(1), row_pairs(2)
    last = jnp.where(block == per // 2 - 1, terms[-1][(per - 1) * side:per * side, LANES:], 0.0)
    if stride == 1:
        first = jnp.where(block == 0, terms[0][0:side, 0:LANES], 0.0)
        by_pair = (same - last, same, same - first, one, one, two)
    else:
        even = block % 2 == 0
        odd_same = jnp.where(even, 0.0, same)
        by_pair = (odd_same - last, jnp.where(even, same, 0.0), odd_same,
                   jnp.where(even, 0.0, one), jnp.where(even, one, 0.0), jnp.where(even, 0.0, two))
    for p in range(6):
        for d in range(5):
            k = 5 * p + d
            sums_ref[k:k + 1, :] = jnp.sum(jnp.where(below - col == d - 2, by_pair[p], 0.0),
                                           axis=0, keepdims=True)
    sums = sums_ref[...]
    col = iota(sums.shape, 1) % side
    values = []
    for b in range(3):
        base = col + 1 - b
        mask = (base >= 0) & (base <= stride * (out_side - 1)) & (base % stride == 0)
        values.append(jnp.sum(jnp.where(mask, sums, 0.0), axis=1, keepdims=True))
    return jnp.concatenate(values + values, axis=0)


def through_basis(parts, basis, rows, flip):
    product = (lambda a: dot_cols(a, basis)) if flip else (lambda a: dot(a, basis))
    if rows % 16 == 0:
        whole = product(jnp.concatenate(parts, axis=0))
        return [whole[u * rows:(u + 1) * rows] for u in range(9)]
    return [product(part) for part in parts]


def mixed_taps(parts, coef):
    out = []
    for t in range(9):
        total = parts[0] * coef(0, t)
        for u in range(1, 9):
            total = total + parts[u] * coef(u, t)
        out.append(total)
    return out


def quadratic(blocks, basis):
    half = blocks.shape[0] // 3
    upper = jnp.concatenate([blocks[0:half], blocks[half:2 * half] * 2], axis=1)
    lower = jnp.concatenate([jnp.zeros((half, half), BF16), blocks[2 * half:]], axis=1)
    turned = dot(jnp.concatenate([upper, lower], axis=0), basis)
    return jnp.sum(basis.astype(F32) * turned, axis=0, keepdims=True)


def remote(src, dst, send, recv, to):
    return pltpu.make_async_remote_copy(src_ref=src, dst_ref=dst, send_sem=send, recv_sem=recv,
                                        device_id=to, device_id_type=MESH)


def main_kernel(cfg, owner_hbm, x0_hbm, g0_hbm, x1_hbm, g1_hbm, w_hbm, qa_hbm, qg_hbm, qs_hbm,
                out_ref, tot_out, tap_out, *scratch):
    side, outs, chans, rows, dp, ng, slot_total, slots, positions = cfg
    (owner_ref, x0_ref, g0_ref, x1_ref, g1_ref, w_ref, qa_ref, qg_ref, qs_ref,
     ones_ref, twos_ref, flat_ref, pick_ref, table_ref, sums_ref, base_out, base_in, base_ref, part_ref, peer_ref,
     ra_ref, raa_ref, rb_ref, tot_ref, tap_ref, row_ref, rowin_ref, in_ref, ins_ref, out1_ref, outs_ref,
     rot_ref, rotin_ref, proj_ref, back_ref, backin_ref, fsp_ref, res_ref,
     loads, s_base, r_base, s_part, r_part, s_a, r_a, s_b, r_b, s_c, r_c, s_d, r_d,
     s_rot, r_rot, s_back, r_back, s_note, r_ins, r_outs, s_tap, r_tap, s_res, r_res, s_row, r_row,
     put_tot, put_tap, put_res) = scratch
    me, grp = lax.axis_index("dp"), lax.axis_index("group")
    cube = CUBE if dp % CUBE == 0 else dp
    halves = dp // cube
    member, part = lax.rem(me, cube), me // cube
    half = chans // 2
    blocks = 9 * chans // LANES
    per_chans = chans // LANES
    size = side * side
    whole = ng == LAYERS
    off_qs, off_qg, off_x, off_rest = chans, chans + 16, 2 * chans + 16, 3 * chans + 16
    handles = lambda fn: when(whole, grp < LAYERS, fn)

    pairs = ((qs_hbm, qs_ref), (qa_hbm, qa_ref), (qg_hbm, qg_ref), (x0_hbm, x0_ref.at[pl.ds(0, size)]),
             (g0_hbm, g0_ref), (w_hbm, w_ref), (x1_hbm, x1_ref.at[pl.ds(0, size)]), (g1_hbm, g1_ref), (owner_hbm, owner_ref))
    order = (3, 4, 8, 0, 1, 2, 6, 7, 5)
    copies = [pltpu.make_async_copy(src, dst, loads.at[i]) for i, (src, dst) in enumerate(pairs)]
    for i in order:
        copies[i].start()
    arrive = lambda i: copies[i].wait()

    barrier = pltpu.get_barrier_semaphore()
    with jax.named_scope("greet"):
        def greet(to, to_grp):
            pl.semaphore_signal(barrier, inc=1, device_id={"dp": to, "group": to_grp},
                                device_id_type=MESH)

        def greet_all(r):
            for q in range(ng):
                greet(partner(me, r, dp), lax.rem(grp + q, ng))
        each(1, dp, greet_all)
        for q in range(1, ng):
            greet(me, lax.rem(grp + q, ng))

    def sibling(q):
        return lax.rem(grp + q, ng)

    def from_group(q):
        return lax.rem(grp + ng - q, ng)

    def copy_base(q, i):
        at, n = ((0, off_qg), (off_qg, off_rest + 16 - off_qg))[i]
        return remote(base_out.at[sibling(q), pl.ds(at, n)], base_in.at[q - 1, pl.ds(at, n)],
                      s_base.at[q - 1, i], r_base.at[q - 1, i], {"group": sibling(q)})

    def copy_part(l, q):
        return remote(part_ref.at[l, sibling(q)], peer_ref.at[l, q - 1], s_part.at[l, q - 1],
                      r_part.at[l, q - 1], {"group": sibling(q)})

    def other(r):
        return me if isinstance(r, int) and r == 0 else partner(me, r, dp)

    def copy_a(l, r):
        to = partner(member, r, cube)
        return remote(ra_ref.at[l, to], raa_ref.at[l, r - 1], s_a.at[l], r_a.at[l],
                      {"dp": part * cube + to})

    def all_a(l):
        return remote(raa_ref.at[l], raa_ref.at[l], s_a.at[l], r_a.at[l], {"dp": me})

    def copy_b(l, r):
        to = lax.rem(part + r, halves)
        return remote(rb_ref.at[l, part], rb_ref.at[l, part], s_b.at[l, r - 1], r_b.at[l, r - 1],
                      {"dp": to * cube + member})

    def copy_c(l, r):
        to = partner(member, r, cube)
        block = tot_ref.at[grp, l, member]
        return remote(block, block, s_c.at[l], r_c.at[l], {"dp": part * cube + to})

    def all_c(l):
        blocks = tot_ref.at[grp, l, pl.ds(0, cube - 1)]
        return remote(blocks, blocks, s_c.at[l], r_c.at[l], {"dp": me})

    def copy_d(l, q, k=grp):
        return remote(tot_ref.at[k, l], tot_out.at[k, l], s_d.at[l, q - 1], r_d.at[l, q - 1],
                      {"group": sibling(q)})

    def put_d(l):
        return pltpu.make_async_copy(tot_ref.at[grp, l], tot_out.at[grp, l], put_tot.at[l])

    def copy_rot(r):
        to = other(r)
        return remote(rot_ref.at[to], rotin_ref.at[0, me], s_rot.at[0], r_rot.at[0], {"dp": to})

    def copy_rot_late(k):
        to = late_at(k)
        return remote(rot_ref.at[k], rotin_ref.at[k // dp, me], s_rot.at[1 + k - dp],
                      r_rot.at[k // dp], {"dp": to})

    def all_rot(s):
        blocks = rotin_ref.at[s, pl.ds(0, dp - 1)]
        return remote(blocks, blocks, s_rot.at[0], r_rot.at[s], {"dp": me})

    def copy_back(s, r):
        to = other(r)
        k = block_at(s)
        recv = r_back.at[0] if s == 0 else r_back.at[k - dp + 1]
        return remote(back_ref.at[s, to], backin_ref.at[k], s_back.at[s], recv, {"dp": to})

    def all_back(s):
        some = backin_ref.at[pl.ds(0, dp - 1)]
        return remote(some, some, s_back.at[s], r_back.at[0], {"dp": me})

    def back_from(k):
        return remote(backin_ref.at[k], backin_ref.at[k], s_back.at[0], r_back.at[k - dp + 1],
                      {"dp": me})

    def copy_row(l):
        k = jnp.maximum(grp, LAYERS) - LAYERS
        return remote(row_ref.at[l], rowin_ref.at[l, k], s_row.at[l], r_row.at[l, k], {"group": 0})

    def row_from(l, k):
        return remote(row_ref.at[l], rowin_ref.at[l, k - LAYERS], s_row.at[l],
                      r_row.at[l, k - LAYERS], {"group": k})

    def copy_in(l, r):
        to = other(r)
        return remote(in_ref.at[l, lax.rem(to, per_chans)], ins_ref.at[me], s_note, r_ins,
                      {"dp": to, "group": l})

    def copy_out(l, r):
        return remote(out1_ref.at[l], outs_ref.at[me], s_note, r_outs,
                      {"dp": other(r), "group": l})

    def some_notes(ref, recv, n):
        return remote(ref.at[pl.ds(0, n)], ref.at[pl.ds(0, n)], s_note, recv, {"dp": me})

    def copy_tap(q, k=grp):
        return remote(tap_ref, tap_out.at[k], s_tap.at[q - 1], r_tap.at[q - 1],
                      {"group": sibling(q)})

    def put_t():
        return pltpu.make_async_copy(tap_ref, tap_out.at[grp], put_tap)

    def copy_res(q, k=grp):
        return remote(res_ref, out_ref.at[k], s_res.at[q - 1], r_res.at[q - 1],
                      {"group": sibling(q)})

    def put_r():
        return pltpu.make_async_copy(res_ref, out_ref.at[grp], put_res)

    late = range(dp, blocks)
    spread = dp // 4 + 2 * grp

    def block_at(s):
        if s == 0:
            return me
        return s * dp + lax.rem((me + 4 * dp - spread) * pow(5, -1, dp), dp)

    def late_at(k):
        return lax.rem(5 * (k % dp) + spread, dp)

    def if_block(s, fn):
        when((s + 1) * dp <= blocks, block_at(s) < blocks, fn)

    def if_to(q, fn):
        when(whole, sibling(q) < LAYERS, fn)

    def if_from(q, fn):
        when(whole, from_group(q) < LAYERS, fn)

    scope = jax.named_scope
    with scope("tables"):
        tap_tables(ones_ref, twos_ref, flat_ref)
        shape = pick_ref.shape
        pick_ref[...] = jnp.where(iota(shape, 0) % 2 == iota(shape, 1) // LANES, 1.0, 0.0)
        for ref in (x0_ref, x1_ref):
            ref[size:size + 2 * side, :] = jnp.zeros((2 * side, chans), BF16)
        sums_ref[...] = jnp.zeros(sums_ref.shape, F32)
        for p in range(ng):
            for at in (off_qs, off_rest):
                base_out[p, at:at + 16] = jnp.zeros((16, chans), BF16)
        for p in range(LAYERS, ng):
            base_out[p, 0:off_qs] = jnp.zeros((off_qs, chans), BF16)
            base_out[p, off_qg:off_rest] = jnp.zeros((off_rest - off_qg, chans), BF16)

    def own_bases():
        with scope("held"):
            arrive(0)
            arrive(8)
            slot = [owner_ref[l] % slot_total for l in range(LAYERS)]
            mine = [owner_ref[l] // slot_total == grp for l in range(LAYERS)]
            taps = qs_ref[...].astype(F32)
            level = iota(taps.shape, 1)

            def held_taps(l):
                value = jnp.sum(jnp.where((level == slot[l]) & mine[l], taps, 0.0), axis=1)
                return jnp.pad(value, ((0, 7), (TAP_LANE, LANES - TAP_LANE - 9))).astype(BF16)

            held = [held_taps(l) for l in range(LAYERS)]
        with scope("mask"):
            arrive(1)
            arrive(2)
            keep = lambda l, ref: jnp.where(mine[l], ref[slot[l]], jnp.zeros(ref.shape[1:], BF16))
            for p in range(LAYERS):
                base_out[p, 0:chans] = keep(p, qa_ref)
                base_out[p, off_qs:off_qs + 16, 0:LANES] = held[p]
                base_out[p, off_qg:off_qg + chans] = keep(p, qg_ref)
                base_out[p, off_x:off_x + chans] = keep(1 - p, qg_ref if p else qa_ref)
                base_out[p, off_rest:off_rest + 16, 0:LANES] = held[1 - p]
            for p in range(LAYERS, ng):
                base_out[p, off_qs:off_qs + 16, 0:LANES] = held[0]
                base_out[p, off_rest:off_rest + 16, 0:LANES] = held[1]

    def take_base(i):
        at, n = ((0, off_qg), (off_qg, off_rest + 16 - off_qg))[i]
        total = base_out[grp, at:at + n]
        for q in range(1, ng):
            copy_base(q, i).wait_recv()
            total = total + base_in[q - 1, at:at + n]
        base_ref[at:at + n] = total

    def tap_table(l):
        near = grp == l if l else (grp == l) | (grp >= LAYERS)
        at = jnp.where(near, off_qs, off_rest)
        qs = base_ref[pl.ds(pl.multiple_of(at, 16), 16), 0:LANES]
        both = dot(ones_ref[...], qs) * dot(twos_ref[...], qs)
        table_ref[l] = flat_ref[...] + both

    def make_row(l):
        row_ref[l] = jnp.sum(fsp_ref[l] * table_ref[l], axis=0, keepdims=True)
        if ng > LAYERS:
            pl.when(grp >= LAYERS)(lambda: copy_row(l).start())

    def local_factors(l, x_ref, g_ref, x_load):
        arrive(x_load)
        arrive(x_load + 1)
        full = channel_gram(x_ref[0:size, :], side, STRIDES[l])
        out = dot_rows(g_ref[...], g_ref[...])
        values = tap_gram(x_ref, sums_ref, side, STRIDES[l], outs[l])
        store_packed(part_ref.at[l, 0], full)
        store_packed(part_ref.at[l, 1], out)
        fsp_ref[l] = jnp.broadcast_to(values, fsp_ref.shape[1:])

    def send_part(l):
        for q in range(1, ng):
            if_to(q, lambda q=q: copy_part(l, q).start())

    def local_taps(l, x_ref):
        values = tap_gram(x_ref, sums_ref, side, STRIDES[l], outs[l])
        fsp_ref[l] = jnp.broadcast_to(values, fsp_ref.shape[1:])

    def chip_sum(l):
        def run():
            total = part_ref[l, grp].astype(F32)
            for q in range(1, ng):
                copy_part(l, q).wait_recv()
                total = total + peer_ref[l, q - 1].astype(F32)
            ra_ref[l] = total.astype(BF16).reshape(cube, 3 * half // cube, LANES)
        handles(run)

    def send_a(l):
        handles(lambda: each(1, cube, lambda r: copy_a(l, r).start()))

    def make_note(l):
        at = jnp.where(grp == l, jnp.where(grp == 0, 0, off_qg), off_x)
        basis = base_ref[pl.ds(pl.multiple_of(at, 16), chans), :]
        blk = ra_ref[l].reshape(3 * half, LANES)
        scale = 1.0 / (jnp.where(grp == 0, 9.0, 1.0) * positions[l])
        lam = quadratic(blk, basis) * scale
        row = row_ref[l]
        for p in range(per_chans):
            in_ref[l, p] = jnp.concatenate([row, lam[:, p * LANES:(p + 1) * LANES]], axis=1)
        out1_ref[l] = jnp.concatenate([row, lam], axis=1)

    def add_rows():
        for l in range(LAYERS):
            total = row_ref[l]
            for k in range(LAYERS, ng):
                row_from(l, k).wait_recv()
                total = total + rowin_ref[l, k - LAYERS]
            row_ref[l] = total

    def send_notes():
        for k, copy in ((0, copy_in), (1, copy_out)):
            def send(k=k, copy=copy):
                def both(r):
                    for l in range(LAYERS):
                        copy(l, r).start()
                copy(1 - k, 0).start()
                each(1, dp, both)
                if k:
                    outs_ref[me] = out1_ref[k]
                else:
                    ins_ref[me] = in_ref[k, lax.rem(me, per_chans)]
            pl.when(grp == k)(send)

    def notes_here():
        for k in range(LAYERS):
            def run(k=k):
                some_notes(ins_ref, r_ins, dp - 1 if k == 0 else dp).wait_recv()
                some_notes(outs_ref, r_outs, dp - 1 if k else dp).wait_recv()
            pl.when(grp == k)(run)

    def reduce_b(l):
        def run():
            all_a(l).wait_recv()
            total = ra_ref[l, member].astype(F32)
            for r in range(1, cube):
                total = total + raa_ref[l, r - 1].astype(F32)
            rb_ref[l, part] = total.astype(BF16)
            for r in range(1, halves):
                copy_b(l, r).start()
        handles(run)

    def gather_c(l):
        def run():
            for r in range(1, halves):
                copy_b(l, r).wait_recv()
            total = rb_ref[l, 0].astype(F32)
            for h in range(1, halves):
                total = total + rb_ref[l, h].astype(F32)
            tot_ref[grp, l, member] = total.astype(BF16)
            each(1, cube, lambda r: copy_c(l, r).start())
        handles(run)

    def forward_d(l):
        def run():
            all_c(l).wait_recv()
            for q in range(1, ng):
                copy_d(l, q).start()
            put_d(l).start()
        handles(run)

    def rotate():
        qs = base_ref[off_qs:off_qs + 16, 0:LANES].astype(F32)
        parts = [w_ref[grp, :, u * chans:(u + 1) * chans] for u in range(9)]
        inner = through_basis(parts, base_ref[0:chans, :], rows, False)
        turned = mixed_taps(inner, lambda u, t: qs[u:u + 1, TAP_LANE + t:TAP_LANE + t + 1])
        per = chans // LANES
        for k in range(blocks):
            lane = (k % per) * LANES
            rot_ref[k] = turned[k // per][:, lane:lane + LANES].astype(BF16)
        if dp <= blocks:
            each(1, dp, lambda r: copy_rot(r).start())
        else:
            each(1, dp, lambda r: pl.when(other(r) < blocks)(lambda: copy_rot(r).start()))
        for k in late:
            pl.when(me != late_at(k))(lambda k=k: copy_rot_late(k).start())
        for s in range(slots):
            def own(s=s):
                rotin_ref[s, me] = rot_ref[block_at(s)]
            if_block(s, own)

    def project():
        for s in range(slots):
            def run(s=s):
                all_rot(s).wait_recv()
                rot = stacked([rotin_ref[s, e] for e in range(dp)])
                proj_ref[s] = dot_rows(base_ref[off_qg:off_qg + chans, :], rot)
            if_block(s, run)

    def precondition():
        with jax.named_scope("notes"):
            notes_here()
        sums = []
        for ref in (ins_ref, outs_ref):
            total = ref[0]
            for e in range(1, dp):
                total = total + ref[e]
            sums.append(total)
        rows_sum = sums[0][:, 0:LANES] + sums[1][:, 0:LANES]
        lam_in = sums[0][:, LANES:]
        spread_out = jnp.concatenate([sums[1][:, LANES:2 * LANES], sums[1][:, 2 * LANES:]], axis=0)
        inv = jnp.where(grp == 0, 1.0 / (chans * positions[0]), 1.0 / (chans * positions[1]))
        every = rows_sum * inv
        tap_ref[...] = every
        for q in range(1, ng):
            copy_tap(q).start()
        put_t().start()
        high = spread_out.astype(BF16).astype(F32)
        col = dot_rows(jnp.concatenate([high, spread_out - high], axis=0), pick_ref[...])
        lam_out = jnp.concatenate([col[:, 0:LANES], col[:, LANES:]], axis=0)
        lane = iota((1, LANES), 1)
        per = chans // LANES
        for s in range(slots):
            def run(s=s):
                k = block_at(s)
                tap = jnp.sum(jnp.where(lane == TAP_LANE + k // per, every, 0.0), axis=1, keepdims=True)
                coords = (proj_ref[s] / (lam_out * (lam_in * tap) + DAMPING)).astype(BF16)
                back = dot(base_ref[off_qg:off_qg + chans, :], coords)
                for e in range(dp):
                    back_ref[s, e] = back[e * rows:(e + 1) * rows].astype(BF16)
                each(1, dp, lambda r: copy_back(s, r).start())
                backin_ref[block_at(s)] = back_ref[s, me]
            if_block(s, run)

    def result():
        with jax.named_scope("back"):
            if dp <= blocks:
                all_back(0).wait_recv()
            else:
                each(0, blocks, lambda k: pl.when(me != k)(
                    lambda: remote(backin_ref.at[k], backin_ref.at[k], s_back.at[0], r_back.at[0],
                                   {"dp": me}).wait_recv()))
            for k in late:
                pl.when(me != late_at(k))(lambda k=k: back_from(k).wait_recv())
        qs = base_ref[off_qs:off_qs + 16, 0:LANES].astype(F32)
        per = chans // LANES
        parts = []
        for t in range(9):
            pieces = [backin_ref[k] for k in range(t * per, (t + 1) * per)]
            parts.append(jnp.concatenate(pieces, axis=1))
        turned = mixed_taps(through_basis(parts, base_ref[0:chans, :], rows, True),
                            lambda t, u: qs[u:u + 1, TAP_LANE + t:TAP_LANE + t + 1])
        for u in range(9):
            res_ref[:, u * chans:(u + 1) * chans] = turned[u].astype(BF16)
        for q in range(1, ng):
            copy_res(q).start()
        put_r().start()

    with scope("first"):
        local_factors(0, x0_ref, g0_ref, 3)
    own_bases()
    with scope("barrier"):
        pl.semaphore_wait(barrier, dp * ng - 1)
    send_part(0)
    for q in range(1, ng):
        for i in range(2):
            copy_base(q, i).start()
    with scope("second"):
        local_factors(1, x1_ref, g1_ref, 6)
        send_part(1)
    with scope("first_sum"):
        chip_sum(0)
        send_a(0)
    with scope("base"):
        take_base(0)
        take_base(1)
    arrive(5)
    with scope("rotate"):
        handles(rotate)
    with scope("second_sum"):
        chip_sum(1)
    with scope("tables2"):
        for l in range(LAYERS):
            tap_table(l)
            make_row(l)

    def notes():
        if ng > LAYERS:
            pl.when(grp == 0)(add_rows)
        for l in range(LAYERS):
            make_note(l)
        send_notes()
    with scope("make_notes"):
        handles(notes)
    send_a(1)
    with scope("first_b"):
        reduce_b(0)
    with scope("second_b"):
        reduce_b(1)
    with scope("first_c"):
        gather_c(0)
    with scope("project"):
        handles(project)
    with scope("precondition"):
        handles(precondition)
    with scope("second_c"):
        gather_c(1)
    with scope("forward0"):
        forward_d(0)
    with scope("result"):
        handles(result)
    with scope("forward"):
        forward_d(1)

    with scope("rest"):
        for q in range(1, ng):
            def arrived(q=q):
                k = from_group(q)
                copy_tap(q, k).wait_recv()
                copy_res(q, k).wait_recv()
                for l in range(LAYERS):
                    copy_d(l, q, k).wait_recv()
            if_from(q, arrived)

    with scope("sent"):
        for q in range(1, ng):
            def sent_to(q=q):
                for l in range(LAYERS):
                    copy_part(l, q).wait_send()
            if_to(q, sent_to)
            for i in range(2):
                copy_base(q, i).wait_send()
        if ng > LAYERS:
            pl.when(grp >= LAYERS)(lambda: [copy_row(l).wait_send() for l in range(LAYERS)] and None)

        def sent():
            pl.when(grp == 0)(lambda: [some_notes(ins_ref, r_ins, n).wait_send() for n in (dp, dp - 1)] and None)
            pl.when(grp == 1)(lambda: [some_notes(outs_ref, r_outs, n).wait_send() for n in (dp, dp - 1)] and None)
            put_t().wait()
            put_r().wait()
            for l in range(LAYERS):
                put_d(l).wait()
                all_a(l).wait_send()
                all_c(l).wait_send()
                for r in range(1, halves):
                    copy_b(l, r).wait_send()
                for q in range(1, ng):
                    copy_d(l, q).wait_send()
            if dp <= blocks:
                all_rot(0).wait_send()
            else:
                each(1, dp, lambda r: pl.when(other(r) < blocks)(
                    lambda: copy_rot(r).wait_send()))
            for k in late:
                pl.when(me != late_at(k))(lambda k=k: copy_rot_late(k).wait_send())
            for s in range(slots):
                if_block(s, lambda s=s: all_back(s).wait_send())
            for q in range(1, ng):
                copy_tap(q).wait_send()
                copy_res(q).wait_send()
        handles(sent)


def finish_kernel(positions, res_ref, tot_ref, tap_ref, out_ref, fin_ref, fsp_ref, fout_ref):
    for l in range(LAYERS):
        for kind, ref, scale in ((0, fin_ref, 9.0), (1, fout_ref, 1.0)):
            blk = tot_ref[kind, l].astype(F32) / (scale * positions[l])
            half = blk.shape[0] // 3
            mid = blk[half:2 * half]
            ref[l, 0:half, 0:half] = blk[0:half]
            ref[l, 0:half, half:] = mid
            ref[l, half:, 0:half] = jnp.transpose(mid)
            ref[l, half:, half:] = blk[2 * half:]
        for u in range(9):
            fsp_ref[u, l:l + 1, :] = tap_ref[l, 0:1, 9 * u:9 * u + 9]
    out_ref[...] = res_ref[...]


def on_device(dp, ng, acts_first, grads_first, acts_second, grads_second, grad_w, owner,
              basis_in, basis_spatial, basis_out):
    images, side = acts_first.shape[0], acts_first.shape[1]
    chans = basis_in.shape[1]
    rows = grad_w.shape[1]
    slot_total = basis_in.shape[0]
    outs = (grads_first.shape[1], grads_second.shape[1])
    positions = tuple(images * o * o * dp * ng for o in outs)
    slots = -(-9 * chans // LANES // dp)
    cube = CUBE if dp % CUBE == 0 else dp
    halves = dp // cube
    half = chans // 2
    share = 3 * half // cube
    base_rows = 3 * chans + 32
    extra = max(9 * chans // LANES - dp, 0)
    vmem = pl.BlockSpec(memory_space=pltpu.VMEM)
    hbm = pl.BlockSpec(memory_space=pltpu.HBM)
    struct = jax.ShapeDtypeStruct
    dma = pltpu.SemaphoreType.DMA
    bf = lambda *shape: pltpu.VMEM(shape, BF16)
    ff = lambda *shape: pltpu.VMEM(shape, F32)
    taps = jnp.transpose(basis_spatial, (1, 0, 2))

    cfg = (side, outs, chans, rows, dp, ng, slot_total, slots, positions)
    res, tot, tap = pl.pallas_call(
        functools.partial(main_kernel, cfg),
        out_shape=(struct((LAYERS, rows, 9 * chans), BF16),
                   struct((2, LAYERS, cube, share, LANES), BF16),
                   struct((LAYERS, 1, LANES), F32)),
        in_specs=[hbm] * 9,
        out_specs=(hbm,) * 3,
        scratch_shapes=[
            pltpu.SMEM((LAYERS,), I32), bf((side + 2) * side, chans), bf(outs[0] * outs[0], chans),
            bf((side + 2) * side, chans), bf(outs[1] * outs[1], chans),
            bf(*grad_w.shape), bf(*basis_in.shape), bf(*basis_out.shape), bf(*taps.shape),
            bf(192, 16), bf(192, 16), ff(192, LANES), ff(4, 2 * LANES), ff(LAYERS, 192, LANES), ff(32, LANES),
            bf(ng, base_rows, chans), bf(ng - 1, base_rows, chans),
            bf(base_rows, chans),
            bf(LAYERS, 2, 3 * half, LANES), bf(LAYERS, ng - 1, 3 * half, LANES),
            bf(LAYERS, cube, share, LANES), bf(LAYERS, max(cube - 1, 1), share, LANES),
            bf(LAYERS, halves, share, LANES), bf(2, LAYERS, cube, share, LANES),
            ff(1, LANES), ff(LAYERS, 1, LANES), ff(LAYERS, max(ng - LAYERS, 1), 1, LANES),
            ff(LAYERS, chans // LANES, 1, 2 * LANES), ff(dp, 1, 2 * LANES), ff(LAYERS, 1, LANES + chans),
            ff(dp, 1, LANES + chans),
            bf(max(9 * chans // LANES, slots * dp), rows, LANES), bf(slots, dp, rows, LANES), ff(slots, chans, LANES),
            bf(slots, dp, rows, LANES), bf(slots * dp, rows, LANES), ff(LAYERS, 192, LANES),
            bf(rows, 9 * chans),
            dma((9,)), dma((ng - 1, 2)), dma((ng - 1, 2)), dma((LAYERS, ng - 1)), dma((LAYERS, ng - 1)),
            dma((LAYERS,)), dma((LAYERS,)), dma((LAYERS, max(halves - 1, 1))), dma((LAYERS, max(halves - 1, 1))),
            dma((LAYERS,)), dma((LAYERS,)), dma((LAYERS, ng - 1)), dma((LAYERS, ng - 1)),
            dma((extra + 1,)), dma((slots,)), dma((slots,)), dma((extra + 1,)),
            dma, dma, dma, dma((ng - 1,)), dma((ng - 1,)), dma((ng - 1,)), dma((ng - 1,)),
            dma((LAYERS,)), dma((LAYERS, max(ng - LAYERS, 1))), dma((LAYERS,)), dma, dma],
        compiler_params=pltpu.CompilerParams(collective_id=0, has_side_effects=True,
                                             vmem_limit_bytes=62 << 20),
        name="precondition",
    )(owner, acts_first.reshape(-1, chans), grads_first.reshape(-1, chans),
      acts_second.reshape(-1, chans), grads_second.reshape(-1, chans), grad_w, basis_in,
      basis_out, taps)

    out, fin, fsp, fout = pl.pallas_call(
        functools.partial(finish_kernel, positions),
        out_shape=(struct((LAYERS, rows, 9 * chans), BF16), struct((LAYERS, chans, chans), F32),
                   struct((9, LAYERS, 9), F32), struct((LAYERS, chans, chans), F32)),
        in_specs=[vmem] * 3,
        out_specs=(vmem,) * 4,
        compiler_params=pltpu.CompilerParams(vmem_limit_bytes=62 << 20),
        name="finish",
    )(res, tot.reshape(2, LAYERS, 3 * half, LANES), tap)
    return out, fin, jnp.transpose(fsp, (1, 0, 2)), fout


def solution(mesh):
    placed = (
        P(("dp", "group"), None, None, None),
        P(("dp", "group"), None, None, None),
        P(("dp", "group"), None, None, None),
        P(("dp", "group"), None, None, None),
        P(None, "dp", None),
        P(),
        P("group", None, None),
        P("group", None, None),
        P("group", None, None),
    )
    return jax.shard_map(
        functools.partial(on_device, mesh.shape["dp"], mesh.shape["group"]),
        mesh=mesh,
        in_specs=placed,
        out_specs=(P(None, "dp", None), P(), P(), P()),
        check_vma=False,
    )
```

```python
import functools

import jax
import jax.numpy as jnp
from jax import lax
from jax.experimental import pallas as pl
from jax.experimental.pallas import tpu as pltpu
from jax.sharding import PartitionSpec as P

LAYERS = 2
STRIDES = (1, 2)
DAMPING = 0.1
LANES = 128
CUBE = 8
TAP_LANE = 96
MESH = pl.DeviceIdType.MESH
F32 = jnp.float32
BF16 = jnp.bfloat16
I32 = jnp.int32
CONTRACT_ROWS = (((0,), (0,)), ((), ()))
CONTRACT_COLS = (((1,), (1,)), ((), ()))
PAIRS = ((0, 0), (1, 1), (2, 2), (0, 1), (1, 2), (0, 2))


def dot(a, b):
    return jnp.dot(a, b, preferred_element_type=F32)


def dot_rows(a, b):
    return lax.dot_general(a, b, CONTRACT_ROWS, preferred_element_type=F32)


def dot_cols(a, b):
    return lax.dot_general(a, b, CONTRACT_COLS, preferred_element_type=F32)


def iota(shape, dim):
    return lax.broadcasted_iota(I32, shape, dim)


def each(start, stop, fn):
    if stop - start <= 16:
        for k in range(start, stop):
            fn(k)
        return

    def body(k, c):
        fn(k)
        return c
    lax.fori_loop(start, stop, body, 0)


def partner(index, step, count):
    if count & (count - 1):
        return lax.rem(index + step, count)
    step = count - step
    bit = 1
    out = index
    while bit < count:
        turn = bit - index // bit % 2 * (2 * bit)
        if not isinstance(step, int):
            out = out + lax.rem(lax.div(step, jnp.int32(bit)), jnp.int32(2)) * turn
        elif step & bit:
            out = out + turn
        bit *= 2
    return out


def when(static, cond, fn):
    if static:
        fn()
    else:
        pl.when(cond)(fn)


def stacked(pieces):
    if pieces[0].shape[0] % 16 == 0:
        return jnp.concatenate(pieces, axis=0)
    return jnp.concatenate([piece.astype(F32) for piece in pieces], axis=0).astype(BF16)


def store_packed(ref, full):
    half = full.shape[0] // 2
    ref[0:half] = full[:half, :half].astype(BF16)
    ref[half:2 * half] = full[:half, half:].astype(BF16)
    ref[2 * half:] = full[half:, half:].astype(BF16)


def channel_gram(x, side, stride):
    chans = x.shape[1]
    col = iota((side, chans), 0)
    if stride == 1:
        counts = jnp.where((col == 0) | (col == side - 1), 2.0, 3.0)
        per_row = lambda i: 2.0 if i in (0, side - 1) else 3.0
    else:
        counts = jnp.where((col % 2 == 1) & (col < side - 1), 2.0, 1.0)
        per_row = lambda i: 2.0 if i % 2 == 1 and i < side - 1 else 1.0
    weights = {n: (n * counts).astype(BF16) for n in sorted({per_row(i) for i in range(side)})}
    weighted = jnp.concatenate([x[i * side:(i + 1) * side] * weights[per_row(i)]
                                for i in range(side)], axis=0)
    return dot_rows(x, weighted)


def tap_places(k):
    form, rest = k // 96, k % 96
    first = rest // 32
    rest = rest % 32
    pair, second = rest // 5, first + rest % 5 - 2
    a = jnp.where(pair < 3, pair, jnp.where(pair == 4, 1, 0))
    b = jnp.where(pair < 3, pair, jnp.where(pair == 3, 1, 2))
    one, two = 3 * a + first, 3 * b + second
    stands = (rest < 30) & (second >= 0) & (second < 3) & ((form == 0) | (pair >= 3))
    return jnp.where(form == 0, one, two), jnp.where(form == 0, two, one), stands


def tap_tables(ones_ref, twos_ref, flat_ref):
    row, col, stands = tap_places(iota(ones_ref.shape, 0))
    lane = iota(ones_ref.shape, 1)
    ones_ref[...] = jnp.where((row == lane) & stands, 1.0, 0.0).astype(BF16)
    twos_ref[...] = jnp.where((col == lane) & stands, 1.0, 0.0).astype(BF16)
    row, col, stands = tap_places(iota(flat_ref.shape, 0))
    flat_ref[...] = jnp.where((9 * row + col == iota(flat_ref.shape, 1)) & stands, 1.0, 0.0)


def tap_gram(x_ref, sums_ref, side, stride, out_side):
    per = 2 * LANES // side
    terms = []
    for q in range(side // per):
        at = 2 * q * LANES
        terms.append(dot_cols(x_ref[at:at + 2 * LANES + 2 * side, :], x_ref[at:at + 2 * LANES, :]))
    total = terms[0]
    for term in terms[1:]:
        total = total + term
    shape = (side, LANES)
    below, lane = iota(shape, 0), iota(shape, 1)
    block, col = lane // side, lane % side

    def row_pairs(dy):
        out = None
        for h in range(2):
            lanes = slice(h * LANES, (h + 1) * LANES)
            pick = None
            for r in range(per // 2):
                at = (h * per // 2 + r + dy) * side
                rows = total[at:at + side, lanes]
                pick = rows if pick is None else jnp.where(block == r, rows, pick)
            out = pick if out is None else out + pick
        return out

    same, one, two = row_pairs(0), row_pairs(1), row_pairs(2)
    last = jnp.where(block == per // 2 - 1, terms[-1][(per - 1) * side:per * side, LANES:], 0.0)
    if stride == 1:
        first = jnp.where(block == 0, terms[0][0:side, 0:LANES], 0.0)
        by_pair = (same - last, same, same - first, one, one, two)
    else:
        even = block % 2 == 0
        odd_same = jnp.where(even, 0.0, same)
        by_pair = (odd_same - last, jnp.where(even, same, 0.0), odd_same,
                   jnp.where(even, 0.0, one), jnp.where(even, one, 0.0), jnp.where(even, 0.0, two))
    for p in range(6):
        for d in range(5):
            k = 5 * p + d
            sums_ref[k:k + 1, :] = jnp.sum(jnp.where(below - col == d - 2, by_pair[p], 0.0),
                                           axis=0, keepdims=True)
    sums = sums_ref[...]
    col = iota(sums.shape, 1) % side
    values = []
    for b in range(3):
        base = col + 1 - b
        mask = (base >= 0) & (base <= stride * (out_side - 1)) & (base % stride == 0)
        values.append(jnp.sum(jnp.where(mask, sums, 0.0), axis=1, keepdims=True))
    return jnp.concatenate(values + values, axis=0)


def through_basis(parts, basis, rows, flip):
    product = (lambda a: dot_cols(a, basis)) if flip else (lambda a: dot(a, basis))
    if rows % 16 == 0:
        whole = product(jnp.concatenate(parts, axis=0))
        return [whole[u * rows:(u + 1) * rows] for u in range(9)]
    return [product(part) for part in parts]


def mixed_taps(parts, coef):
    out = []
    for t in range(9):
        total = parts[0] * coef(0, t)
        for u in range(1, 9):
            total = total + parts[u] * coef(u, t)
        out.append(total)
    return out


def quadratic(blocks, basis):
    half = blocks.shape[0] // 3
    upper = jnp.concatenate([blocks[0:half], blocks[half:2 * half] * 2], axis=1)
    lower = jnp.concatenate([jnp.zeros((half, half), BF16), blocks[2 * half:]], axis=1)
    turned = dot(jnp.concatenate([upper, lower], axis=0), basis)
    return jnp.sum(basis.astype(F32) * turned, axis=0, keepdims=True)


def remote(src, dst, send, recv, to):
    return pltpu.make_async_remote_copy(src_ref=src, dst_ref=dst, send_sem=send, recv_sem=recv,
                                        device_id=to, device_id_type=MESH)


def main_kernel(cfg, owner_hbm, x0_hbm, g0_hbm, x1_hbm, g1_hbm, w_hbm, qa_hbm, qg_hbm, qs_hbm,
                out_ref, tot_out, tap_out, *scratch):
    side, outs, chans, rows, dp, ng, slot_total, slots, positions = cfg
    (owner_ref, x0_ref, g0_ref, x1_ref, g1_ref, w_ref, qa_ref, qg_ref, qs_ref,
     ones_ref, twos_ref, flat_ref, pick_ref, table_ref, sums_ref, base_out, base_in, base_ref, part_ref, peer_ref,
     ra_ref, raa_ref, rb_ref, tot_ref, tap_ref, row_ref, rowin_ref, in_ref, ins_ref, out1_ref, outs_ref,
     rot_ref, rotin_ref, proj_ref, back_ref, backin_ref, fsp_ref, res_ref,
     loads, s_base, r_base, s_part, r_part, s_a, r_a, s_b, r_b, s_c, r_c, s_d, r_d,
     s_rot, r_rot, s_back, r_back, s_note, r_ins, r_outs, s_tap, r_tap, s_res, r_res, s_row, r_row,
     put_tot, put_tap, put_res, s_e, r_e) = scratch
    me, grp = lax.axis_index("dp"), lax.axis_index("group")
    cube = CUBE if dp % CUBE == 0 else dp
    halves = dp // cube
    member, part = lax.rem(me, cube), me // cube
    half = chans // 2
    blocks = 9 * chans // LANES
    per_chans = chans // LANES
    size = side * side
    whole = ng == LAYERS
    off_qs, off_qg, off_x, off_rest = chans, chans + 16, 2 * chans + 16, 3 * chans + 16
    handles = lambda fn: when(whole, grp < LAYERS, fn)

    pairs = ((qs_hbm, qs_ref), (qa_hbm, qa_ref), (qg_hbm, qg_ref), (x0_hbm, x0_ref.at[pl.ds(0, size)]),
             (g0_hbm, g0_ref), (w_hbm, w_ref), (x1_hbm, x1_ref.at[pl.ds(0, size)]), (g1_hbm, g1_ref), (owner_hbm, owner_ref))
    order = (3, 4, 8, 0, 1, 2, 6, 7, 5)
    copies = [pltpu.make_async_copy(src, dst, loads.at[i]) for i, (src, dst) in enumerate(pairs)]
    for i in order:
        copies[i].start()
    arrive = lambda i: copies[i].wait()

    barrier = pltpu.get_barrier_semaphore()
    with jax.named_scope("greet"):
        def greet(to, to_grp):
            pl.semaphore_signal(barrier, inc=1, device_id={"dp": to, "group": to_grp},
                                device_id_type=MESH)

        def greet_all(r):
            for q in range(ng):
                greet(partner(me, r, dp), lax.rem(grp + q, ng))
        each(1, dp, greet_all)
        for q in range(1, ng):
            greet(me, lax.rem(grp + q, ng))

    def sibling(q):
        return lax.rem(grp + q, ng)

    def from_group(q):
        return lax.rem(grp + ng - q, ng)

    def copy_base(q, i):
        at, n = ((0, off_qg), (off_qg, off_rest + 16 - off_qg))[i]
        return remote(base_out.at[sibling(q), pl.ds(at, n)], base_in.at[q - 1, pl.ds(at, n)],
                      s_base.at[q - 1, i], r_base.at[q - 1, i], {"group": sibling(q)})

    def copy_part(l, q):
        return remote(part_ref.at[l, sibling(q)], peer_ref.at[l, q - 1], s_part.at[l, q - 1],
                      r_part.at[l, q - 1], {"group": sibling(q)})

    def other(r):
        return me if isinstance(r, int) and r == 0 else partner(me, r, dp)

    def copy_a(l, r):
        to = partner(member, r, cube)
        return remote(ra_ref.at[l, to], raa_ref.at[l, r - 1], s_a.at[l], r_a.at[l],
                      {"dp": part * cube + to})

    def all_a(l):
        return remote(raa_ref.at[l], raa_ref.at[l], s_a.at[l], r_a.at[l], {"dp": me})

    def copy_b(l, r):
        to = lax.rem(part + r, halves)
        return remote(rb_ref.at[l, part], rb_ref.at[l, part], s_b.at[l, r - 1], r_b.at[l, r - 1],
                      {"dp": to * cube + member})

    def copy_c(l, r):
        to = partner(member, r, cube)
        block = tot_ref.at[grp, l, member]
        return remote(block, block, s_c.at[l], r_c.at[l], {"dp": part * cube + to})

    def all_c(l):
        blocks = tot_ref.at[grp, l, pl.ds(0, cube - 1)]
        return remote(blocks, blocks, s_c.at[l], r_c.at[l], {"dp": me})

    def copy_d(l, q, k=grp):
        return remote(tot_ref.at[k, l], tot_out.at[k, l], s_d.at[l, q - 1], r_d.at[l, q - 1],
                      {"group": sibling(q)})

    def copy_e(q, r):
        to = partner(member, r, cube) if r else member
        return remote(tot_ref.at[grp, LAYERS - 1, member], tot_out.at[grp, LAYERS - 1, member],
                      s_e.at[q], r_e.at[q], {"dp": part * cube + to, "group": sibling(q)})

    def all_e(q, k=grp):
        some = tot_out.at[k, LAYERS - 1, pl.ds(0, cube if q else cube - 1)]
        return remote(some, some, s_e.at[q], r_e.at[q], {"group": sibling(q)})

    def put_e():
        return pltpu.make_async_copy(tot_ref.at[grp, LAYERS - 1, member],
                                     tot_out.at[grp, LAYERS - 1, member], put_tot.at[LAYERS - 1])

    def put_d(l):
        return pltpu.make_async_copy(tot_ref.at[grp, l], tot_out.at[grp, l], put_tot.at[l])

    def copy_rot(r):
        to = other(r)
        return remote(rot_ref.at[to], rotin_ref.at[0, me], s_rot.at[0], r_rot.at[0], {"dp": to})

    def copy_rot_late(k):
        to = late_at(k)
        return remote(rot_ref.at[k], rotin_ref.at[k // dp, me], s_rot.at[1 + k - dp],
                      r_rot.at[k // dp], {"dp": to})

    def all_rot(s):
        blocks = rotin_ref.at[s, pl.ds(0, dp - 1)]
        return remote(blocks, blocks, s_rot.at[0], r_rot.at[s], {"dp": me})

    def copy_back(s, r):
        to = other(r)
        k = block_at(s)
        recv = r_back.at[0] if s == 0 else r_back.at[k - dp + 1]
        return remote(back_ref.at[s, to], backin_ref.at[k], s_back.at[s], recv, {"dp": to})

    def all_back(s):
        some = backin_ref.at[pl.ds(0, dp - 1)]
        return remote(some, some, s_back.at[s], r_back.at[0], {"dp": me})

    def back_from(k):
        return remote(backin_ref.at[k], backin_ref.at[k], s_back.at[0], r_back.at[k - dp + 1],
                      {"dp": me})

    def copy_row(l):
        k = jnp.maximum(grp, LAYERS) - LAYERS
        return remote(row_ref.at[l], rowin_ref.at[l, k], s_row.at[l], r_row.at[l, k], {"group": 0})

    def row_from(l, k):
        return remote(row_ref.at[l], rowin_ref.at[l, k - LAYERS], s_row.at[l],
                      r_row.at[l, k - LAYERS], {"group": k})

    def copy_in(l, r):
        to = other(r)
        return remote(in_ref.at[l, lax.rem(to, per_chans)], ins_ref.at[me], s_note, r_ins,
                      {"dp": to, "group": l})

    def copy_out(l, r):
        return remote(out1_ref.at[l], outs_ref.at[me], s_note, r_outs,
                      {"dp": other(r), "group": l})

    def some_notes(ref, recv, n):
        return remote(ref.at[pl.ds(0, n)], ref.at[pl.ds(0, n)], s_note, recv, {"dp": me})

    def copy_tap(q, k=grp):
        return remote(tap_ref, tap_out.at[k], s_tap.at[q - 1], r_tap.at[q - 1],
                      {"group": sibling(q)})

    def put_t():
        return pltpu.make_async_copy(tap_ref, tap_out.at[grp], put_tap)

    def copy_res(q, k=grp):
        return remote(res_ref, out_ref.at[k], s_res.at[q - 1], r_res.at[q - 1],
                      {"group": sibling(q)})

    def put_r():
        return pltpu.make_async_copy(res_ref, out_ref.at[grp], put_res)

    late = range(dp, blocks)
    spread = dp // 4 + 2 * grp

    def block_at(s):
        if s == 0:
            return me
        return s * dp + lax.rem((me + 4 * dp - spread) * pow(5, -1, dp), dp)

    def late_at(k):
        return lax.rem(5 * (k % dp) + spread, dp)

    def if_block(s, fn):
        when((s + 1) * dp <= blocks, block_at(s) < blocks, fn)

    def if_to(q, fn):
        when(whole, sibling(q) < LAYERS, fn)

    def if_from(q, fn):
        when(whole, from_group(q) < LAYERS, fn)

    scope = jax.named_scope
    with scope("tables"):
        tap_tables(ones_ref, twos_ref, flat_ref)
        shape = pick_ref.shape
        pick_ref[...] = jnp.where(iota(shape, 0) % 2 == iota(shape, 1) // LANES, 1.0, 0.0)
        for ref in (x0_ref, x1_ref):
            ref[size:size + 2 * side, :] = jnp.zeros((2 * side, chans), BF16)
        sums_ref[...] = jnp.zeros(sums_ref.shape, F32)
        for p in range(ng):
            for at in (off_qs, off_rest):
                base_out[p, at:at + 16] = jnp.zeros((16, chans), BF16)
        for p in range(LAYERS, ng):
            base_out[p, 0:off_qs] = jnp.zeros((off_qs, chans), BF16)
            base_out[p, off_qg:off_rest] = jnp.zeros((off_rest - off_qg, chans), BF16)

    def own_bases():
        with scope("held"):
            arrive(0)
            arrive(8)
            slot = [owner_ref[l] % slot_total for l in range(LAYERS)]
            mine = [owner_ref[l] // slot_total == grp for l in range(LAYERS)]
            taps = qs_ref[...].astype(F32)
            level = iota(taps.shape, 1)

            def held_taps(l):
                value = jnp.sum(jnp.where((level == slot[l]) & mine[l], taps, 0.0), axis=1)
                return jnp.pad(value, ((0, 7), (TAP_LANE, LANES - TAP_LANE - 9))).astype(BF16)

            held = [held_taps(l) for l in range(LAYERS)]
        with scope("mask"):
            arrive(1)
            arrive(2)
            keep = lambda l, ref: jnp.where(mine[l], ref[slot[l]], jnp.zeros(ref.shape[1:], BF16))
            for p in range(LAYERS):
                base_out[p, 0:chans] = keep(p, qa_ref)
                base_out[p, off_qs:off_qs + 16, 0:LANES] = held[p]
                base_out[p, off_qg:off_qg + chans] = keep(p, qg_ref)
                base_out[p, off_x:off_x + chans] = keep(1 - p, qg_ref if p else qa_ref)
                base_out[p, off_rest:off_rest + 16, 0:LANES] = held[1 - p]
            for p in range(LAYERS, ng):
                base_out[p, off_qs:off_qs + 16, 0:LANES] = held[0]
                base_out[p, off_rest:off_rest + 16, 0:LANES] = held[1]

    def take_base(i):
        at, n = ((0, off_qg), (off_qg, off_rest + 16 - off_qg))[i]
        total = base_out[grp, at:at + n]
        for q in range(1, ng):
            copy_base(q, i).wait_recv()
            total = total + base_in[q - 1, at:at + n]
        base_ref[at:at + n] = total

    def tap_table(l):
        near = grp == l if l else (grp == l) | (grp >= LAYERS)
        at = jnp.where(near, off_qs, off_rest)
        qs = base_ref[pl.ds(pl.multiple_of(at, 16), 16), 0:LANES]
        both = dot(ones_ref[...], qs) * dot(twos_ref[...], qs)
        table_ref[l] = flat_ref[...] + both

    def make_row(l):
        row_ref[l] = jnp.sum(fsp_ref[l] * table_ref[l], axis=0, keepdims=True)
        if ng > LAYERS:
            pl.when(grp >= LAYERS)(lambda: copy_row(l).start())

    def local_factors(l, x_ref, g_ref, x_load):
        arrive(x_load)
        arrive(x_load + 1)
        full = channel_gram(x_ref[0:size, :], side, STRIDES[l])
        out = dot_rows(g_ref[...], g_ref[...])
        values = tap_gram(x_ref, sums_ref, side, STRIDES[l], outs[l])
        store_packed(part_ref.at[l, 0], full)
        store_packed(part_ref.at[l, 1], out)
        fsp_ref[l] = jnp.broadcast_to(values, fsp_ref.shape[1:])

    def send_part(l):
        for q in range(1, ng):
            if_to(q, lambda q=q: copy_part(l, q).start())

    def local_taps(l, x_ref):
        values = tap_gram(x_ref, sums_ref, side, STRIDES[l], outs[l])
        fsp_ref[l] = jnp.broadcast_to(values, fsp_ref.shape[1:])

    def chip_sum(l):
        def run():
            total = part_ref[l, grp].astype(F32)
            for q in range(1, ng):
                copy_part(l, q).wait_recv()
                total = total + peer_ref[l, q - 1].astype(F32)
            ra_ref[l] = total.astype(BF16).reshape(cube, 3 * half // cube, LANES)
        handles(run)

    def send_a(l):
        handles(lambda: each(1, cube, lambda r: copy_a(l, r).start()))

    def make_note(l):
        at = jnp.where(grp == l, jnp.where(grp == 0, 0, off_qg), off_x)
        basis = base_ref[pl.ds(pl.multiple_of(at, 16), chans), :]
        blk = ra_ref[l].reshape(3 * half, LANES)
        scale = 1.0 / (jnp.where(grp == 0, 9.0, 1.0) * positions[l])
        lam = quadratic(blk, basis) * scale
        row = row_ref[l]
        for p in range(per_chans):
            in_ref[l, p] = jnp.concatenate([row, lam[:, p * LANES:(p + 1) * LANES]], axis=1)
        out1_ref[l] = jnp.concatenate([row, lam], axis=1)

    def add_rows():
        for l in range(LAYERS):
            total = row_ref[l]
            for k in range(LAYERS, ng):
                row_from(l, k).wait_recv()
                total = total + rowin_ref[l, k - LAYERS]
            row_ref[l] = total

    def send_notes():
        for k, copy in ((0, copy_in), (1, copy_out)):
            def send(k=k, copy=copy):
                def both(r):
                    for l in range(LAYERS):
                        copy(l, r).start()
                copy(1 - k, 0).start()
                each(1, dp, both)
                if k:
                    outs_ref[me] = out1_ref[k]
                else:
                    ins_ref[me] = in_ref[k, lax.rem(me, per_chans)]
            pl.when(grp == k)(send)

    def notes_here():
        for k in range(LAYERS):
            def run(k=k):
                some_notes(ins_ref, r_ins, dp - 1 if k == 0 else dp).wait_recv()
                some_notes(outs_ref, r_outs, dp - 1 if k else dp).wait_recv()
            pl.when(grp == k)(run)

    def reduce_b(l):
        def run():
            all_a(l).wait_recv()
            total = ra_ref[l, member].astype(F32)
            for r in range(1, cube):
                total = total + raa_ref[l, r - 1].astype(F32)
            rb_ref[l, part] = total.astype(BF16)
            for r in range(1, halves):
                copy_b(l, r).start()
        handles(run)

    def gather_c(l):
        def run():
            for r in range(1, halves):
                copy_b(l, r).wait_recv()
            total = rb_ref[l, 0].astype(F32)
            for h in range(1, halves):
                total = total + rb_ref[l, h].astype(F32)
            tot_ref[grp, l, member] = total.astype(BF16)
            if l == LAYERS - 1:
                for r in range(1, cube):
                    for q in range(ng):
                        copy_e(q, r).start()
                for q in range(1, ng):
                    copy_e(q, 0).start()
                put_e().start()
            else:
                each(1, cube, lambda r: copy_c(l, r).start())
        handles(run)

    def forward_d(l):
        def run():
            all_c(l).wait_recv()
            for q in range(1, ng):
                copy_d(l, q).start()
            put_d(l).start()
        handles(run)

    def rotate():
        qs = base_ref[off_qs:off_qs + 16, 0:LANES].astype(F32)
        parts = [w_ref[grp, :, u * chans:(u + 1) * chans] for u in range(9)]
        inner = through_basis(parts, base_ref[0:chans, :], rows, False)
        turned = mixed_taps(inner, lambda u, t: qs[u:u + 1, TAP_LANE + t:TAP_LANE + t + 1])
        per = chans // LANES
        for k in range(blocks):
            lane = (k % per) * LANES
            rot_ref[k] = turned[k // per][:, lane:lane + LANES].astype(BF16)
        if dp <= blocks:
            each(1, dp, lambda r: copy_rot(r).start())
        else:
            each(1, dp, lambda r: pl.when(other(r) < blocks)(lambda: copy_rot(r).start()))
        for k in late:
            pl.when(me != late_at(k))(lambda k=k: copy_rot_late(k).start())
        for s in range(slots):
            def own(s=s):
                rotin_ref[s, me] = rot_ref[block_at(s)]
            if_block(s, own)

    def project():
        for s in range(slots):
            def run(s=s):
                all_rot(s).wait_recv()
                rot = stacked([rotin_ref[s, e] for e in range(dp)])
                proj_ref[s] = dot_rows(base_ref[off_qg:off_qg + chans, :], rot)
            if_block(s, run)

    def precondition():
        with jax.named_scope("notes"):
            notes_here()
        sums = []
        for ref in (ins_ref, outs_ref):
            total = ref[0]
            for e in range(1, dp):
                total = total + ref[e]
            sums.append(total)
        rows_sum = sums[0][:, 0:LANES] + sums[1][:, 0:LANES]
        lam_in = sums[0][:, LANES:]
        spread_out = jnp.concatenate([sums[1][:, LANES:2 * LANES], sums[1][:, 2 * LANES:]], axis=0)
        inv = jnp.where(grp == 0, 1.0 / (chans * positions[0]), 1.0 / (chans * positions[1]))
        every = rows_sum * inv
        tap_ref[...] = every
        for q in range(1, ng):
            copy_tap(q).start()
        put_t().start()
        high = spread_out.astype(BF16).astype(F32)
        col = dot_rows(jnp.concatenate([high, spread_out - high], axis=0), pick_ref[...])
        lam_out = jnp.concatenate([col[:, 0:LANES], col[:, LANES:]], axis=0)
        lane = iota((1, LANES), 1)
        per = chans // LANES
        for s in range(slots):
            def run(s=s):
                k = block_at(s)
                tap = jnp.sum(jnp.where(lane == TAP_LANE + k // per, every, 0.0), axis=1, keepdims=True)
                coords = (proj_ref[s] / (lam_out * (lam_in * tap) + DAMPING)).astype(BF16)
                back = dot(base_ref[off_qg:off_qg + chans, :], coords)
                for e in range(dp):
                    back_ref[s, e] = back[e * rows:(e + 1) * rows].astype(BF16)
                each(1, dp, lambda r: copy_back(s, r).start())
                backin_ref[block_at(s)] = back_ref[s, me]
            if_block(s, run)

    def result():
        with jax.named_scope("back"):
            if dp <= blocks:
                all_back(0).wait_recv()
            else:
                each(0, blocks, lambda k: pl.when(me != k)(
                    lambda: remote(backin_ref.at[k], backin_ref.at[k], s_back.at[0], r_back.at[0],
                                   {"dp": me}).wait_recv()))
            for k in late:
                pl.when(me != late_at(k))(lambda k=k: back_from(k).wait_recv())
        qs = base_ref[off_qs:off_qs + 16, 0:LANES].astype(F32)
        per = chans // LANES
        parts = []
        for t in range(9):
            pieces = [backin_ref[k] for k in range(t * per, (t + 1) * per)]
            parts.append(jnp.concatenate(pieces, axis=1))
        turned = mixed_taps(through_basis(parts, base_ref[0:chans, :], rows, True),
                            lambda t, u: qs[u:u + 1, TAP_LANE + t:TAP_LANE + t + 1])
        for u in range(9):
            res_ref[:, u * chans:(u + 1) * chans] = turned[u].astype(BF16)
        for q in range(1, ng):
            copy_res(q).start()
        put_r().start()

    with scope("first"):
        local_factors(0, x0_ref, g0_ref, 3)
    own_bases()
    with scope("barrier"):
        pl.semaphore_wait(barrier, dp * ng - 1)
    send_part(0)
    for q in range(1, ng):
        for i in range(2):
            copy_base(q, i).start()
    with scope("second"):
        local_factors(1, x1_ref, g1_ref, 6)
        send_part(1)
    with scope("first_sum"):
        chip_sum(0)
        send_a(0)
    with scope("base"):
        take_base(0)
        take_base(1)
    arrive(5)
    with scope("rotate"):
        handles(rotate)
    with scope("second_sum"):
        chip_sum(1)
    with scope("tables2"):
        for l in range(LAYERS):
            tap_table(l)
            make_row(l)

    def notes():
        if ng > LAYERS:
            pl.when(grp == 0)(add_rows)
        for l in range(LAYERS):
            make_note(l)
        send_notes()
    with scope("make_notes"):
        handles(notes)
    send_a(1)
    with scope("first_b"):
        reduce_b(0)
    with scope("second_b"):
        reduce_b(1)
    with scope("project"):
        handles(project)
    with scope("first_c"):
        gather_c(0)
    with scope("precondition"):
        handles(precondition)
    with scope("second_c"):
        gather_c(1)
    with scope("forward0"):
        forward_d(0)
    with scope("result"):
        handles(result)
    with scope("forward"):
        handles(lambda: all_e(0).wait_recv())

    with scope("rest"):
        for q in range(1, ng):
            def arrived(q=q):
                k = from_group(q)
                copy_tap(q, k).wait_recv()
                copy_res(q, k).wait_recv()
                for l in range(LAYERS - 1):
                    copy_d(l, q, k).wait_recv()
                all_e(q, k).wait_recv()
            if_from(q, arrived)

    with scope("sent"):
        for q in range(1, ng):
            def sent_to(q=q):
                for l in range(LAYERS):
                    copy_part(l, q).wait_send()
            if_to(q, sent_to)
            for i in range(2):
                copy_base(q, i).wait_send()
        if ng > LAYERS:
            pl.when(grp >= LAYERS)(lambda: [copy_row(l).wait_send() for l in range(LAYERS)] and None)

        def sent():
            pl.when(grp == 0)(lambda: [some_notes(ins_ref, r_ins, n).wait_send() for n in (dp, dp - 1)] and None)
            pl.when(grp == 1)(lambda: [some_notes(outs_ref, r_outs, n).wait_send() for n in (dp, dp - 1)] and None)
            put_t().wait()
            put_r().wait()
            put_e().wait()
            for q in range(ng):
                all_e(q).wait_send()
            for l in range(LAYERS):
                all_a(l).wait_send()
                for r in range(1, halves):
                    copy_b(l, r).wait_send()
                if l < LAYERS - 1:
                    put_d(l).wait()
                    all_c(l).wait_send()
                    for q in range(1, ng):
                        copy_d(l, q).wait_send()
            if dp <= blocks:
                all_rot(0).wait_send()
            else:
                each(1, dp, lambda r: pl.when(other(r) < blocks)(
                    lambda: copy_rot(r).wait_send()))
            for k in late:
                pl.when(me != late_at(k))(lambda k=k: copy_rot_late(k).wait_send())
            for s in range(slots):
                if_block(s, lambda s=s: all_back(s).wait_send())
            for q in range(1, ng):
                copy_tap(q).wait_send()
                copy_res(q).wait_send()
        handles(sent)


def finish_kernel(positions, res_ref, tot_ref, tap_ref, out_ref, fin_ref, fsp_ref, fout_ref):
    for l in range(LAYERS):
        for kind, ref, scale in ((0, fin_ref, 9.0), (1, fout_ref, 1.0)):
            blk = tot_ref[kind, l].astype(F32) / (scale * positions[l])
            half = blk.shape[0] // 3
            mid = blk[half:2 * half]
            ref[l, 0:half, 0:half] = blk[0:half]
            ref[l, 0:half, half:] = mid
            ref[l, half:, 0:half] = jnp.transpose(mid)
            ref[l, half:, half:] = blk[2 * half:]
        for u in range(9):
            fsp_ref[u, l:l + 1, :] = tap_ref[l, 0:1, 9 * u:9 * u + 9]
    out_ref[...] = res_ref[...]


def on_device(dp, ng, acts_first, grads_first, acts_second, grads_second, grad_w, owner,
              basis_in, basis_spatial, basis_out):
    images, side = acts_first.shape[0], acts_first.shape[1]
    chans = basis_in.shape[1]
    rows = grad_w.shape[1]
    slot_total = basis_in.shape[0]
    outs = (grads_first.shape[1], grads_second.shape[1])
    positions = tuple(images * o * o * dp * ng for o in outs)
    slots = -(-9 * chans // LANES // dp)
    cube = CUBE if dp % CUBE == 0 else dp
    halves = dp // cube
    half = chans // 2
    share = 3 * half // cube
    base_rows = 3 * chans + 32
    extra = max(9 * chans // LANES - dp, 0)
    vmem = pl.BlockSpec(memory_space=pltpu.VMEM)
    hbm = pl.BlockSpec(memory_space=pltpu.HBM)
    struct = jax.ShapeDtypeStruct
    dma = pltpu.SemaphoreType.DMA
    bf = lambda *shape: pltpu.VMEM(shape, BF16)
    ff = lambda *shape: pltpu.VMEM(shape, F32)
    taps = jnp.transpose(basis_spatial, (1, 0, 2))

    cfg = (side, outs, chans, rows, dp, ng, slot_total, slots, positions)
    res, tot, tap = pl.pallas_call(
        functools.partial(main_kernel, cfg),
        out_shape=(struct((LAYERS, rows, 9 * chans), BF16),
                   struct((2, LAYERS, cube, share, LANES), BF16),
                   struct((LAYERS, 1, LANES), F32)),
        in_specs=[hbm] * 9,
        out_specs=(hbm,) * 3,
        scratch_shapes=[
            pltpu.SMEM((LAYERS,), I32), bf((side + 2) * side, chans), bf(outs[0] * outs[0], chans),
            bf((side + 2) * side, chans), bf(outs[1] * outs[1], chans),
            bf(*grad_w.shape), bf(*basis_in.shape), bf(*basis_out.shape), bf(*taps.shape),
            bf(192, 16), bf(192, 16), ff(192, LANES), ff(4, 2 * LANES), ff(LAYERS, 192, LANES), ff(32, LANES),
            bf(ng, base_rows, chans), bf(ng - 1, base_rows, chans),
            bf(base_rows, chans),
            bf(LAYERS, 2, 3 * half, LANES), bf(LAYERS, ng - 1, 3 * half, LANES),
            bf(LAYERS, cube, share, LANES), bf(LAYERS, max(cube - 1, 1), share, LANES),
            bf(LAYERS, halves, share, LANES), bf(2, LAYERS, cube, share, LANES),
            ff(1, LANES), ff(LAYERS, 1, LANES), ff(LAYERS, max(ng - LAYERS, 1), 1, LANES),
            ff(LAYERS, chans // LANES, 1, 2 * LANES), ff(dp, 1, 2 * LANES), ff(LAYERS, 1, LANES + chans),
            ff(dp, 1, LANES + chans),
            bf(max(9 * chans // LANES, slots * dp), rows, LANES), bf(slots, dp, rows, LANES), ff(slots, chans, LANES),
            bf(slots, dp, rows, LANES), bf(slots * dp, rows, LANES), ff(LAYERS, 192, LANES),
            bf(rows, 9 * chans),
            dma((9,)), dma((ng - 1, 2)), dma((ng - 1, 2)), dma((LAYERS, ng - 1)), dma((LAYERS, ng - 1)),
            dma((LAYERS,)), dma((LAYERS,)), dma((LAYERS, max(halves - 1, 1))), dma((LAYERS, max(halves - 1, 1))),
            dma((LAYERS,)), dma((LAYERS,)), dma((LAYERS, ng - 1)), dma((LAYERS, ng - 1)),
            dma((extra + 1,)), dma((slots,)), dma((slots,)), dma((extra + 1,)),
            dma, dma, dma, dma((ng - 1,)), dma((ng - 1,)), dma((ng - 1,)), dma((ng - 1,)),
            dma((LAYERS,)), dma((LAYERS, max(ng - LAYERS, 1))), dma((LAYERS,)), dma, dma, dma((ng,)), dma((ng,))],
        compiler_params=pltpu.CompilerParams(collective_id=0, has_side_effects=True,
                                             vmem_limit_bytes=62 << 20),
        name="precondition",
    )(owner, acts_first.reshape(-1, chans), grads_first.reshape(-1, chans),
      acts_second.reshape(-1, chans), grads_second.reshape(-1, chans), grad_w, basis_in,
      basis_out, taps)

    out, fin, fsp, fout = pl.pallas_call(
        functools.partial(finish_kernel, positions),
        out_shape=(struct((LAYERS, rows, 9 * chans), BF16), struct((LAYERS, chans, chans), F32),
                   struct((9, LAYERS, 9), F32), struct((LAYERS, chans, chans), F32)),
        in_specs=[vmem] * 3,
        out_specs=(vmem,) * 4,
        compiler_params=pltpu.CompilerParams(vmem_limit_bytes=62 << 20),
        name="finish",
    )(res, tot.reshape(2, LAYERS, 3 * half, LANES), tap)
    return out, fin, jnp.transpose(fsp, (1, 0, 2)), fout


def solution(mesh):
    placed = (
        P(("dp", "group"), None, None, None),
        P(("dp", "group"), None, None, None),
        P(("dp", "group"), None, None, None),
        P(("dp", "group"), None, None, None),
        P(None, "dp", None),
        P(),
        P("group", None, None),
        P("group", None, None),
        P("group", None, None),
    )
    return jax.shard_map(
        functools.partial(on_device, mesh.shape["dp"], mesh.shape["group"]),
        mesh=mesh,
        in_specs=placed,
        out_specs=(P(None, "dp", None), P(), P(), P()),
        check_vma=False,
    )
```
